32 devices in a mesh: groups: 2 (over y), tiles: 4 (over z), sub: 2 (over x), adj: 2 (over core).
Axes of the slice: x: 2, y: 2, z: 4, core: 2. Of those that a mesh axis runs over, the one named last changes fastest.
Arguments:
- innovation: float32 [128, 256], P(('groups', 'tiles'), 'sub'), parts along dimension 0, may hold values from -6 to 6
- cluster: int32 [128, 256], P(('groups', 'tiles'), 'sub'), parts along dimension 0, may hold values from 0 to 8
- kernel: float32 [36, 64, 256], P(None, 'tiles', 'sub'), may hold values from 0.2 to 1.5
- wind_x: float32 [36, 64, 256], P(None, 'tiles', 'sub'), may hold values from -0.24 to 0.24
- wind_y: float32 [36, 64, 256], P(None, 'tiles', 'sub'), may hold values from -0.24 to 0.24
- conv_strength: float32 [64, 256], P('tiles', 'sub'), may hold values from 0 to 0.9
- conv_matrix: float32 [36, 36], replicated, may hold values from 0 to 1, as said below
- margin_cell: int32 [6144, 8], P(('tiles', 'sub')), may hold values from 0 to 16383, as said below
- margin_weight: float32 [6144, 8], P(('tiles', 'sub')), may hold values from 0 to 1, as said below
Outputs:
- adjoint_field: float32 [16, 36, 64, 256], P(('groups', 'adj'), None, 'tiles', 'sub'), parts along dimension 0
- sensitivity: float32 [16, 6144], P(('groups', 'adj'), ('tiles', 'sub')), parts along dimension 0
The draws below stay inside these ranges and needn't reach their ends.
There are 2 independent parts, one for each index of `groups`. The reference program is written for one: setup_inputs(seed, part) draws one part's arguments, and reference() takes and returns one part's arrays. A program takes and returns all parts, laid end to end along the dimension named above; an argument that names none is the same for every part. Nothing has to cross between parts.
Inputs may be any that keep to these rules, and one draw needn't show every extreme that they name: `conv_matrix`: entries are positive and every column sums to 1. `margin_cell`: state element e is owned by block b = e // 768, with t = b // 2 and s = b % 2; the column index of each of its cells lies in t * 16 - 16 to t * 16 + 2 * 16 - 1, taken modulo 64, and its row in s * 128 - 128 to s * 128 + 2 * 128 - 1 (within 0 to 255). `margin_weight`: each state element has 1 to 8 live slots first, element 0 all 8; the others have weight 0.
All inputs are finite; a program needn't handle non-finite values.
Results may differ from the reference program's by a relative error of at most 0.0003.
Values sent between devices are 32-bit elements; how exact they have to be, the bound alone decides.
No kernel may reach another device: no remote copies, remote signals or barrier semaphores. Data moves between devices by JAX's collectives and lax.ppermute only.
A program may use at most 64 MiB of HBM per device.

```python
import jax
import jax.numpy as jnp
from jax import lax

ADJ = 8
LEV = 36
NSTEP = 2
KOV = 8
CX = 16
CY = 128
E_DEV = 768
NX = 64
NY = 256
NE = 6144
N_SUB = 2


def margin_tables(key):
    folded = jax.random.fold_in(key, 11)
    subkeys = jax.random.split(folded, 5)
    element = jnp.arange(NE, dtype=jnp.int32)
    owner_block = element // E_DEV
    tile_block = owner_block // N_SUB
    cross_block = owner_block % N_SUB
    live_count = jax.random.randint(subkeys[0], (NE,), 1, KOV + 1)
    live_count = jnp.where(element == 0, KOV, live_count)
    shift_x = jax.random.randint(subkeys[1], (NE, KOV), -CX, 2 * CX)
    column_x = (tile_block[:, None] * CX + shift_x + NX) % NX
    low_y = jnp.maximum(cross_block * CY - CY, 0)
    high_y = jnp.minimum(cross_block * CY + 2 * CY, NY)
    row_y = jax.random.randint(subkeys[2], (NE, KOV), low_y[:, None], high_y[:, None])
    cells = (column_x * NY + row_y).astype(jnp.int32)
    live_slot = jnp.arange(KOV)[None, :] < live_count[:, None]
    weights = jax.random.uniform(subkeys[4], (NE, KOV), jnp.float32, 0.2, 1.0) * live_slot.astype(jnp.float32)
    return (cells, weights)


def draw_margin_cell(key, part):
    return margin_tables(key)[0]


def draw_margin_weight(key, part):
    return margin_tables(key)[1]


def draw_conv_matrix(key, part):
    folded = jax.random.fold_in(key, 23)
    spread = jnp.exp(jax.random.uniform(folded, (LEV, LEV), jnp.float32, -2.0, 1.5))
    mixing = spread / jnp.sum(spread, axis=0, keepdims=True)
    return 0.4 * jnp.eye(LEV, dtype=jnp.float32) + 0.6 * mixing


def plant(values, rng, smallest, top_value):
    index_at = [jax.random.randint(jax.random.fold_in(rng, axis), (), 0, length) for axis, length in enumerate(values.shape)]
    longest = values.shape.index(max(values.shape))
    beside = index_at[:longest] + [(index_at[longest] + 1) % values.shape[longest]] + index_at[longest + 1:]
    return values.at[tuple(index_at)].set(smallest).at[tuple(beside)].set(top_value)


def levels(own_key, dims, shards, low, high):
    loudness = 1.0
    for axis_at, shards_of in shards:
        heights = jax.random.uniform(jax.random.fold_in(jax.random.fold_in(own_key, 6), axis_at), (shards_of,), jnp.float32, low / len(shards), high / len(shards))
        loudness = loudness * jnp.repeat(jnp.exp(heights), dims[axis_at] // shards_of).reshape((-1,) + (1,) * (len(dims) - 1 - axis_at))
    return loudness


def scatter_about(stream_key, dims, deviation, most, cuts=(), kind=jnp.bfloat16):
    values = deviation * jax.random.normal(stream_key, dims, jnp.float32)
    if cuts:
        values = values * levels(stream_key, dims, cuts, -0.22, 0.18)
    return jnp.clip(values, -most, most).astype(kind)


def setup_inputs(seed: int = 0, part: int = 0) -> dict:
    key_list = jax.random.split(jax.random.key(seed), 10)
    own_keys = jax.random.split(jax.random.fold_in(key_list[9], part), 10)
    innovation = scatter_about(own_keys[0], (NX, NY), 1.0, 6.0, ((0, 4), (1, 2)), jnp.float32)
    cluster = plant(jax.random.randint(own_keys[1], (NX, NY), 0, ADJ + 1), jax.random.fold_in(own_keys[1], 1), 0, ADJ).astype(jnp.int32)
    kernel = jnp.clip(0.2 + 1.3 * jax.random.uniform(key_list[2], (LEV, NX, NY), jnp.float32) ** levels(key_list[2], (LEV, NX, NY), ((1, 4), (2, 2)), -0.2, 0.2), 0.2, 1.5)
    wind_x = jnp.clip(jax.random.uniform(key_list[3], (LEV, NX, NY), jnp.float32, -0.24, 0.24) * levels(key_list[3], (LEV, NX, NY), ((1, 4), (2, 2)), -0.4, 0.0), -0.24, 0.24)
    wind_y = jnp.clip(jax.random.uniform(key_list[4], (LEV, NX, NY), jnp.float32, -0.24, 0.24) * levels(key_list[4], (LEV, NX, NY), ((1, 4), (2, 2)), -0.4, 0.0), -0.24, 0.24)
    conv_strength = jnp.clip(0.9 * jax.random.uniform(key_list[5], (NX, NY), jnp.float32) ** levels(key_list[5], (NX, NY), ((0, 4), (1, 2)), -0.2, 0.2), 0.0, 0.9)
    conv_matrix = draw_conv_matrix(jax.random.fold_in(key_list[9], 71), part)
    margin_cell = draw_margin_cell(jax.random.fold_in(key_list[9], 71), part)
    margin_weight = draw_margin_weight(jax.random.fold_in(key_list[9], 71), part)
    return {"innovation": innovation, "cluster": cluster, "kernel": kernel, "wind_x": wind_x, "wind_y": wind_y, "conv_strength": conv_strength, "conv_matrix": conv_matrix, "margin_cell": margin_cell, "margin_weight": margin_weight}


def transport(adjoint, wind_x, wind_y):
    east_rate = jnp.maximum(wind_x, 0.0)
    west_rate = jnp.minimum(jnp.roll(wind_x, 1, axis=1), 0.0)
    north_rate = jnp.maximum(wind_y, 0.0)
    south_rate = jnp.pad(jnp.minimum(wind_y[:, :, :-1], 0.0), ((0, 0), (0, 0), (1, 0)))
    east = jnp.roll(adjoint, -1, axis=1)
    west = jnp.roll(adjoint, 1, axis=1)
    north = jnp.pad(adjoint[:, :, 1:], ((0, 0), (0, 0), (0, 1)))
    south = jnp.pad(adjoint[:, :, :-1], ((0, 0), (0, 0), (1, 0)))
    center = 1.0 - east_rate + west_rate - north_rate + south_rate
    return adjoint * center + east_rate * east - west_rate * west + north_rate * north - south_rate * south


def convect(adjoint, strength, matrix):
    mixed = jnp.einsum("lk,lxy->kxy", matrix, adjoint, precision=lax.Precision.HIGHEST)
    return adjoint + strength * (mixed - adjoint)


def reference(innovation, cluster, kernel, wind_x, wind_y, conv_strength, conv_matrix, margin_cell, margin_weight):
    def single(index):
        adjoint = jnp.where(cluster == index, innovation, 0.0)[None] * kernel
        for step in range(NSTEP):
            adjoint = convect(adjoint, conv_strength, conv_matrix)
            adjoint = transport(adjoint, wind_x, wind_y)
        surface = adjoint[0].reshape(-1)
        values = surface[margin_cell]
        return adjoint, jnp.sum(margin_weight * values, axis=1)

    field, sensed = lax.map(single, jnp.arange(ADJ, dtype=jnp.int32))
    return (field, sensed)
```

```python
import functools

import jax
import jax.numpy as jnp
from jax import lax
from jax.experimental import pallas as pl
from jax.experimental.pallas import tpu as pltpu
from jax.sharding import PartitionSpec as P

ADJ = 8
NSTEP = 2
F32 = jnp.float32
BF16 = jnp.bfloat16


def vmem(value):
    return pltpu.with_memory_space_constraint(value, pltpu.VMEM)


def call(kernel, outs, args, scratch=(), hbm_out=(), name=None):
    out_shape = []
    out_specs = []
    for at, out in enumerate(outs):
        if at in hbm_out:
            out_shape.append(jax.ShapeDtypeStruct(out, F32))
            out_specs.append(pl.BlockSpec(memory_space=pl.ANY))
        else:
            out_shape.append(pltpu.VMEM(out, F32))
            out_specs.append(pl.BlockSpec(memory_space=pltpu.VMEM))
    return pl.pallas_call(
        kernel,
        out_shape=out_shape,
        in_specs=[pl.BlockSpec(memory_space=pltpu.VMEM)] * len(args),
        out_specs=out_specs,
        scratch_shapes=list(scratch),
        name=name,
    )(*[vmem(arg) for arg in args])


def split_matrix(matrix):
    lev = matrix.shape[0]
    turned = matrix.T
    high = turned.astype(BF16)
    high32 = high.astype(F32)
    low32 = turned - high32
    fill = jnp.zeros((-lev % 8, lev), F32)
    both = jnp.concatenate([high32, fill, low32, fill], axis=0).astype(BF16)
    return both, high


def mix(matrices, field):
    both, high_matrix = matrices
    lev = field.shape[0]
    pad = both.shape[0] // 2
    high = field.astype(BF16)
    low = (field - high.astype(F32)).astype(BF16)
    major = jnp.dot(both, high, preferred_element_type=F32)
    minor = jnp.dot(high_matrix, low, preferred_element_type=F32)
    return major[:lev] + (major[pad : pad + lev] + minor)


def lane_of(shape):
    return lax.broadcasted_iota(jnp.int32, shape, len(shape) - 1)


def turn(value, steps):
    steps = steps % value.shape[-1]
    return value if steps == 0 else pltpu.roll(value, steps, value.ndim - 1)


def column(ref, x, lev, width_x):
    return ref[pl.ds(x, lev, stride=width_x), :]


def pack_rim_kernel(lev, width_x, kernel_ref, wx_ref, wy_ref, innov_ref, cluster_ref, strength_ref, out_ref):
    lanes = kernel_ref.shape[1]
    pad = lev + -lev % 8
    half = 4 * width_x
    slot = lane_of((1, lanes)) // 4

    def packed(ref, first):
        total = jnp.zeros((lev, lanes), F32)
        for x in range(width_x):
            moved = turn(column(ref, x, lev, width_x), first + 4 * x + 2)
            total = jnp.where(slot == first // 4 + x, moved, total)
        return total

    def packed_row(value):
        total = jnp.zeros((1, lanes), F32)
        for x in range(width_x):
            total = jnp.where(slot == x, turn(value[x : x + 1], 4 * x + 2), total)
        return total

    upper = slot * 4 >= half
    out_ref[0:lev, :] = jnp.where(upper, packed(wy_ref, half), packed(kernel_ref, 0))
    out_ref[pad : pad + lev, :] = packed(wx_ref, 0)
    out_ref[2 * pad : 2 * pad + 1, :] = packed_row(innov_ref[...])
    out_ref[2 * pad + 1 : 2 * pad + 2, :] = packed_row(cluster_ref[...].astype(F32))
    out_ref[2 * pad + 2 : 2 * pad + 3, :] = packed_row(strength_ref[...])


def first_mix_kernel(lev, width_x, kernel_ref, innov_ref, strength_ref, matrix_ref, out_ref):
    matrices = split_matrix(matrix_ref[...])
    for x in range(0, width_x, 2):
        tiles = [column(kernel_ref, at, lev, width_x) * innov_ref[at : at + 1, :] for at in (x, x + 1)]
        lanes = tiles[0].shape[1]
        mixed = mix(matrices, jnp.concatenate(tiles, axis=1))
        for k, tile in enumerate(tiles):
            part = mixed[:, k * lanes : (k + 1) * lanes]
            out_ref[x + k, 0:lev, :] = tile + strength_ref[x + k : x + k + 1, :] * (part - tile)


def pack_ends_kernel(
    lev,
    width_x,
    subs,
    own_ref,
    south_ref,
    north_ref,
    c_ref,
    wx_ref,
    wy_ref,
    cluster_ref,
    strength_ref,
    matrix_ref,
    rim_ref,
    east_ref,
    west_ref,
):
    lanes = wx_ref.shape[1]
    pad = lev + -lev % 8
    half = 4 * width_x
    cross = lax.axis_index("sub")
    lane = lane_of((1, lanes))
    lower = lane < half
    southern = lane % 4 < 2
    present = jnp.where(southern, cross, subs - 1 - cross) > 0

    def halo(rows):
        value = jnp.where(southern, south_ref[rows, :], north_ref[rows, :])
        return jnp.where(present, value, 0.0)

    own = own_ref[0:lev, :]
    far = halo(slice(0, lev))
    far_misc = halo(slice(2 * pad, 2 * pad + 3))
    own_misc = own_ref[2 * pad : 2 * pad + 3, :]
    sources = [
        jnp.where(lower, own, 0.0) * own_misc[0:1],
        jnp.where(lower, far, 0.0) * far_misc[0:1],
    ]
    mixed = mix(split_matrix(matrix_ref[...]), jnp.concatenate(sources, axis=1))
    rim_c = sources[0] + own_misc[2:3] * (mixed[:, :lanes] - sources[0])
    far_c = sources[1] + far_misc[2:3] * (mixed[:, lanes:] - sources[1])
    own_wy = jnp.where(lower, turn(own, half), 0.0)
    far_wy = jnp.where(lower, turn(far, half), 0.0)
    far_wx = halo(slice(pad, pad + lev))
    for at, value in enumerate((rim_c, far_c, own_wy, far_wy, far_wx)):
        rim_ref[at * pad : at * pad + lev, :] = value
    base = 5 * pad
    rim_ref[base : base + 1, :] = own_misc[1:2]
    rim_ref[base + 1 : base + 2, :] = far_misc[1:2]
    rim_ref[base + 2 : base + 3, :] = far_misc[2:3]

    last = width_x - 1
    cluster = cluster_ref[...].astype(F32)
    corner_lane = lane // 4

    def corner(slot):
        away = -4 * slot
        value = turn(far_c, away)
        value = jnp.where(corner_lane == 1, turn(far_wy, away + 4), value)
        return jnp.where(corner_lane == 2, turn(far_wx, away + 8), value)

    def put(ref, tiles, near, next_one):
        for at, value in enumerate(tiles):
            ref[at * pad : at * pad + lev, :] = value
        base = len(tiles) * pad
        ref[base : base + 1, :] = cluster[near : near + 1]
        ref[base + 1 : base + 2, :] = cluster[next_one : next_one + 1]
        ref[base + 2 : base + 3, :] = strength_ref[near : near + 1, :]
        ref[base + 3 : base + 4, :] = turn(far_misc[1:2], -4 * near)

    put(
        east_ref,
        (
            c_ref[last, 0:lev, :],
            c_ref[last - 1, 0:lev, :],
            column(wx_ref, last, lev, width_x),
            column(wy_ref, last, lev, width_x),
            corner(last),
            column(wx_ref, last - 1, lev, width_x),
        ),
        last,
        last - 1,
    )
    put(
        west_ref,
        (
            c_ref[0, 0:lev, :],
            c_ref[1, 0:lev, :],
            column(wx_ref, 0, lev, width_x),
            column(wy_ref, 0, lev, width_x),
            corner(0),
        ),
        0,
        1,
    )


def steps_kernel(
    lev,
    width_x,
    subs,
    per_device,
    rim_ref,
    before_ref,
    after_ref,
    c_ref,
    wx_ref,
    wy_ref,
    cluster_ref,
    strength_ref,
    matrix_ref,
    out_ref,
    surface_ref,
    mixed_ref,
    field_ref,
    sem,
):
    lanes = wx_ref.shape[1]
    pad = lev + -lev % 8
    half = 4 * width_x
    cross = lax.axis_index("sub")
    first_id = (lax.axis_index("adj") * per_device).astype(F32)
    matrices = split_matrix(matrix_ref[...])
    lane = lane_of((1, lanes))
    place = lane % 4
    cluster = cluster_ref[...].astype(F32)

    def rows_of(ref, at):
        return ref[at * pad : at * pad + lev, :]

    before_base = 6 * pad
    after_base = 5 * pad
    rim_base = 5 * pad
    after_slot = lane // 4 == width_x
    before_slot = lane >= lanes - 4

    def with_corners(value, before, after):
        return jnp.where(before_slot, before, jnp.where(after_slot, after, value))

    corner_before = rows_of(before_ref, 4)
    corner_after = rows_of(after_ref, 4)
    rim_c = rows_of(rim_ref, 0)
    rim_wy = rows_of(rim_ref, 2)
    far_c = with_corners(rows_of(rim_ref, 1), turn(corner_before, -4), turn(corner_after, half))
    far_wy = with_corners(rows_of(rim_ref, 3), turn(corner_before, -8), turn(corner_after, half - 4))
    far_wx = jnp.where(before_slot, turn(corner_before, -12), rows_of(rim_ref, 4))
    rim_cluster = rim_ref[rim_base : rim_base + 1, :]
    far_cluster = with_corners(
        rim_ref[rim_base + 1 : rim_base + 2, :],
        turn(before_ref[before_base + 3 : before_base + 4, :], -4),
        turn(after_ref[after_base + 3 : after_base + 4, :], half),
    )
    far_strength = rim_ref[rim_base + 2 : rim_base + 3, :]

    def tile(ref, x):
        return column(ref, x, lev, width_x)

    def c_at(x):
        if x < 0:
            return rows_of(before_ref, -1 - x)
        if x >= width_x:
            return rows_of(after_ref, x - width_x)
        return c_ref[x, 0:lev, :]

    def wx_at(x):
        if x < 0:
            return rows_of(before_ref, 2 if x == -1 else 5)
        return rows_of(after_ref, 2) if x >= width_x else tile(wx_ref, x)

    def wy_at(x):
        if x < 0:
            return rows_of(before_ref, 3)
        return rows_of(after_ref, 3) if x >= width_x else tile(wy_ref, x)

    def cluster_at(x):
        if x < 0:
            return before_ref[before_base - 1 - x : before_base - x, :]
        if x >= width_x:
            at = after_base + x - width_x
            return after_ref[at : at + 1, :]
        return cluster[x : x + 1]

    def strength_at(x):
        if x < 0:
            return before_ref[before_base + 2 : before_base + 3, :]
        if x >= width_x:
            return after_ref[after_base + 2 : after_base + 3, :]
        return strength_ref[x : x + 1, :]

    def from_north(value, rim):
        return turn(jnp.where(lane == 0, rim, value), -1)

    def from_south(value, rim):
        return turn(jnp.where(lane == lanes - 1, rim, value), 1)

    def rates(wx, wx_west, wy, wy_south):
        east = jnp.maximum(wx, 0.0)
        west = jnp.maximum(-wx_west, 0.0)
        north = jnp.maximum(wy, 0.0)
        south = jnp.maximum(-wy_south, 0.0)
        return 1.0 - east - west - north - south, east, west, north, south

    def rates_at(x):
        wy = wy_at(x)
        return rates(wx_at(x), wx_at(x - 1), wy, from_south(wy, turn(far_wy, -4 * x - 2)))

    def parted(terms, clusters):
        fields = []
        for a in range(per_device):
            wanted = first_id + a
            parts = [jnp.where(where == wanted, term, 0.0) for term, where in zip(terms, clusters)]
            fields.append(((parts[0] + parts[1]) + (parts[2] + parts[3])) + parts[4])
        return fields

    def convect(fields, strength):
        mixed = mix(matrices, jnp.concatenate(fields, axis=1))
        return [f + strength * (mixed[:, k * lanes : (k + 1) * lanes] - f) for k, f in enumerate(fields)]

    for x in range(-1, width_x + 1):
        center, east, west, north, south = rates_at(x)
        own, own_cluster = c_at(x), cluster_at(x)
        rim = turn(far_c, -4 * x - 2)
        rim_row = turn(far_cluster, -4 * x - 2)
        terms = (
            center * own,
            east * c_at(x + 1),
            west * c_at(x - 1),
            north * from_north(own, rim),
            south * from_south(own, rim),
        )
        clusters = (
            own_cluster,
            cluster_at(x + 1),
            cluster_at(x - 1),
            from_north(own_cluster, rim_row),
            from_south(own_cluster, rim_row),
        )
        for a, value in enumerate(convect(parted(terms, clusters), strength_at(x))):
            mixed_ref[a, x + 1, 0:lev, :] = value

    def rim_north(far, own):
        return turn(jnp.where(place == 2, own, far), -1)

    def rim_south(far, own):
        return turn(jnp.where(place == 1, own, far), 1)

    center, east, west, north, south = rates(far_wx, turn(far_wx, 4), far_wy, rim_south(far_wy, rim_wy))
    terms = (
        center * far_c,
        east * turn(far_c, -4),
        west * turn(far_c, 4),
        north * rim_north(far_c, rim_c),
        south * rim_south(far_c, rim_c),
    )
    clusters = (
        far_cluster,
        turn(far_cluster, -4),
        turn(far_cluster, 4),
        rim_north(far_cluster, rim_cluster),
        rim_south(far_cluster, rim_cluster),
    )
    inside = jnp.where(lane < half, jnp.where(place < 2, cross, subs - 1 - cross), 0) > 0
    fields = [jnp.where(inside, f, 0.0) for f in parted(terms, clusters)]
    joined = [fields[a] + turn(fields[a + 1], half) for a in range(0, per_device, 2)]
    far_mixed = convect(joined, far_strength + turn(far_strength, half))

    copies = []
    for a in range(per_device):
        rim_field = far_mixed[a // 2]
        for x in range(width_x):
            center, east, west, north, south = rates_at(x)
            own = mixed_ref[a, x + 1, 0:lev, :]
            rim = turn(rim_field, -4 * x - 2 - half * (a % 2))
            value = (
                (center * own + east * mixed_ref[a, x + 2, 0:lev, :])
                + (west * mixed_ref[a, x, 0:lev, :] + north * from_north(own, rim))
                + south * from_south(own, rim)
            )
            field_ref[pl.ds(a * lev * width_x + x, lev, stride=width_x), :] = value
            surface_ref[a * width_x + x : a * width_x + x + 1, :] = value[0:1]
        rows = pl.ds(a * lev * width_x, lev * width_x)
        copies.append(pltpu.make_async_copy(field_ref.at[rows, :], out_ref.at[rows, :], sem.at[a]))
        copies[-1].start()
    for copy in copies:
        copy.wait()


def quotient(value, count):
    if count & (count - 1) == 0:
        return value >> (count.bit_length() - 1), value & (count - 1)
    return lax.div(value, count), lax.rem(value, count)


def sense_kernel(width_x, width_y, tiles, subs, per_device, n_rim, cell_ref, weight_ref, *refs):
    *blocks, out_ref = refs
    slots, elements = cell_ref.shape
    tile_pos = lax.axis_index("tiles")
    cross = lax.axis_index("sub")
    group = width_y
    rows = per_device * width_x

    def one_group(g, carry):
        lanes = pl.ds(pl.multiple_of(g * group, group), group)
        cell = cell_ref[:, lanes]
        weight = weight_ref[:, lanes]
        column_x, row_y = quotient(cell, width_y * subs)
        block_x, inner_x = quotient(column_x, width_x)
        block_y, lane_y = quotient(row_y, width_y)
        step = block_x - tile_pos
        step = jnp.where(step < -1, step + tiles, jnp.where(step > 1, step - tiles, step))
        if n_rim == 2:
            side = jnp.where(block_y == cross, 0, 1)
        else:
            side = block_y - cross + 1
        row_id = ((step + 1) * n_rim + side) * width_x + inner_x
        sums = [jnp.zeros((8, group), F32) for _ in range(per_device)]
        within = lax.broadcasted_iota(jnp.int32, (8, group), 0)
        for k in range(slots):
            pick = jnp.broadcast_to(lane_y[k : k + 1], (8, group))
            row = jnp.broadcast_to(row_id[k : k + 1], (8, group))
            share = jnp.broadcast_to(weight[k : k + 1], (8, group))
            for at in range(3 * n_rim):
                ref, base = blocks[at]
                for part in range(0, width_x, 8):
                    chosen = jnp.where(row == within + (at * width_x + part), share, 0.0)
                    for a in range(per_device):
                        first = base + a * width_x + part
                        value = jnp.take_along_axis(ref[first : first + 8, :], pick, axis=1)
                        sums[a] = sums[a] + chosen * value
        out_ref[:, lanes] = jnp.concatenate([jnp.sum(s, axis=0, keepdims=True) for s in sums], axis=0)
        return carry

    lax.fori_loop(0, elements // group, one_group, 0)


def ring(value, axis, steps):
    count = lax.axis_size(axis)
    return lax.ppermute(value, axis, [(i, (i + steps) % count) for i in range(count)])


def across(value):
    count = lax.axis_size("sub")
    if count == 2:
        other = ring(value, "sub", 1)
        return other, other
    from_south = lax.ppermute(value, "sub", [(i, i + 1) for i in range(count - 1)])
    from_north = lax.ppermute(value, "sub", [(i + 1, i) for i in range(count - 1)])
    return from_south, from_north


def body(
    innovation,
    cluster,
    kernel,
    wind_x,
    wind_y,
    conv_strength,
    conv_matrix,
    margin_cell,
    margin_weight,
):
    lev, width_x, width_y = kernel.shape
    tiles = lax.axis_size("tiles")
    subs = lax.axis_size("sub")
    per_device = ADJ // lax.axis_size("adj")
    pad = lev + -lev % 8
    flat_kernel = kernel.reshape(lev * width_x, width_y)
    flat_x = wind_x.reshape(lev * width_x, width_y)
    flat_y = wind_y.reshape(lev * width_x, width_y)

    (own_rim,) = call(
        functools.partial(pack_rim_kernel, lev, width_x),
        [(2 * pad + 8, width_y)],
        (flat_kernel, flat_x, flat_y, innovation, cluster, conv_strength),
        name="pack_rim",
    )
    south_rim, north_rim = across(own_rim)
    (first,) = call(
        functools.partial(first_mix_kernel, lev, width_x),
        [(width_x, pad, width_y)],
        (flat_kernel, innovation, conv_strength, conv_matrix),
        name="first_mix",
    )
    rim, to_east, to_west = call(
        functools.partial(pack_ends_kernel, lev, width_x, subs),
        [(5 * pad + 8, width_y), (6 * pad + 8, width_y), (5 * pad + 8, width_y)],
        (own_rim, south_rim, north_rim, first, flat_x, flat_y, cluster, conv_strength, conv_matrix),
        name="pack_ends",
    )
    before = ring(to_east, "tiles", 1)
    after = ring(to_west, "tiles", -1)
    field, surface = call(
        functools.partial(steps_kernel, lev, width_x, subs, per_device),
        [(per_device * lev * width_x, width_y), (per_device * width_x, width_y)],
        (rim, before, after, first, flat_x, flat_y, cluster, conv_strength, conv_matrix),
        scratch=(
            pltpu.VMEM((per_device, width_x + 2, pad, width_y), F32),
            pltpu.VMEM((per_device * lev * width_x, width_y), F32),
            pltpu.SemaphoreType.DMA((per_device,)),
        ),
        hbm_out=(0,),
        name="steps",
    )
    south_surface, north_surface = across(surface)
    if subs == 2:
        strip = [surface, south_surface]
    else:
        strip = [south_surface, surface, north_surface]
    n_rim = len(strip)
    whole = jnp.concatenate(strip, axis=0)
    surface_before = ring(whole, "tiles", 1)
    surface_after = ring(whole, "tiles", -1)
    rows = per_device * width_x

    def sense(cell_ref, weight_ref, before_ref, after_ref, *rest):
        *here, out_ref = rest
        blocks = [(before_ref, k * rows) for k in range(n_rim)]
        blocks += [(ref, 0) for ref in here]
        blocks += [(after_ref, k * rows) for k in range(n_rim)]
        sense_kernel(width_x, width_y, tiles, subs, per_device, n_rim, cell_ref, weight_ref, *blocks, out_ref)

    (sensed,) = call(
        sense,
        [(per_device, margin_cell.shape[0])],
        (margin_cell.T, margin_weight.T, surface_before, surface_after, *strip),
        name="sense",
    )
    return (field.reshape(per_device, lev, width_x, width_y), sensed)


def solution(mesh):
    in_specs = (
        P(("groups", "tiles"), "sub"),
        P(("groups", "tiles"), "sub"),
        P(None, "tiles", "sub"),
        P(None, "tiles", "sub"),
        P(None, "tiles", "sub"),
        P("tiles", "sub"),
        P(),
        P(("tiles", "sub"), None),
        P(("tiles", "sub"), None),
    )
    out_specs = (P(("groups", "adj"), None, "tiles", "sub"), P(("groups", "adj"), ("tiles", "sub")))
    return jax.shard_map(body, mesh=mesh, in_specs=in_specs, out_specs=out_specs, check_vma=False)
```

```python
import functools

import jax
import jax.numpy as jnp
from jax import lax
from jax.experimental import pallas as pl
from jax.experimental.pallas import tpu as pltpu
from jax.sharding import PartitionSpec as P

ADJ = 8
NSTEP = 2
F32 = jnp.float32
BF16 = jnp.bfloat16
VMEM_BYTES = 16 << 20


def call(kernel, outs, args, scratch=(), far_in=False, far_out=False, name=None, cost=0):
    near = pl.BlockSpec(memory_space=pltpu.VMEM)
    far = pl.BlockSpec(memory_space=pl.ANY)
    outs = [out if isinstance(out[-1], int) else out for out in outs]
    shapes = [(out, F32) if isinstance(out[-1], int) else out for out in outs]
    return pl.pallas_call(
        kernel,
        out_shape=[(jax.ShapeDtypeStruct if far_out else pltpu.VMEM)(*out) for out in shapes],
        in_specs=[far if far_in else near] * len(args),
        out_specs=[far if far_out else near] * len(outs),
        scratch_shapes=list(scratch),
        compiler_params=pltpu.CompilerParams(vmem_limit_bytes=VMEM_BYTES),
        cost_estimate=pl.CostEstimate(flops=cost, bytes_accessed=cost, transcendentals=0) if cost else None,
        name=name,
    )(*[pltpu.with_memory_space_constraint(arg, pltpu.HBM if far_in else pltpu.VMEM) for arg in args])


def round_up(count, unit):
    return count + -count % unit


def split(value):
    high = value.astype(BF16)
    return high, (value - high.astype(F32)).astype(BF16)


def mix(lhs, field):
    short = lhs.shape[1] // 3 - field.shape[0]
    if short:
        field = jnp.concatenate([field, jnp.zeros((short, field.shape[1]), F32)], axis=0)
    high, low = split(field)
    return jnp.dot(lhs, jnp.concatenate([high, high, low], axis=0), preferred_element_type=F32)


def lane_of(shape):
    return lax.broadcasted_iota(jnp.int32, shape, len(shape) - 1)


def turn(value, steps):
    steps = steps % value.shape[-1]
    return value if steps == 0 else pltpu.roll(value, steps, value.ndim - 1)


def total(parts):
    while len(parts) > 1:
        parts = [parts[i] + parts[i + 1] if i + 1 < len(parts) else parts[i] for i in range(0, len(parts), 2)]
    return parts[0]


def fetch_kernel(dims, *refs):
    lev, width_x, lanes = dims
    sources, (kernel, wx, wy, innov, cluster, strength, matrix, cell, weight, lhs, rim), scratch = (
        refs[:9],
        refs[9:20],
        refs[20:],
    )
    (sem,) = scratch
    pad = round_up(lev, 8)
    deep = lhs.shape[1] // 3
    half = 4 * width_x
    whole = lev * width_x
    targets = [ref.at[pl.ds(0, whole), :] for ref in (kernel, wx, wy)]
    targets += [innov, cluster, strength, matrix, cell, weight]
    copies = [pltpu.make_async_copy(s, t, sem.at[i]) for i, (s, t) in enumerate(zip(sources, targets))]
    for copy in copies:
        copy.start()
    for ref in (kernel, wx, wy):
        ref[pl.ds(whole, (pad - lev) * width_x), :] = jnp.zeros(((pad - lev) * width_x, lanes), F32)
    slot = lane_of((1, lanes)) // 4

    def packed(ref, first, r):
        value = jnp.zeros((8, lanes), F32)
        for x in range(width_x):
            moved = turn(ref[pl.ds(8 * r * width_x + x, 8, stride=width_x), :], first + 4 * x + 2)
            value = jnp.where(slot == first // 4 + x, moved, value)
        return value

    def packed_row(value):
        row = jnp.zeros((1, lanes), F32)
        for x in range(width_x):
            row = jnp.where(slot == x, turn(value[x : x + 1], 4 * x + 2), row)
        return row

    for copy in copies[3:7]:
        copy.wait()
    rim[2 * pad : 2 * pad + 1, :] = packed_row(innov[...])
    rim[2 * pad + 1 : 2 * pad + 2, :] = packed_row(cluster[...].astype(F32))
    rim[2 * pad + 2 : 2 * pad + 3, :] = packed_row(strength[...])
    rim[2 * pad + 3 : 2 * pad + 8, :] = jnp.zeros((5, lanes), F32)
    turned = matrix[...].T
    turned = jnp.concatenate([turned, jnp.zeros((pad - lev, lev), F32)], axis=0)
    turned = jnp.concatenate([turned, jnp.zeros((pad, deep - lev), F32)], axis=1)
    high = turned.astype(BF16).astype(F32)
    lhs[...] = jnp.concatenate([high, turned - high, high], axis=1).astype(BF16)
    for copy in copies[:3]:
        copy.wait()
    for r in range(pad // 8):
        rim[8 * r : 8 * r + 8, :] = jnp.where(slot * 4 >= half, packed(wy, half, r), packed(kernel, 0, r))
        rim[pad + 8 * r : pad + 8 * r + 8, :] = packed(wx, 0, r)
    for copy in copies[7:]:
        copy.wait()


def first_mix_kernel(dims, kernel_ref, innov_ref, strength_ref, lhs_ref, out_ref):
    lev, width_x, lanes = dims
    pad = round_up(lev, 8)
    lhs = lhs_ref[...]
    for x in range(0, width_x, 2):
        tiles = [kernel_ref[pl.ds(at, pad, stride=width_x), :] * innov_ref[at : at + 1, :] for at in (x, x + 1)]
        mixed = mix(lhs, jnp.concatenate(tiles, axis=1))
        for k, tile in enumerate(tiles):
            part = mixed[:, k * lanes : (k + 1) * lanes]
            out_ref[x + k, :, :] = tile + strength_ref[x + k : x + k + 1, :] * (part - tile)


def pack_ends_kernel(dims, subs, *refs):
    lev, width_x, lanes = dims
    own_ref, south_ref, north_ref, c_ref, wx_ref, wy_ref, cluster_ref, strength_ref, lhs_ref = refs[:9]
    rim_ref, east_ref, west_ref = refs[9:]
    pad = round_up(lev, 8)
    half = 4 * width_x
    cross = lax.axis_index("sub")
    lane = lane_of((1, lanes))
    lower = lane < half
    southern = lane % 4 < 2
    present = jnp.where(southern, cross, subs - 1 - cross) > 0

    def halo(rows):
        value = jnp.where(southern, south_ref[rows, :], north_ref[rows, :])
        return jnp.where(present, value, 0.0)

    own = own_ref[0:pad, :]
    far = halo(slice(0, pad))
    far_misc = halo(slice(2 * pad, 2 * pad + 8))
    own_misc = own_ref[2 * pad : 2 * pad + 8, :]
    sources = [
        jnp.where(lower, own, 0.0) * own_misc[0:1],
        jnp.where(lower, far, 0.0) * far_misc[0:1],
    ]
    mixed = mix(lhs_ref[...], jnp.concatenate(sources, axis=1))
    rim_c = sources[0] + own_misc[2:3] * (mixed[:, :lanes] - sources[0])
    far_c = sources[1] + far_misc[2:3] * (mixed[:, lanes:] - sources[1])
    own_wy = jnp.where(lower, turn(own, half), 0.0)
    far_wy = jnp.where(lower, turn(far, half), 0.0)
    far_wx = halo(slice(pad, 2 * pad))
    for at, value in enumerate((rim_c, far_c, own_wy, far_wy, far_wx)):
        rim_ref[at * pad : (at + 1) * pad, :] = value
    base = 5 * pad
    rim_ref[base : base + 1, :] = own_misc[1:2]
    rim_ref[base + 1 : base + 2, :] = far_misc[1:2]
    rim_ref[base + 2 : base + 8, :] = far_misc[2:8]

    last = width_x - 1
    cluster = cluster_ref[...].astype(F32)

    def upright(value):
        square = jnp.concatenate([value, jnp.zeros((lanes - pad, lanes), F32)], axis=0).T
        return square[0:4], square[4 * last : 4 * last + 4]

    corners = [
        c + turn(wy, pad) + turn(wx, 2 * pad)
        for c, wy, wx in zip(upright(far_c), upright(far_wy), upright(far_wx))
    ]

    def put(ref, tiles, near, next_one, corner):
        for at, value in enumerate(tiles):
            top = min(pad, ref.shape[0] - at * lev)
            ref[at * lev : at * lev + top, :] = value[:top]
        base = len(tiles) * lev
        ref[base : base + 1, :] = cluster[near : near + 1]
        ref[base + 1 : base + 2, :] = cluster[next_one : next_one + 1]
        ref[base + 2 : base + 3, :] = strength_ref[near : near + 1, :]
        ref[base + 3 : base + 4, :] = turn(far_misc[1:2], -4 * near)
        ref[base + 4 : base + 8, :] = corner

    def column(ref, x):
        return ref[pl.ds(x, pad, stride=width_x), :]

    ends = (c_ref[last], c_ref[last - 1], column(wx_ref, last), column(wy_ref, last), column(wx_ref, last - 1))
    put(east_ref, ends, last, last - 1, corners[1])
    put(west_ref, (c_ref[0], c_ref[1], column(wx_ref, 0), column(wy_ref, 0)), 0, 1, corners[0])


def rates_of(wx, wx_west, wy, wy_south):
    east = jnp.maximum(wx, 0.0)
    west = jnp.maximum(-wx_west, 0.0)
    north = jnp.maximum(wy, 0.0)
    south = jnp.maximum(-wy_south, 0.0)
    return (1.0 - east) - west - (north + south), east, west, north, south


def from_north(value, halo):
    lanes = value.shape[1]
    return jnp.where(lane_of((1, lanes)) == lanes - 1, halo, turn(value, -1))


def from_south(value, halo):
    return jnp.where(lane_of((1, value.shape[1])) == 0, halo, turn(value, 1))


def crossed(far):
    place = lane_of((1, far.shape[1])) % 4
    return jnp.where(place == 1, turn(far, -1), turn(far, 1))


def halo_of(far, x):
    return turn(far, -4 * x - 2)


def parted(terms, clusters, ids):
    return [total([jnp.where(c == wanted, t, 0.0) for t, c in zip(terms, clusters)]) for wanted in ids]


def convect(lhs, fields, strength):
    lanes = strength.shape[1]
    mixed = mix(lhs, jnp.concatenate(fields, axis=1))
    return [f + strength * (mixed[:, k * lanes : (k + 1) * lanes] - f) for k, f in enumerate(fields)]


def advance(dims, ids, lhs, x, at, rim):
    lev, width_x, lanes = dims
    pad = round_up(lev, 8)
    own_cluster = at.cluster(x)
    rim_row = halo_of(rim.cluster, x)
    clusters = (
        own_cluster,
        at.cluster(x + 1),
        at.cluster(x - 1),
        from_north(own_cluster, rim_row),
        from_south(own_cluster, rim_row),
    )
    clusters = [jnp.broadcast_to(c, (8, lanes)) for c in clusters]
    groups = []
    for r in range(pad // 8):
        wy, own = at.wy(x, r), at.c(x, r)
        south_wy = from_south(wy, halo_of(rim.wy(r), x))
        center, east, west, north, south = rates_of(at.wx(x, r), at.wx(x - 1, r), wy, south_wy)
        halo = halo_of(rim.c(r), x)
        terms = (
            center * own,
            east * at.c(x + 1, r),
            west * at.c(x - 1, r),
            north * from_north(own, halo),
            south * from_south(own, halo),
        )
        groups.append(parted(terms, clusters, ids))
    fields = [jnp.concatenate([group[a] for group in groups], axis=0) for a in range(len(ids))]
    return convect(lhs, fields, at.strength(x))


class Columns:
    def __init__(self, dims, c_ref, wx_ref, wy_ref, cluster_ref, strength_ref, before_ref=None, after_ref=None):
        self.lev, self.width_x, self.lanes = dims
        self.c_ref, self.wx_ref, self.wy_ref = c_ref, wx_ref, wy_ref
        self.cluster_rows = cluster_ref[...].astype(F32)
        self.strength_ref = strength_ref
        self.before_ref, self.after_ref = before_ref, after_ref

    def sent(self, ref, tile, r):
        first = tile * self.lev + 8 * r
        return ref[first : first + 8, :]

    def strided(self, ref, x, r):
        return ref[pl.ds(8 * r * self.width_x + x, 8, stride=self.width_x), :]

    def c(self, x, r):
        if x < 0:
            return self.sent(self.before_ref, -1 - x, r)
        if x >= self.width_x:
            return self.sent(self.after_ref, x - self.width_x, r)
        return self.c_ref[x, 8 * r : 8 * r + 8, :]

    def wx(self, x, r):
        if x < 0:
            return self.sent(self.before_ref, 2 if x == -1 else 4, r)
        return self.sent(self.after_ref, 2, r) if x >= self.width_x else self.strided(self.wx_ref, x, r)

    def wy(self, x, r):
        if x < 0:
            return self.sent(self.before_ref, 3, r)
        return self.sent(self.after_ref, 3, r) if x >= self.width_x else self.strided(self.wy_ref, x, r)

    def misc(self, ref, tiles, row):
        return ref[tiles * self.lev + row : tiles * self.lev + row + 1, :]

    def cluster(self, x):
        if x < 0:
            return self.misc(self.before_ref, 5, -1 - x)
        if x >= self.width_x:
            return self.misc(self.after_ref, 4, x - self.width_x)
        return self.cluster_rows[x : x + 1]

    def strength(self, x):
        if x < 0:
            return self.misc(self.before_ref, 5, 2)
        if x >= self.width_x:
            return self.misc(self.after_ref, 4, 2)
        return self.strength_ref[x : x + 1, :]


class Rim:
    def __init__(self, c, wy, cluster):
        self.c_tile, self.wy_tile, self.cluster = crossed(c), crossed(wy), crossed(cluster)

    def c(self, r):
        return self.c_tile[8 * r : 8 * r + 8]

    def wy(self, r):
        return self.wy_tile[8 * r : 8 * r + 8]


def adjoint_ids(per_device):
    first = (lax.axis_index("adj") * per_device).astype(F32)
    return [first + a for a in range(per_device)]


def inner_kernel(dims, per_device, rim_ref, c_ref, wx_ref, wy_ref, cluster_ref, strength_ref, lhs_ref, mixed_ref):
    lev, width_x, lanes = dims
    pad = round_up(lev, 8)
    at = Columns(dims, c_ref, wx_ref, wy_ref, cluster_ref, strength_ref)
    base = 5 * pad
    rim = Rim(rim_ref[pad : 2 * pad, :], rim_ref[3 * pad : 4 * pad, :], rim_ref[base + 1 : base + 2, :])
    ids = adjoint_ids(per_device)
    lhs = lhs_ref[...]
    for x in range(1, width_x - 1):
        for a, value in enumerate(advance(dims, ids, lhs, x, at, rim)):
            mixed_ref[a, x - 1, :, :] = value


def mixed_at(dims, inner_ref, ends_ref, a, x, r):
    width_x = dims[1]
    rows = slice(8 * r, 8 * r + 8)
    if 1 <= x < width_x - 1:
        return inner_ref[a, x - 1, rows, :]
    return ends_ref[a, x + 1 if x < 1 else x - width_x + 3, rows, :]


def second_transport(dims, at, rim_wy, far, inner_ref, ends_ref, ids, x, r):
    half = 4 * dims[1]
    wy = at.wy(x, r)
    south_wy = from_south(wy, halo_of(rim_wy, x))
    center, east, west, north, south = rates_of(at.wx(x, r), at.wx(x - 1, r), wy, south_wy)
    values = []
    for a in range(len(ids)):
        own = mixed_at(dims, inner_ref, ends_ref, a, x, r)
        halo = turn(far(a // 2, r), -4 * x - 2 - half * (a % 2))
        parts = [
            center * own,
            east * mixed_at(dims, inner_ref, ends_ref, a, x + 1, r),
            west * mixed_at(dims, inner_ref, ends_ref, a, x - 1, r),
            north * from_north(own, halo),
            south * from_south(own, halo),
        ]
        values.append(total(parts))
    return values


def ends_kernel(dims, subs, per_device, *refs):
    lev, width_x, lanes = dims
    rim_ref, before_ref, after_ref, inner_ref, c_ref, wx_ref, wy_ref, cluster_ref, strength_ref, lhs_ref = refs[:10]
    ends_ref, far_ref, surface_ref = refs[10:]
    pad = round_up(lev, 8)
    half = 4 * width_x
    cross = lax.axis_index("sub")
    lane = lane_of((1, lanes))
    place = lane % 4
    after_slot = lane // 4 == width_x
    before_slot = lane >= lanes - 4
    at = Columns(dims, c_ref, wx_ref, wy_ref, cluster_ref, strength_ref, before_ref, after_ref)
    ids = adjoint_ids(per_device)
    lhs = lhs_ref[...]

    def upright(ref, tiles):
        rows = ref[tiles * lev + 4 : tiles * lev + 8, :]
        square = jnp.concatenate([rows, jnp.zeros((lanes - 4, lanes), F32)], axis=0).T
        return [square[i * pad : (i + 1) * pad] for i in range(3)]

    def with_corners(value, before, after):
        return jnp.where(before_slot, turn(before, -4), jnp.where(after_slot, turn(after, half), value))

    corner_before = upright(before_ref, 5)
    corner_after = upright(after_ref, 4)
    base = 5 * pad
    rim_c = rim_ref[0:pad, :]
    rim_wy = rim_ref[2 * pad : 3 * pad, :]
    far_c = with_corners(rim_ref[pad : 2 * pad, :], corner_before[0], corner_after[0])
    far_wy = with_corners(rim_ref[3 * pad : 4 * pad, :], corner_before[1], corner_after[1])
    far_wx = with_corners(rim_ref[4 * pad : 5 * pad, :], corner_before[2], corner_after[2])
    rim_cluster = rim_ref[base : base + 1, :]
    far_cluster = with_corners(
        rim_ref[base + 1 : base + 2, :], at.misc(before_ref, 5, 3), at.misc(after_ref, 4, 3)
    )
    far_strength = rim_ref[base + 2 : base + 3, :]
    rim = Rim(far_c, far_wy, far_cluster)
    for k, x in enumerate((-1, 0, width_x - 1, width_x)):
        for a, value in enumerate(advance(dims, ids, lhs, x, at, rim)):
            ends_ref[a, k, :, :] = value

    def rim_north(far, own):
        return turn(jnp.where(place == 2, own, far), -1)

    def rim_south(far, own):
        return turn(jnp.where(place == 1, own, far), 1)

    center, east, west, north, south = rates_of(far_wx, turn(far_wx, 4), far_wy, rim_south(far_wy, rim_wy))
    terms = (
        center * far_c,
        east * turn(far_c, -4),
        west * turn(far_c, 4),
        north * rim_north(far_c, rim_c),
        south * rim_south(far_c, rim_c),
    )
    clusters = (
        far_cluster,
        turn(far_cluster, -4),
        turn(far_cluster, 4),
        rim_north(far_cluster, rim_cluster),
        rim_south(far_cluster, rim_cluster),
    )
    inside = jnp.where(lane < half, jnp.where(place < 2, cross, subs - 1 - cross), 0) > 0
    fields = [jnp.where(inside, f, 0.0) for f in parted(terms, clusters, ids)]
    joined = [fields[a] + turn(fields[a + 1], half) for a in range(0, per_device, 2)]
    far_mixed = [crossed(f) for f in convect(lhs, joined, far_strength + turn(far_strength, half))]
    for at_pair, value in enumerate(far_mixed):
        far_ref[at_pair, 0:pad, :] = value
    far_ref[0, pad : pad + 8, :] = jnp.zeros((8, lanes), F32)
    for pair in range(1, len(far_mixed)):
        far_ref[pair, pad : pad + 8, :] = jnp.zeros((8, lanes), F32)

    def far(pair, r):
        return far_mixed[pair][8 * r : 8 * r + 8]

    for x in range(width_x):
        values = second_transport(dims, at, rim.wy(0), far, inner_ref, ends_ref, ids, x, 0)
        for a, value in enumerate(values):
            surface_ref[a * width_x + x : a * width_x + x + 1, :] = value[0:1]


def output_kernel(dims, per_device, *refs):
    lev, width_x, lanes = dims
    rim_ref, before_ref, inner_ref, ends_ref, far_ref, wx_ref, wy_ref, cluster_ref, strength_ref = refs[:9]
    out_ref, field_ref, sem = refs[9:]
    pad = round_up(lev, 8)
    at = Columns(dims, None, wx_ref, wy_ref, cluster_ref, strength_ref, before_ref)
    ids = range(per_device)

    def far(pair, r):
        return far_ref[pair, 8 * r : 8 * r + 8, :]

    rim_wys = [crossed(rim_ref[3 * pad + 8 * r : 3 * pad + 8 * r + 8, :]) for r in range(pad // 8)]
    copies = []
    for x in range(width_x):
        for r in range(pad // 8):
            rim_wy = rim_wys[r]
            values = second_transport(dims, at, rim_wy, far, inner_ref, ends_ref, ids, x, r)
            for a, value in enumerate(values):
                field_ref[a, x, 8 * r : 8 * r + 8, :] = value
        for a in range(per_device):
            source = field_ref.at[a, x, pl.ds(0, lev), :]
            copies.append(pltpu.make_async_copy(source, out_ref.at[a, :, x, 0, :], sem.at[len(copies)]))
            copies[-1].start()
    for copy in copies:
        copy.wait()


def quotient(value, count):
    if count & (count - 1) == 0:
        return value >> (count.bit_length() - 1), value & (count - 1)
    return lax.div(value, count), lax.rem(value, count)


def sense_kernel(width_x, width_y, tiles, subs, per_device, n_rim, blocks, cell_ref, weight_ref, partial_ref, out_ref):
    slots, elements = cell_ref.shape
    tile_pos = lax.axis_index("tiles")
    cross = lax.axis_index("sub")
    group = width_y

    def one_group(g, carry):
        lanes = pl.ds(pl.multiple_of(g * group, group), group)
        cell = cell_ref[:, lanes]
        weight = weight_ref[:, lanes]
        column_x, row_y = quotient(cell, width_y * subs)
        block_x, inner_x = quotient(column_x, width_x)
        block_y, lane_y = quotient(row_y, width_y)
        step = block_x - tile_pos
        step = jnp.where(step < -1, step + tiles, jnp.where(step > 1, step - tiles, step))
        if n_rim == 2:
            side = jnp.where(block_y == cross, 0, 1)
        else:
            side = block_y - cross + 1
        row_id = ((step + 1) * n_rim + side) * width_x + inner_x
        sums = [jnp.zeros((8, group), F32) for _ in range(per_device)]
        within = lax.broadcasted_iota(jnp.int32, (8, group), 0)
        for k in range(slots):
            pick = jnp.broadcast_to(lane_y[k : k + 1], (8, group))
            row = jnp.broadcast_to(row_id[k : k + 1], (8, group)) - within
            share = jnp.broadcast_to(weight[k : k + 1], (8, group))
            for at_step, at_side, ref, base in blocks:
                for part in range(0, width_x, 8):
                    first_id = ((at_step + 1) * n_rim + at_side) * width_x + part
                    chosen = jnp.where(row == first_id, share, 0.0)
                    for a in range(per_device):
                        first = base + a * width_x + part
                        value = jnp.take_along_axis(ref[first : first + 8, :], pick, axis=1)
                        sums[a] = sums[a] + chosen * value
        sensed = jnp.concatenate([jnp.sum(s, axis=0, keepdims=True) for s in sums], axis=0)
        if partial_ref is not None:
            sensed = sensed + partial_ref[:, lanes]
        out_ref[:, lanes] = sensed
        return carry

    lax.fori_loop(0, elements // group, one_group, 0)


def ring(value, axis, steps):
    count = lax.axis_size(axis)
    return lax.ppermute(value, axis, [(i, (i + steps) % count) for i in range(count)])


def across(value):
    count = lax.axis_size("sub")
    if count == 2:
        other = ring(value, "sub", 1)
        return other, other
    from_south = lax.ppermute(value, "sub", [(i, i + 1) for i in range(count - 1)])
    from_north = lax.ppermute(value, "sub", [(i + 1, i) for i in range(count - 1)])
    return from_south, from_north


def body(
    innovation,
    cluster,
    kernel,
    wind_x,
    wind_y,
    conv_strength,
    conv_matrix,
    margin_cell,
    margin_weight,
):
    dims = kernel.shape
    lev, width_x, width_y = dims
    tiles = lax.axis_size("tiles")
    subs = lax.axis_size("sub")
    per_device = ADJ // lax.axis_size("adj")
    pad = round_up(lev, 8)
    deep = round_up(lev, 16)
    flat = (lev * width_x, width_y)
    tall = (pad * width_x, width_y)
    small = innovation.shape
    sources = (
        kernel.reshape(flat),
        wind_x.reshape(flat),
        wind_y.reshape(flat),
        innovation,
        cluster,
        conv_strength,
        conv_matrix,
        margin_cell.T,
        margin_weight.T,
    )
    outs = [tall, tall, tall, small, (small, jnp.int32), small, conv_matrix.shape]
    outs += [(sources[7].shape, jnp.int32), sources[8].shape, ((pad, 3 * deep), BF16), (2 * pad + 8, width_y)]
    fetched = call(
        functools.partial(fetch_kernel, dims),
        outs,
        sources,
        scratch=(pltpu.SemaphoreType.DMA((len(sources),)),),
        far_in=True,
        name="fetch",
    )
    air, wx, wy, innov, group, strength, _, cell, weight, lhs, own_rim = fetched
    south_rim, north_rim = across(own_rim)
    (first,) = call(
        functools.partial(first_mix_kernel, dims),
        [(width_x, pad, width_y)],
        (air, innov, strength, lhs),
        name="first_mix",
        cost=400000,
    )
    rim, to_east, to_west = call(
        functools.partial(pack_ends_kernel, dims, subs),
        [(5 * pad + 8, width_y), (5 * lev + 8, width_y), (4 * lev + 8, width_y)],
        (own_rim, south_rim, north_rim, first, wx, wy, group, strength, lhs),
        name="pack_ends",
    )
    before = ring(to_east, "tiles", 1)
    after = ring(to_west, "tiles", -1)
    (inner,) = call(
        functools.partial(inner_kernel, dims, per_device),
        [(per_device, width_x - 2, pad, width_y)],
        (rim, first, wx, wy, group, strength, lhs),
        name="inner",
        cost=4000000,
    )
    ends, far, surface = call(
        functools.partial(ends_kernel, dims, subs, per_device),
        [
            (per_device, 4, pad, width_y),
            ((per_device + 1) // 2, pad + 8, width_y),
            (per_device * width_x, width_y),
        ],
        (rim, before, after, inner, first, wx, wy, group, strength, lhs),
        name="ends",
    )
    south_surface, north_surface = across(surface)
    (field,) = call(
        functools.partial(output_kernel, dims, per_device),
        [(per_device, lev, width_x, 1, width_y)],
        (rim, before, inner, ends, far, wx, wy, group, strength),
        scratch=(
            pltpu.VMEM((per_device, width_x, pad, width_y), F32),
            pltpu.SemaphoreType.DMA((per_device * width_x,)),
        ),
        far_out=True,
        name="output",
        cost=4000000,
    )
    if subs == 2:
        strip = [surface, south_surface]
    else:
        strip = [south_surface, surface, north_surface]
    n_rim = len(strip)
    whole = jnp.concatenate(strip, axis=0)
    surface_after = ring(whole, "tiles", -1)
    surface_before = ring(whole, "tiles", 1)
    rows = per_device * width_x
    looked_up = functools.partial(sense_kernel, width_x, width_y, tiles, subs, per_device, n_rim)

    def sense_here(cell_ref, weight_ref, *rest):
        *here, out_ref = rest
        looked_up([(0, k, ref, 0) for k, ref in enumerate(here)], cell_ref, weight_ref, None, out_ref)

    def sense_beside(step, cell_ref, weight_ref, partial_ref, block_ref, out_ref):
        blocks = [(step, k, block_ref, k * rows) for k in range(n_rim)]
        looked_up(blocks, cell_ref, weight_ref, partial_ref, out_ref)

    sensed_shape = [(per_device, cell.shape[1])]
    (sensed,) = call(sense_here, sensed_shape, (cell, weight, *strip), name="sense_here", cost=2000000)
    for step, block in ((1, surface_after), (-1, surface_before)):
        (sensed,) = call(
            functools.partial(sense_beside, step), sensed_shape, (cell, weight, sensed, block), name="sense_beside", cost=2000000
        )
    return (field.reshape(per_device, lev, width_x, width_y), sensed)


def solution(mesh):
    in_specs = (
        P(("groups", "tiles"), "sub"),
        P(("groups", "tiles"), "sub"),
        P(None, "tiles", "sub"),
        P(None, "tiles", "sub"),
        P(None, "tiles", "sub"),
        P("tiles", "sub"),
        P(),
        P(("tiles", "sub"), None),
        P(("tiles", "sub"), None),
    )
    out_specs = (P(("groups", "adj"), None, "tiles", "sub"), P(("groups", "adj"), ("tiles", "sub")))
    return jax.shard_map(body, mesh=mesh, in_specs=in_specs, out_specs=out_specs, check_vma=False)
```

```python
import functools

import jax
import jax.numpy as jnp
from jax import lax
from jax.experimental import pallas as pl
from jax.experimental.pallas import tpu as pltpu
from jax.sharding import PartitionSpec as P

ADJ = 8
NSTEP = 2
F32 = jnp.float32
BF16 = jnp.bfloat16
VMEM_BYTES = 16 << 20


def call(kernel, outs, args, scratch=(), far_in=False, far_out=(), name=None, cost=0):
    near = pl.BlockSpec(memory_space=pltpu.VMEM)
    far = pl.BlockSpec(memory_space=pl.ANY)
    outs = [out if isinstance(out[-1], int) else out for out in outs]
    shapes = [(out, F32) if isinstance(out[-1], int) else out for out in outs]
    return pl.pallas_call(
        kernel,
        out_shape=[(jax.ShapeDtypeStruct if at in far_out else pltpu.VMEM)(*out) for at, out in enumerate(shapes)],
        in_specs=[far if far_in else near] * len(args),
        out_specs=[far if at in far_out else near for at in range(len(outs))],
        scratch_shapes=list(scratch),
        compiler_params=pltpu.CompilerParams(vmem_limit_bytes=VMEM_BYTES),
        cost_estimate=pl.CostEstimate(flops=cost, bytes_accessed=cost, transcendentals=0) if cost else None,
        name=name,
    )(*[pltpu.with_memory_space_constraint(arg, pltpu.HBM if far_in else pltpu.VMEM) for arg in args])


def round_up(count, unit):
    return count + -count % unit


def split(value):
    high = value.astype(BF16)
    return high, (value - high.astype(F32)).astype(BF16)


def mix(lhs, field):
    short = lhs.shape[1] // 3 - field.shape[0]
    if short:
        field = jnp.concatenate([field, jnp.zeros((short, field.shape[1]), F32)], axis=0)
    high, low = split(field)
    return jnp.dot(lhs, jnp.concatenate([high, high, low], axis=0), preferred_element_type=F32)


def lane_of(shape):
    return lax.broadcasted_iota(jnp.int32, shape, len(shape) - 1)


def turn(value, steps):
    steps = steps % value.shape[-1]
    return value if steps == 0 else pltpu.roll(value, steps, value.ndim - 1)


def total(parts):
    while len(parts) > 1:
        parts = [parts[i] + parts[i + 1] if i + 1 < len(parts) else parts[i] for i in range(0, len(parts), 2)]
    return parts[0]


def fetch_kernel(dims, *refs):
    lev, width_x, lanes = dims
    sources, (kernel, wx, wy, innov, cluster, strength, matrix, cell, weight, lhs, rim), scratch = (
        refs[:9],
        refs[9:20],
        refs[20:],
    )
    (sem,) = scratch
    pad = round_up(lev, 8)
    deep = lhs.shape[1] // 3
    half = 4 * width_x
    whole = lev * width_x
    targets = [ref.at[pl.ds(0, whole), :] for ref in (kernel, wx, wy)]
    targets += [innov, cluster, strength, matrix, cell, weight]
    copies = [pltpu.make_async_copy(s, t, sem.at[i]) for i, (s, t) in enumerate(zip(sources, targets))]
    for copy in copies:
        copy.start()
    for ref in (kernel, wx, wy):
        ref[pl.ds(whole, (pad - lev) * width_x), :] = jnp.zeros(((pad - lev) * width_x, lanes), F32)
    slot = lane_of((1, lanes)) // 4

    def packed(ref, first, r):
        value = jnp.zeros((8, lanes), F32)
        for x in range(width_x):
            moved = turn(ref[pl.ds(8 * r * width_x + x, 8, stride=width_x), :], first + 4 * x + 2)
            value = jnp.where(slot == first // 4 + x, moved, value)
        return value

    def packed_row(value):
        row = jnp.zeros((1, lanes), F32)
        for x in range(width_x):
            row = jnp.where(slot == x, turn(value[x : x + 1], 4 * x + 2), row)
        return row

    for copy in copies[3:7]:
        copy.wait()
    rim[2 * pad : 2 * pad + 1, :] = packed_row(innov[...])
    rim[2 * pad + 1 : 2 * pad + 2, :] = packed_row(cluster[...].astype(F32))
    rim[2 * pad + 2 : 2 * pad + 3, :] = packed_row(strength[...])
    rim[2 * pad + 3 : 2 * pad + 8, :] = jnp.zeros((5, lanes), F32)
    turned = matrix[...].T
    turned = jnp.concatenate([turned, jnp.zeros((pad - lev, lev), F32)], axis=0)
    turned = jnp.concatenate([turned, jnp.zeros((pad, deep - lev), F32)], axis=1)
    high = turned.astype(BF16).astype(F32)
    lhs[...] = jnp.concatenate([high, turned - high, high], axis=1).astype(BF16)
    for copy in copies[:3]:
        copy.wait()
    for r in range(pad // 8):
        rim[8 * r : 8 * r + 8, :] = jnp.where(slot * 4 >= half, packed(wy, half, r), packed(kernel, 0, r))
        rim[pad + 8 * r : pad + 8 * r + 8, :] = packed(wx, 0, r)
    for copy in copies[7:]:
        copy.wait()


def first_mix_kernel(dims, kernel_ref, innov_ref, strength_ref, lhs_ref, out_ref):
    lev, width_x, lanes = dims
    pad = round_up(lev, 8)
    lhs = lhs_ref[...]
    for x in range(0, width_x, 2):
        tiles = [kernel_ref[pl.ds(at, pad, stride=width_x), :] * innov_ref[at : at + 1, :] for at in (x, x + 1)]
        mixed = mix(lhs, jnp.concatenate(tiles, axis=1))
        for k, tile in enumerate(tiles):
            part = mixed[:, k * lanes : (k + 1) * lanes]
            out_ref[x + k, :, :] = tile + strength_ref[x + k : x + k + 1, :] * (part - tile)


def pack_ends_kernel(dims, subs, *refs):
    lev, width_x, lanes = dims
    own_ref, south_ref, north_ref, c_ref, wx_ref, wy_ref, cluster_ref, strength_ref, lhs_ref = refs[:9]
    rim_ref, east_ref, west_ref = refs[9:]
    pad = round_up(lev, 8)
    half = 4 * width_x
    cross = lax.axis_index("sub")
    lane = lane_of((1, lanes))
    lower = lane < half
    southern = lane % 4 < 2
    present = jnp.where(southern, cross, subs - 1 - cross) > 0

    def halo(rows):
        value = jnp.where(southern, south_ref[rows, :], north_ref[rows, :])
        return jnp.where(present, value, 0.0)

    own = own_ref[0:pad, :]
    far = halo(slice(0, pad))
    far_misc = halo(slice(2 * pad, 2 * pad + 8))
    own_misc = own_ref[2 * pad : 2 * pad + 8, :]
    sources = [
        jnp.where(lower, own, 0.0) * own_misc[0:1],
        jnp.where(lower, far, 0.0) * far_misc[0:1],
    ]
    mixed = mix(lhs_ref[...], jnp.concatenate(sources, axis=1))
    rim_c = sources[0] + own_misc[2:3] * (mixed[:, :lanes] - sources[0])
    far_c = sources[1] + far_misc[2:3] * (mixed[:, lanes:] - sources[1])
    own_wy = jnp.where(lower, turn(own, half), 0.0)
    far_wy = jnp.where(lower, turn(far, half), 0.0)
    far_wx = halo(slice(pad, 2 * pad))
    for at, value in enumerate((rim_c, far_c, own_wy, far_wy, far_wx)):
        rim_ref[at * pad : (at + 1) * pad, :] = value
    base = 5 * pad
    rim_ref[base : base + 1, :] = own_misc[1:2]
    rim_ref[base + 1 : base + 2, :] = far_misc[1:2]
    rim_ref[base + 2 : base + 8, :] = far_misc[2:8]

    last = width_x - 1
    cluster = cluster_ref[...].astype(F32)

    def upright(value):
        square = jnp.concatenate([value, jnp.zeros((lanes - pad, lanes), F32)], axis=0).T
        return square[0:4], square[4 * last : 4 * last + 4]

    corners = [
        c + turn(wy, pad) + turn(wx, 2 * pad)
        for c, wy, wx in zip(upright(far_c), upright(far_wy), upright(far_wx))
    ]

    def put(ref, tiles, near, next_one, corner):
        for at, value in enumerate(tiles):
            top = min(pad, ref.shape[0] - at * lev)
            ref[at * lev : at * lev + top, :] = value[:top]
        base = len(tiles) * lev
        ref[base : base + 1, :] = cluster[near : near + 1]
        ref[base + 1 : base + 2, :] = cluster[next_one : next_one + 1]
        ref[base + 2 : base + 3, :] = strength_ref[near : near + 1, :]
        ref[base + 3 : base + 4, :] = turn(far_misc[1:2], -4 * near)
        ref[base + 4 : base + 8, :] = corner

    def column(ref, x):
        return ref[pl.ds(x, pad, stride=width_x), :]

    ends = (c_ref[last], c_ref[last - 1], column(wx_ref, last), column(wy_ref, last), column(wx_ref, last - 1))
    put(east_ref, ends, last, last - 1, corners[1])
    put(west_ref, (c_ref[0], c_ref[1], column(wx_ref, 0), column(wy_ref, 0)), 0, 1, corners[0])


def rates_of(wx, wx_west, wy, wy_south):
    east = jnp.maximum(wx, 0.0)
    west = jnp.maximum(-wx_west, 0.0)
    north = jnp.maximum(wy, 0.0)
    south = jnp.maximum(-wy_south, 0.0)
    return (1.0 - east) - west - (north + south), east, west, north, south


def from_north(value, halo):
    lanes = value.shape[1]
    return jnp.where(lane_of((1, lanes)) == lanes - 1, halo, turn(value, -1))


def from_south(value, halo):
    return jnp.where(lane_of((1, value.shape[1])) == 0, halo, turn(value, 1))


def crossed(far):
    place = lane_of((1, far.shape[1])) % 4
    return jnp.where(place == 1, turn(far, -1), turn(far, 1))


def halo_of(far, x):
    return turn(far, -4 * x - 2)


def parted(terms, clusters, ids):
    return [total([jnp.where(c == wanted, t, 0.0) for t, c in zip(terms, clusters)]) for wanted in ids]


def convect(lhs, fields, strength):
    lanes = strength.shape[1]
    mixed = mix(lhs, jnp.concatenate(fields, axis=1))
    return [f + strength * (mixed[:, k * lanes : (k + 1) * lanes] - f) for k, f in enumerate(fields)]


def advance(dims, ids, lhs, x, at, rim):
    lev, width_x, lanes = dims
    pad = round_up(lev, 8)
    own_cluster = at.cluster(x)
    rim_row = halo_of(rim.cluster, x)
    clusters = (
        own_cluster,
        at.cluster(x + 1),
        at.cluster(x - 1),
        from_north(own_cluster, rim_row),
        from_south(own_cluster, rim_row),
    )
    clusters = [jnp.broadcast_to(c, (8, lanes)) for c in clusters]
    groups = []
    for r in range(pad // 8):
        wy, own = at.wy(x, r), at.c(x, r)
        south_wy = from_south(wy, halo_of(rim.wy(r), x))
        center, east, west, north, south = rates_of(at.wx(x, r), at.wx(x - 1, r), wy, south_wy)
        halo = halo_of(rim.c(r), x)
        terms = (
            center * own,
            east * at.c(x + 1, r),
            west * at.c(x - 1, r),
            north * from_north(own, halo),
            south * from_south(own, halo),
        )
        groups.append(parted(terms, clusters, ids))
    fields = [jnp.concatenate([group[a] for group in groups], axis=0) for a in range(len(ids))]
    return convect(lhs, fields, at.strength(x))


class Columns:
    def __init__(self, dims, c_ref, wx_ref, wy_ref, cluster_ref, strength_ref, before_ref=None, after_ref=None):
        self.lev, self.width_x, self.lanes = dims
        self.c_ref, self.wx_ref, self.wy_ref = c_ref, wx_ref, wy_ref
        self.cluster_rows = cluster_ref[...].astype(F32)
        self.strength_ref = strength_ref
        self.before_ref, self.after_ref = before_ref, after_ref

    def sent(self, ref, tile, r):
        first = tile * self.lev + 8 * r
        return ref[first : first + 8, :]

    def strided(self, ref, x, r):
        return ref[pl.ds(8 * r * self.width_x + x, 8, stride=self.width_x), :]

    def c(self, x, r):
        if x < 0:
            return self.sent(self.before_ref, -1 - x, r)
        if x >= self.width_x:
            return self.sent(self.after_ref, x - self.width_x, r)
        return self.c_ref[x, 8 * r : 8 * r + 8, :]

    def wx(self, x, r):
        if x < 0:
            return self.sent(self.before_ref, 2 if x == -1 else 4, r)
        return self.sent(self.after_ref, 2, r) if x >= self.width_x else self.strided(self.wx_ref, x, r)

    def wy(self, x, r):
        if x < 0:
            return self.sent(self.before_ref, 3, r)
        return self.sent(self.after_ref, 3, r) if x >= self.width_x else self.strided(self.wy_ref, x, r)

    def misc(self, ref, tiles, row):
        return ref[tiles * self.lev + row : tiles * self.lev + row + 1, :]

    def cluster(self, x):
        if x < 0:
            return self.misc(self.before_ref, 5, -1 - x)
        if x >= self.width_x:
            return self.misc(self.after_ref, 4, x - self.width_x)
        return self.cluster_rows[x : x + 1]

    def strength(self, x):
        if x < 0:
            return self.misc(self.before_ref, 5, 2)
        if x >= self.width_x:
            return self.misc(self.after_ref, 4, 2)
        return self.strength_ref[x : x + 1, :]


class Rim:
    def __init__(self, c, wy, cluster):
        self.c_tile, self.wy_tile, self.cluster = crossed(c), crossed(wy), crossed(cluster)

    def c(self, r):
        return self.c_tile[8 * r : 8 * r + 8]

    def wy(self, r):
        return self.wy_tile[8 * r : 8 * r + 8]


def adjoint_ids(per_device):
    first = (lax.axis_index("adj") * per_device).astype(F32)
    return [first + a for a in range(per_device)]


def inner_kernel(dims, per_device, rim_ref, c_ref, wx_ref, wy_ref, cluster_ref, strength_ref, lhs_ref, mixed_ref):
    lev, width_x, lanes = dims
    pad = round_up(lev, 8)
    at = Columns(dims, c_ref, wx_ref, wy_ref, cluster_ref, strength_ref)
    base = 5 * pad
    rim = Rim(rim_ref[pad : 2 * pad, :], rim_ref[3 * pad : 4 * pad, :], rim_ref[base + 1 : base + 2, :])
    ids = adjoint_ids(per_device)
    lhs = lhs_ref[...]
    for x in range(1, width_x - 1):
        for a, value in enumerate(advance(dims, ids, lhs, x, at, rim)):
            mixed_ref[a, x - 1, :, :] = value


def mixed_at(dims, inner_ref, ends_ref, a, x, r):
    width_x = dims[1]
    rows = slice(8 * r, 8 * r + 8)
    if 1 <= x < width_x - 1:
        return inner_ref[a, x - 1, rows, :]
    return ends_ref[a, x + 1 if x < 1 else x - width_x + 3, rows, :]


def second_transport(dims, at, rim_wy, far, inner_ref, ends_ref, ids, x, r):
    half = 4 * dims[1]
    wy = at.wy(x, r)
    south_wy = from_south(wy, halo_of(rim_wy, x))
    center, east, west, north, south = rates_of(at.wx(x, r), at.wx(x - 1, r), wy, south_wy)
    values = []
    for a in range(len(ids)):
        own = mixed_at(dims, inner_ref, ends_ref, a, x, r)
        halo = turn(far(a // 2, r), -4 * x - 2 - half * (a % 2))
        parts = [
            center * own,
            east * mixed_at(dims, inner_ref, ends_ref, a, x + 1, r),
            west * mixed_at(dims, inner_ref, ends_ref, a, x - 1, r),
            north * from_north(own, halo),
            south * from_south(own, halo),
        ]
        values.append(total(parts))
    return values


def ends_kernel(dims, subs, per_device, *refs):
    lev, width_x, lanes = dims
    rim_ref, before_ref, after_ref, inner_ref, c_ref, wx_ref, wy_ref, cluster_ref, strength_ref, lhs_ref = refs[:10]
    ends_ref, far_ref, surface_ref = refs[10:]
    pad = round_up(lev, 8)
    half = 4 * width_x
    cross = lax.axis_index("sub")
    lane = lane_of((1, lanes))
    place = lane % 4
    after_slot = lane // 4 == width_x
    before_slot = lane >= lanes - 4
    at = Columns(dims, c_ref, wx_ref, wy_ref, cluster_ref, strength_ref, before_ref, after_ref)
    ids = adjoint_ids(per_device)
    lhs = lhs_ref[...]

    def upright(ref, tiles):
        rows = ref[tiles * lev + 4 : tiles * lev + 8, :]
        square = jnp.concatenate([rows, jnp.zeros((lanes - 4, lanes), F32)], axis=0).T
        return [square[i * pad : (i + 1) * pad] for i in range(3)]

    def with_corners(value, before, after):
        return jnp.where(before_slot, turn(before, -4), jnp.where(after_slot, turn(after, half), value))

    corner_before = upright(before_ref, 5)
    corner_after = upright(after_ref, 4)
    base = 5 * pad
    rim_c = rim_ref[0:pad, :]
    rim_wy = rim_ref[2 * pad : 3 * pad, :]
    far_c = with_corners(rim_ref[pad : 2 * pad, :], corner_before[0], corner_after[0])
    far_wy = with_corners(rim_ref[3 * pad : 4 * pad, :], corner_before[1], corner_after[1])
    far_wx = with_corners(rim_ref[4 * pad : 5 * pad, :], corner_before[2], corner_after[2])
    rim_cluster = rim_ref[base : base + 1, :]
    far_cluster = with_corners(
        rim_ref[base + 1 : base + 2, :], at.misc(before_ref, 5, 3), at.misc(after_ref, 4, 3)
    )
    far_strength = rim_ref[base + 2 : base + 3, :]
    rim = Rim(far_c, far_wy, far_cluster)
    for k, x in enumerate((-1, 0, width_x - 1, width_x)):
        for a, value in enumerate(advance(dims, ids, lhs, x, at, rim)):
            ends_ref[a, k, :, :] = value

    def rim_north(far, own):
        return turn(jnp.where(place == 2, own, far), -1)

    def rim_south(far, own):
        return turn(jnp.where(place == 1, own, far), 1)

    center, east, west, north, south = rates_of(far_wx, turn(far_wx, 4), far_wy, rim_south(far_wy, rim_wy))
    terms = (
        center * far_c,
        east * turn(far_c, -4),
        west * turn(far_c, 4),
        north * rim_north(far_c, rim_c),
        south * rim_south(far_c, rim_c),
    )
    clusters = (
        far_cluster,
        turn(far_cluster, -4),
        turn(far_cluster, 4),
        rim_north(far_cluster, rim_cluster),
        rim_south(far_cluster, rim_cluster),
    )
    inside = jnp.where(lane < half, jnp.where(place < 2, cross, subs - 1 - cross), 0) > 0
    fields = [jnp.where(inside, f, 0.0) for f in parted(terms, clusters, ids)]
    joined = [fields[a] + turn(fields[a + 1], half) for a in range(0, per_device, 2)]
    far_mixed = [crossed(f) for f in convect(lhs, joined, far_strength + turn(far_strength, half))]
    for at_pair, value in enumerate(far_mixed):
        far_ref[at_pair, 0:pad, :] = value
    far_ref[0, pad : pad + 8, :] = jnp.zeros((8, lanes), F32)
    for pair in range(1, len(far_mixed)):
        far_ref[pair, pad : pad + 8, :] = jnp.zeros((8, lanes), F32)

    def far(pair, r):
        return far_mixed[pair][8 * r : 8 * r + 8]

    for x in range(width_x):
        values = second_transport(dims, at, rim.wy(0), far, inner_ref, ends_ref, ids, x, 0)
        for a, value in enumerate(values):
            surface_ref[a * width_x + x : a * width_x + x + 1, :] = value[0:1]


def output_kernel(dims, per_device, *refs):
    lev, width_x, lanes = dims
    rim_ref, before_ref, inner_ref, ends_ref, far_ref, wx_ref, wy_ref, cluster_ref, strength_ref = refs[:9]
    out_ref, token_ref, field_ref, sem = refs[9:]
    token_ref[...] = jnp.zeros(token_ref.shape, F32)
    pad = round_up(lev, 8)
    at = Columns(dims, None, wx_ref, wy_ref, cluster_ref, strength_ref, before_ref)
    ids = range(per_device)

    def far(pair, r):
        return far_ref[pair, 8 * r : 8 * r + 8, :]

    rim_wys = [crossed(rim_ref[3 * pad + 8 * r : 3 * pad + 8 * r + 8, :]) for r in range(pad // 8)]
    copies = []
    for x in range(width_x):
        for r in range(pad // 8):
            rim_wy = rim_wys[r]
            values = second_transport(dims, at, rim_wy, far, inner_ref, ends_ref, ids, x, r)
            for a, value in enumerate(values):
                field_ref[a, x, 8 * r : 8 * r + 8, :] = value
        for a in range(per_device):
            source = field_ref.at[a, x, pl.ds(0, lev), :]
            copies.append(pltpu.make_async_copy(source, out_ref.at[a, :, x, 0, :], sem.at[len(copies)]))
            copies[-1].start()
    for copy in copies:
        copy.wait()


def quotient(value, count):
    if count & (count - 1) == 0:
        return value >> (count.bit_length() - 1), value & (count - 1)
    return lax.div(value, count), lax.rem(value, count)


def tables_kernel(dims, tiles, subs, n_rim, cell_ref, weight_ref, hot_ref, share_ref):
    _, width_x, width_y = dims
    slots, elements = cell_ref.shape
    tile_pos = lax.axis_index("tiles")
    cross = lax.axis_index("sub")
    column_x, row_y = quotient(cell_ref[...], width_y * subs)
    block_x, inner_x = quotient(column_x, width_x)
    block_y, lane_y = quotient(row_y, width_y)
    step = block_x - tile_pos
    step = jnp.where(step < -1, step + tiles, jnp.where(step > 1, step - tiles, step))
    if n_rim == 2:
        side = jnp.where(block_y == cross, 0, 1)
    else:
        side = block_y - cross + 1
    at_y = side * width_y + lane_y
    at_x = (step + 1) * width_x + inner_x
    weight = weight_ref[...]
    group = width_y
    rows = lax.broadcasted_iota(jnp.int32, (16, group), 0)
    for g in range(0, elements, group):
        lanes = slice(g, g + group)
        for k in range(slots):
            y = jnp.broadcast_to(at_y[k : k + 1, lanes], (16, group)) - rows
            for first in range(0, n_rim * width_y, 16):
                hot_ref[k, first : first + 16, lanes] = jnp.where(y == first, 1.0, 0.0).astype(BF16)
            x = jnp.broadcast_to(at_x[k : k + 1, lanes], (16, group)) - rows
            w = jnp.broadcast_to(weight[k : k + 1, lanes], (16, group))
            for first in range(0, 3 * width_x, 16):
                share_ref[k, first : first + 16, lanes] = jnp.where(x == first, w, 0.0)


def looked_up(dims, per_device, n_rim, blocks, hot_ref, share_ref, lanes):
    width_x = dims[1]
    rows = per_device * width_x
    surfaces = [split(jnp.concatenate(places, axis=1)) for _, places in blocks]
    lhs = jnp.concatenate([part for pair in surfaces for part in pair], axis=0)
    sums = [None] * per_device
    for k in range(hot_ref.shape[0]):
        found = jnp.dot(lhs, hot_ref[k, :, lanes], preferred_element_type=F32)
        for at, (step, _) in enumerate(blocks):
            share = share_ref[k, (step + 1) * width_x : (step + 2) * width_x, lanes]
            for a in range(per_device):
                high = 2 * at * rows + a * width_x
                low = high + rows
                value = (found[high : high + width_x] + found[low : low + width_x]) * share
                sums[a] = value if sums[a] is None else sums[a] + value
    return jnp.concatenate([jnp.sum(s, axis=0, keepdims=True) for s in sums], axis=0)


def wide_lanes(elements):
    wide = 256 if elements % 256 == 0 else 128
    return [slice(g, g + wide) for g in range(0, elements, wide)]


def sense_here_kernel(dims, per_device, hot_ref, share_ref, *refs):
    *here, out_ref = refs
    blocks = [(0, [ref[...] for ref in here])]
    for lanes in wide_lanes(out_ref.shape[1]):
        out_ref[:, lanes] = looked_up(dims, per_device, len(here), blocks, hot_ref, share_ref, lanes)


def sense_kernel(dims, per_device, n_rim, hot_ref, share_ref, partial_ref, before_ref, after_ref, out_ref, own_ref, sem):
    rows = per_device * dims[1]
    blocks = [
        (step, [ref[k * rows : (k + 1) * rows, :] for k in range(n_rim)])
        for step, ref in ((-1, before_ref), (1, after_ref))
    ]
    for lanes in wide_lanes(own_ref.shape[1]):
        value = looked_up(dims, per_device, n_rim, blocks, hot_ref, share_ref, lanes)
        own_ref[:, lanes] = partial_ref[:, lanes] + value
    copy = pltpu.make_async_copy(own_ref, out_ref, sem)
    copy.start()
    copy.wait()


def join_kernel(*refs):
    *parts, _, out_ref = refs
    first = 0
    for part in parts:
        out_ref[first : first + part.shape[0], :] = part[...]
        first += part.shape[0]


def ring(value, axis, steps):
    count = lax.axis_size(axis)
    return lax.ppermute(value, axis, [(i, (i + steps) % count) for i in range(count)])


def across(value):
    count = lax.axis_size("sub")
    if count == 2:
        other = ring(value, "sub", 1)
        return other, other
    from_south = lax.ppermute(value, "sub", [(i, i + 1) for i in range(count - 1)])
    from_north = lax.ppermute(value, "sub", [(i + 1, i) for i in range(count - 1)])
    return from_south, from_north


def body(
    innovation,
    cluster,
    kernel,
    wind_x,
    wind_y,
    conv_strength,
    conv_matrix,
    margin_cell,
    margin_weight,
):
    dims = kernel.shape
    lev, width_x, width_y = dims
    tiles = lax.axis_size("tiles")
    subs = lax.axis_size("sub")
    per_device = ADJ // lax.axis_size("adj")
    pad = round_up(lev, 8)
    deep = round_up(lev, 16)
    flat = (lev * width_x, width_y)
    tall = (pad * width_x, width_y)
    small = innovation.shape
    sources = (
        kernel.reshape(flat),
        wind_x.reshape(flat),
        wind_y.reshape(flat),
        innovation,
        cluster,
        conv_strength,
        conv_matrix,
        margin_cell.T,
        margin_weight.T,
    )
    outs = [tall, tall, tall, small, (small, jnp.int32), small, conv_matrix.shape]
    outs += [(sources[7].shape, jnp.int32), sources[8].shape, ((pad, 3 * deep), BF16), (2 * pad + 8, width_y)]
    fetched = call(
        functools.partial(fetch_kernel, dims),
        outs,
        sources,
        scratch=(pltpu.SemaphoreType.DMA((len(sources),)),),
        far_in=True,
        name="fetch",
    )
    air, wx, wy, innov, group, strength, _, cell, weight, lhs, own_rim = fetched
    south_rim, north_rim = across(own_rim)
    (first,) = call(
        functools.partial(first_mix_kernel, dims),
        [(width_x, pad, width_y)],
        (air, innov, strength, lhs),
        name="first_mix",
        cost=400000,
    )
    rim, to_east, to_west = call(
        functools.partial(pack_ends_kernel, dims, subs),
        [(5 * pad + 8, width_y), (5 * lev + 8, width_y), (4 * lev + 8, width_y)],
        (own_rim, south_rim, north_rim, first, wx, wy, group, strength, lhs),
        name="pack_ends",
    )
    before = ring(to_east, "tiles", 1)
    after = ring(to_west, "tiles", -1)
    (inner,) = call(
        functools.partial(inner_kernel, dims, per_device),
        [(per_device, width_x - 2, pad, width_y)],
        (rim, first, wx, wy, group, strength, lhs),
        name="inner",
        cost=4000000,
    )
    ends, far, surface = call(
        functools.partial(ends_kernel, dims, subs, per_device),
        [
            (per_device, 4, pad, width_y),
            ((per_device + 1) // 2, pad + 8, width_y),
            (per_device * width_x, width_y),
        ],
        (rim, before, after, inner, first, wx, wy, group, strength, lhs),
        name="ends",
    )
    south_surface, north_surface = across(surface)
    field, token = call(
        functools.partial(output_kernel, dims, per_device),
        [(per_device, lev, width_x, 1, width_y), (8, width_y)],
        (rim, before, inner, ends, far, wx, wy, group, strength),
        scratch=(
            pltpu.VMEM((per_device, width_x, pad, width_y), F32),
            pltpu.SemaphoreType.DMA((per_device * width_x,)),
        ),
        far_out=(0,),
        name="output",
        cost=4000000,
    )
    if subs == 2:
        strip = [surface, south_surface]
    else:
        strip = [south_surface, surface, north_surface]
    n_rim = len(strip)
    rows = per_device * width_x
    (whole,) = call(join_kernel, [(n_rim * rows, width_y)], (*strip, token), name="join")
    surface_before = ring(whole, "tiles", 1)
    surface_after = ring(whole, "tiles", -1)
    slots, elements = cell.shape
    hot, share = call(
        functools.partial(tables_kernel, dims, tiles, subs, n_rim),
        [((slots, n_rim * width_y, elements), BF16), (slots, 3 * width_x, elements)],
        (cell, weight),
        name="tables",
        cost=2000000,
    )
    (partial,) = call(
        functools.partial(sense_here_kernel, dims, per_device),
        [(per_device, elements)],
        (hot, share, *strip),
        name="sense_here",
        cost=2000000,
    )
    (sensed,) = call(
        functools.partial(sense_kernel, dims, per_device, n_rim),
        [(per_device, elements)],
        (hot, share, partial, surface_before, surface_after),
        scratch=(pltpu.VMEM((per_device, elements), F32), pltpu.SemaphoreType.DMA),
        far_out=(0,),
        name="sense",
    )
    return (field.reshape(per_device, lev, width_x, width_y), sensed)


def solution(mesh):
    in_specs = (
        P(("groups", "tiles"), "sub"),
        P(("groups", "tiles"), "sub"),
        P(None, "tiles", "sub"),
        P(None, "tiles", "sub"),
        P(None, "tiles", "sub"),
        P("tiles", "sub"),
        P(),
        P(("tiles", "sub"), None),
        P(("tiles", "sub"), None),
    )
    out_specs = (P(("groups", "adj"), None, "tiles", "sub"), P(("groups", "adj"), ("tiles", "sub")))
    return jax.shard_map(body, mesh=mesh, in_specs=in_specs, out_specs=out_specs, check_vma=False)
```

```python
import functools

import jax
import jax.numpy as jnp
from jax import lax
from jax.experimental import pallas as pl
from jax.experimental.pallas import tpu as pltpu
from jax.sharding import PartitionSpec as P

ADJ = 8
NSTEP = 2
F32 = jnp.float32
BF16 = jnp.bfloat16
VMEM_BYTES = 16 << 20
RIM_TILES = 6


def call(kernel, outs, args, scratch=(), far_in=False, far_out=(), name=None, cost=0):
    near = pl.BlockSpec(memory_space=pltpu.VMEM)
    far = pl.BlockSpec(memory_space=pl.ANY)
    outs = [out if isinstance(out[-1], int) else out for out in outs]
    shapes = [(out, F32) if isinstance(out[-1], int) else out for out in outs]
    return pl.pallas_call(
        kernel,
        out_shape=[(jax.ShapeDtypeStruct if at in far_out else pltpu.VMEM)(*out) for at, out in enumerate(shapes)],
        in_specs=[far if far_in else near] * len(args),
        out_specs=[far if at in far_out else near for at in range(len(outs))],
        scratch_shapes=list(scratch),
        compiler_params=pltpu.CompilerParams(vmem_limit_bytes=VMEM_BYTES),
        cost_estimate=pl.CostEstimate(flops=cost, bytes_accessed=cost, transcendentals=0) if cost else None,
        name=name,
    )(*[pltpu.with_memory_space_constraint(arg, pltpu.HBM if far_in else pltpu.VMEM) for arg in args])


def round_up(count, unit):
    return count + -count % unit


def split(value):
    high = value.astype(BF16)
    return high, (value - high.astype(F32)).astype(BF16)


def mix(lhs, field):
    short = lhs.shape[1] // 3 - field.shape[0]
    if short:
        field = jnp.concatenate([field, jnp.zeros((short, field.shape[1]), F32)], axis=0)
    high, low = split(field)
    return jnp.dot(lhs, jnp.concatenate([high, high, low], axis=0), preferred_element_type=F32)


def lane_of(shape):
    return lax.broadcasted_iota(jnp.int32, shape, len(shape) - 1)


def turn(value, steps):
    steps = steps % value.shape[-1]
    return value if steps == 0 else pltpu.roll(value, steps, value.ndim - 1)


def total(parts):
    while len(parts) > 1:
        parts = [parts[i] + parts[i + 1] if i + 1 < len(parts) else parts[i] for i in range(0, len(parts), 2)]
    return parts[0]


def fetch_kernel(dims, *refs):
    lev, width_x, lanes = dims
    sources, (kernel, wx, wy, innov, cluster, strength, matrix, cell, weight, lhs, rim), scratch = (
        refs[:9],
        refs[9:20],
        refs[20:],
    )
    (sem,) = scratch
    pad = round_up(lev, 8)
    deep = lhs.shape[1] // 3
    half = 4 * width_x
    whole = lev * width_x
    copies = [pltpu.make_async_copy(s, t, sem.at[i]) for i, (s, t) in enumerate(zip(sources[3:], refs[12:18]))]
    targets = [ref.at[pl.ds(0, whole), :] for ref in (kernel, wx, wy)]
    large = [pltpu.make_async_copy(s, t, sem.at[6 + i]) for i, (s, t) in enumerate(zip(sources, targets))]
    for copy in copies[:4] + large + copies[4:]:
        copy.start()
    for ref in (kernel, wx, wy):
        ref[pl.ds(whole, (pad - lev) * width_x), :] = jnp.zeros(((pad - lev) * width_x, lanes), F32)
    slot = lane_of((1, lanes)) // 4

    def packed(ref, first, r):
        value = jnp.zeros((8, lanes), F32)
        for x in range(width_x):
            moved = turn(ref[pl.ds(8 * r * width_x + x, 8, stride=width_x), :], first + 4 * x + 2)
            value = jnp.where(slot == first // 4 + x, moved, value)
        return value

    def packed_row(value):
        moved = pltpu.roll(value, 2, 1, stride=4, stride_axis=0)
        own = lax.broadcasted_iota(jnp.int32, value.shape, 0) == slot
        return jnp.sum(jnp.where(own, moved, 0.0), axis=0, keepdims=True)

    for copy in copies[:4]:
        copy.wait()
    rim[2 * pad : 2 * pad + 1, :] = packed_row(innov[...])
    rim[2 * pad + 1 : 2 * pad + 2, :] = packed_row(cluster[...].astype(F32))
    rim[2 * pad + 2 : 2 * pad + 3, :] = packed_row(strength[...])
    rim[2 * pad + 3 : 2 * pad + 8, :] = jnp.zeros((5, lanes), F32)
    turned = matrix[...].T
    turned = jnp.concatenate([turned, jnp.zeros((pad - lev, lev), F32)], axis=0)
    turned = jnp.concatenate([turned, jnp.zeros((pad, deep - lev), F32)], axis=1)
    high = turned.astype(BF16).astype(F32)
    lhs[...] = jnp.concatenate([high, turned - high, high], axis=1).astype(BF16)
    groups = [slice(8 * r, 8 * r + 8) for r in range(pad // 8)]
    large[0].wait()
    lower = [packed(kernel, 0, r) for r in range(pad // 8)]
    large[2].wait()
    for r, rows in enumerate(groups):
        rim[rows, :] = jnp.where(slot * 4 >= half, packed(wy, half, r), lower[r])
    large[1].wait()
    for r in range(pad // 8):
        rim[pad + 8 * r : pad + 8 * r + 8, :] = packed(wx, 0, r)
    for copy in copies[4:]:
        copy.wait()


def first_mix_kernel(dims, *refs):
    lev, width_x, lanes = dims
    kernel_ref, innov_ref, strength_ref, lhs_ref, wx_ref, wy_ref, cluster_ref, out_ref, east_ref, west_ref = refs
    pad = round_up(lev, 8)
    lhs = lhs_ref[...]
    last = width_x - 1
    cluster = cluster_ref[...].astype(F32)
    held = {}
    order = [0, width_x - 2] + list(range(2, width_x - 2, 2))

    def column(ref, x):
        return ref[pl.ds(x, pad, stride=width_x), :]

    def put(ref, tiles, near, next_one):
        for at, value in enumerate(tiles):
            top = min(pad, ref.shape[0] - at * lev)
            ref[at * lev : at * lev + top, :] = value[:top]
        base = len(tiles) * lev
        ref[base : base + 1, :] = cluster[near : near + 1]
        ref[base + 1 : base + 2, :] = cluster[next_one : next_one + 1]
        ref[base + 2 : base + 3, :] = strength_ref[near : near + 1, :]
        ref[base + 3 : base + 4, :] = jnp.zeros((1, lanes), F32)

    for x in order:
        tiles = [column(kernel_ref, at) * innov_ref[at : at + 1, :] for at in (x, x + 1)]
        mixed = mix(lhs, jnp.concatenate(tiles, axis=1))
        for k, tile in enumerate(tiles):
            part = mixed[:, k * lanes : (k + 1) * lanes]
            held[x + k] = tile + strength_ref[x + k : x + k + 1, :] * (part - tile)
            out_ref[x + k, :, :] = held[x + k]
        if x == width_x - 2:
            ends = (held[last], held[last - 1], column(wx_ref, last), column(wy_ref, last), column(wx_ref, last - 1))
            put(east_ref, ends, last, last - 1)
            put(west_ref, (held[0], held[1], column(wx_ref, 0), column(wy_ref, 0)), 0, 1)


def rim_kernel(dims, subs, own_ref, south_ref, north_ref, lhs_ref, rim_ref):
    lev, width_x, lanes = dims
    pad = round_up(lev, 8)
    half = 4 * width_x
    cross = lax.axis_index("sub")
    lane = lane_of((1, lanes))
    lower = lane < half
    southern = lane % 4 < 2
    present = jnp.where(southern, cross, subs - 1 - cross) > 0

    def halo(rows):
        value = jnp.where(southern, south_ref[rows, :], north_ref[rows, :])
        return jnp.where(present, value, 0.0)

    own = own_ref[0:pad, :]
    far = halo(slice(0, pad))
    far_misc = halo(slice(2 * pad, 2 * pad + 8))
    own_misc = own_ref[2 * pad : 2 * pad + 8, :]
    sources = [
        jnp.where(lower, own, 0.0) * own_misc[0:1],
        jnp.where(lower, far, 0.0) * far_misc[0:1],
    ]
    mixed = mix(lhs_ref[...], jnp.concatenate(sources, axis=1))
    rim_c = sources[0] + own_misc[2:3] * (mixed[:, :lanes] - sources[0])
    far_c = sources[1] + far_misc[2:3] * (mixed[:, lanes:] - sources[1])
    own_wy = jnp.where(lower, turn(own, half), 0.0)
    far_wy = jnp.where(lower, turn(far, half), 0.0)
    far_wx = halo(slice(pad, 2 * pad))
    for at, value in enumerate((rim_c, far_c, own_wy, far_wy, far_wx, own_ref[pad : 2 * pad, :])):
        rim_ref[at * pad : (at + 1) * pad, :] = value
    base = RIM_TILES * pad
    rim_ref[base : base + 1, :] = own_misc[1:2]
    rim_ref[base + 1 : base + 3, :] = far_misc[1:3]
    rim_ref[base + 3 : base + 4, :] = own_misc[2:3]
    rim_ref[base + 4 : base + 8, :] = jnp.zeros((4, lanes), F32)


def rates_of(wx, wx_west, wy, wy_south):
    east = jnp.maximum(wx, 0.0)
    west = jnp.maximum(-wx_west, 0.0)
    north = jnp.maximum(wy, 0.0)
    south = jnp.maximum(-wy_south, 0.0)
    return (1.0 - east) - west - (north + south), east, west, north, south


def from_north(value, halo):
    lanes = value.shape[1]
    return jnp.where(lane_of((1, lanes)) == lanes - 1, halo, turn(value, -1))


def from_south(value, halo):
    return jnp.where(lane_of((1, value.shape[1])) == 0, halo, turn(value, 1))


def crossed(far):
    place = lane_of((1, far.shape[1])) % 4
    return jnp.where(place == 1, turn(far, -1), turn(far, 1))


def halo_of(far, x):
    return turn(far, -4 * x - 2)


def parted(terms, clusters, ids):
    return [total([jnp.where(c == wanted, t, 0.0) for t, c in zip(terms, clusters)]) for wanted in ids]


def convect(lhs, fields, strength):
    lanes = strength.shape[1]
    mixed = mix(lhs, jnp.concatenate(fields, axis=1))
    return [f + strength * (mixed[:, k * lanes : (k + 1) * lanes] - f) for k, f in enumerate(fields)]


def advance(dims, ids, lhs, x, at, rim):
    lev, width_x, lanes = dims
    pad = round_up(lev, 8)
    own_cluster = at.cluster(x)
    rim_row = halo_of(rim.cluster, x)
    clusters = (
        own_cluster,
        at.cluster(x + 1),
        at.cluster(x - 1),
        from_north(own_cluster, rim_row),
        from_south(own_cluster, rim_row),
    )
    clusters = [jnp.broadcast_to(c, (8, lanes)) for c in clusters]
    groups = []
    for r in range(pad // 8):
        wy, own = at.wy(x, r), at.c(x, r)
        south_wy = from_south(wy, halo_of(rim.wy(r), x))
        center, east, west, north, south = rates_of(at.wx(x, r), at.wx(x - 1, r), wy, south_wy)
        halo = halo_of(rim.c(r), x)
        terms = (
            center * own,
            east * at.c(x + 1, r),
            west * at.c(x - 1, r),
            north * from_north(own, halo),
            south * from_south(own, halo),
        )
        groups.append(parted(terms, clusters, ids))
    fields = [jnp.concatenate([group[a] for group in groups], axis=0) for a in range(len(ids))]
    return convect(lhs, fields, at.strength(x))


class Columns:
    def __init__(self, dims, c_ref, wx_ref, wy_ref, cluster_ref, strength_ref, before_ref=None, after_ref=None):
        self.lev, self.width_x, self.lanes = dims
        self.c_ref, self.wx_ref, self.wy_ref = c_ref, wx_ref, wy_ref
        self.cluster_rows = cluster_ref[...].astype(F32)
        self.strength_ref = strength_ref
        self.before_ref, self.after_ref = before_ref, after_ref

    def sent(self, ref, tile, r):
        first = tile * self.lev + 8 * r
        return ref[first : first + 8, :]

    def strided(self, ref, x, r):
        return ref[pl.ds(8 * r * self.width_x + x, 8, stride=self.width_x), :]

    def c(self, x, r):
        if x < 0:
            return self.sent(self.before_ref, -1 - x, r)
        if x >= self.width_x:
            return self.sent(self.after_ref, x - self.width_x, r)
        return self.c_ref[x, 8 * r : 8 * r + 8, :]

    def wx(self, x, r):
        if x < 0:
            return self.sent(self.before_ref, 2 if x == -1 else 4, r)
        return self.sent(self.after_ref, 2, r) if x >= self.width_x else self.strided(self.wx_ref, x, r)

    def wy(self, x, r):
        if x < 0:
            return self.sent(self.before_ref, 3, r)
        return self.sent(self.after_ref, 3, r) if x >= self.width_x else self.strided(self.wy_ref, x, r)

    def misc(self, ref, tiles, row):
        return ref[tiles * self.lev + row : tiles * self.lev + row + 1, :]

    def cluster(self, x):
        if x < 0:
            return self.misc(self.before_ref, 5, -1 - x)
        if x >= self.width_x:
            return self.misc(self.after_ref, 4, x - self.width_x)
        return self.cluster_rows[x : x + 1]

    def strength(self, x):
        if x < 0:
            return self.misc(self.before_ref, 5, 2)
        if x >= self.width_x:
            return self.misc(self.after_ref, 4, 2)
        return self.strength_ref[x : x + 1, :]


class Rim:
    def __init__(self, c, wy, cluster):
        self.c_tile, self.wy_tile, self.cluster = crossed(c), crossed(wy), crossed(cluster)

    def c(self, r):
        return self.c_tile[8 * r : 8 * r + 8]

    def wy(self, r):
        return self.wy_tile[8 * r : 8 * r + 8]


def adjoint_ids(per_device):
    first = (lax.axis_index("adj") * per_device).astype(F32)
    return [first + a for a in range(per_device)]


def inner_kernel(
    dims, per_device, rim_ref, c_ref, wx_ref, wy_ref, cluster_ref, strength_ref, lhs_ref, mixed_ref, ground_ref
):
    lev, width_x, lanes = dims
    pad = round_up(lev, 8)
    at = Columns(dims, c_ref, wx_ref, wy_ref, cluster_ref, strength_ref)
    base = RIM_TILES * pad
    rim = Rim(rim_ref[pad : 2 * pad, :], rim_ref[3 * pad : 4 * pad, :], rim_ref[base + 1 : base + 2, :])
    ids = adjoint_ids(per_device)
    lhs = lhs_ref[...]
    for x in range(1, width_x - 1):
        for a, value in enumerate(advance(dims, ids, lhs, x, at, rim)):
            mixed_ref[a, x - 1, :, :] = value
            ground_ref[a, x + 1 : x + 2, :] = value[0:1]


def mixed_at(dims, inner_ref, ends_ref, a, x, r):
    width_x = dims[1]
    rows = slice(8 * r, 8 * r + 8)
    if 1 <= x < width_x - 1:
        return inner_ref[a, x - 1, rows, :]
    return ends_ref[a, x + 1 if x < 1 else x - width_x + 3, rows, :]


def second_transport(dims, at, rim_wy, far, inner_ref, ends_ref, ids, x, r):
    half = 4 * dims[1]
    wy = at.wy(x, r)
    south_wy = from_south(wy, halo_of(rim_wy, x))
    center, east, west, north, south = rates_of(at.wx(x, r), at.wx(x - 1, r), wy, south_wy)
    values = []
    for a in range(len(ids)):
        own = mixed_at(dims, inner_ref, ends_ref, a, x, r)
        halo = turn(far(a // 2, r), -4 * x - 2 - half * (a % 2))
        parts = [
            center * own,
            east * mixed_at(dims, inner_ref, ends_ref, a, x + 1, r),
            west * mixed_at(dims, inner_ref, ends_ref, a, x - 1, r),
            north * from_north(own, halo),
            south * from_south(own, halo),
        ]
        values.append(total(parts))
    return values


def ends_kernel(dims, subs, per_device, *refs):
    lev, width_x, lanes = dims
    rim_ref, before_ref, after_ref, inner_ground_ref, c_ref, wx_ref, wy_ref, cluster_ref, strength_ref, lhs_ref = refs[:10]
    ends_ref, far_ref, surface_ref, full_ref, ground_ref, west_ref, beside_ref = refs[10:]
    pad = round_up(lev, 8)
    half = 4 * width_x
    cross = lax.axis_index("sub")
    lane = lane_of((1, lanes))
    place = lane % 4
    after_slot = lane // 4 == width_x
    before_slot = lane >= lanes - 4
    at = Columns(dims, c_ref, wx_ref, wy_ref, cluster_ref, strength_ref, before_ref, after_ref)
    ids = adjoint_ids(per_device)
    lhs = lhs_ref[...]

    base = RIM_TILES * pad
    rim_c, far_c, rim_wy, far_wy, far_wx, rim_wx = (rim_ref[i * pad : (i + 1) * pad, :] for i in range(RIM_TILES))
    rim_cluster = rim_ref[base : base + 1, :]
    far_cluster = rim_ref[base + 1 : base + 2, :]
    far_strength = rim_ref[base + 2 : base + 3, :]
    rim = Rim(far_c, far_wy, far_cluster)

    def sent(ref, tile):
        return jnp.concatenate([at.sent(ref, tile, r) for r in range(pad // 8)], axis=0)

    def full(value, before, after):
        return jnp.where(before_slot, turn(before, -2), jnp.where(after_slot, turn(after, half + 2), value))

    full_c = full(rim_c, sent(before_ref, 0), sent(after_ref, 0))
    full_wy = full(rim_wy, sent(before_ref, 3), sent(after_ref, 3))
    full_wx = full(rim_wx, sent(before_ref, 2), rim_wx)
    for i, value in enumerate((full_c, full_wy, full_wx)):
        full_ref[i * pad : (i + 1) * pad, :] = value
    rows = [
        full(rim_cluster, at.cluster(-1), at.cluster(width_x)),
        full(rim_ref[base + 3 : base + 4, :], at.strength(-1), at.strength(width_x)),
    ]
    full_ref[3 * pad : 3 * pad + 2, :] = jnp.concatenate(rows, axis=0)
    full_ref[3 * pad + 2 : 3 * pad + 8, :] = jnp.zeros((6, lanes), F32)
    picked = jnp.where(before_slot | after_slot, full_c, 0.0)
    wy_slot = (lane < 4) | (lane // 4 == width_x + 1)
    wx_slot = lane // 4 == 1
    moved_wy = full(jnp.zeros_like(rim_wy), turn(sent(before_ref, 3), 0), turn(sent(after_ref, 3), 0))
    picked = jnp.where(wy_slot, turn(moved_wy, 4), picked)
    picked = jnp.where(wx_slot, turn(sent(before_ref, 2), 6), picked).T
    picked = jnp.concatenate([picked, jnp.zeros((lanes, lanes - pad), F32)], axis=1)
    packet = picked[half : half + 8] + turn(picked[lanes - 8 : lanes], pad) + turn(picked[0:8], 2 * pad)
    tail = per_device * width_x
    surface_ref[tail : tail + 8, :] = packet
    surface_ref[tail + 8 : tail + 10, :] = jnp.concatenate(rows, axis=0)
    surface_ref[tail + 10 : tail + 16, :] = jnp.zeros((6, lanes), F32)
    for k, x in ((1, 0), (2, width_x - 1), (0, -1), (3, width_x)):
        for a, value in enumerate(advance(dims, ids, lhs, x, at, rim)):
            ends_ref[a, k, :, :] = value
            ground_ref[a, x + 1 : x + 2, :] = value[0:1]

    def rim_north(far, own):
        return turn(jnp.where(place == 2, own, far), -1)

    def rim_south(far, own):
        return turn(jnp.where(place == 1, own, far), 1)

    center, east, west, north, south = rates_of(far_wx, turn(far_wx, 4), far_wy, rim_south(far_wy, rim_wy))
    terms = (
        center * far_c,
        east * turn(far_c, -4),
        west * turn(far_c, 4),
        north * rim_north(far_c, rim_c),
        south * rim_south(far_c, rim_c),
    )
    clusters = (
        far_cluster,
        turn(far_cluster, -4),
        turn(far_cluster, 4),
        rim_north(far_cluster, rim_cluster),
        rim_south(far_cluster, rim_cluster),
    )
    inside = jnp.where(lane < half, jnp.where(place < 2, cross, subs - 1 - cross), 0) > 0
    fields = [jnp.where(inside, f, 0.0) for f in parted(terms, clusters, ids)]
    joined = [fields[a] + turn(fields[a + 1], half) for a in range(0, per_device, 2)]
    far_mixed = [crossed(f) for f in convect(lhs, joined, far_strength + turn(far_strength, half))]
    for at_pair, value in enumerate(far_mixed):
        far_ref[at_pair, 0:pad, :] = value
    far_ref[0, pad : pad + 8, :] = jnp.zeros((8, lanes), F32)
    for pair in range(1, len(far_mixed)):
        far_ref[pair, pad : pad + 8, :] = jnp.zeros((8, lanes), F32)

    rows = [rim.wy_tile[0:1]] + [turn(far_mixed[a // 2][0:1], half * (a % 2)) for a in range(per_device)]
    tall = round_up(len(rows), 8)
    stack = jnp.concatenate(rows + [jnp.zeros((tall - len(rows), lanes), F32)], axis=0)
    for x in range(width_x):
        beside_ref[x * tall : (x + 1) * tall, :] = halo_of(stack, x)

    def beside(at_row):
        return beside_ref[pl.ds(at_row, width_x, stride=tall), :]

    west_ref[0:1, :] = at.sent(before_ref, 2, 0)[0:1]
    west_ref[1 : width_x + 1, :] = wx_ref[0:width_x, :]
    wx, wy = wx_ref[0:width_x, :], wy_ref[0:width_x, :]
    south_wy = from_south(wy, beside(0))
    center, east, west, north, south = rates_of(wx, west_ref[0:width_x, :], wy, south_wy)
    for a in range(per_device):
        ground_ref[a, 2:width_x, :] = inner_ground_ref[a, 2:width_x, :]
        own = ground_ref[a, 1 : width_x + 1, :]
        rim_rows = beside(1 + a)
        parts = [
            center * own,
            east * ground_ref[a, 2 : width_x + 2, :],
            west * ground_ref[a, 0:width_x, :],
            north * from_north(own, rim_rows),
            south * from_south(own, rim_rows),
        ]
        surface_ref[a * width_x : (a + 1) * width_x, :] = total(parts)


def output_kernel(dims, per_device, *refs):
    lev, width_x, lanes = dims
    rim_ref, before_ref, inner_ref, ends_ref, far_ref, wx_ref, wy_ref, cluster_ref, strength_ref = refs[:9]
    out_ref, token_ref, edge_ref, field_ref, sem = refs[9:]
    token_ref[...] = jnp.zeros(token_ref.shape, F32)
    pad = round_up(lev, 8)
    at = Columns(dims, None, wx_ref, wy_ref, cluster_ref, strength_ref, before_ref)
    ids = range(per_device)

    def far(pair, r):
        return far_ref[pair, 8 * r : 8 * r + 8, :]

    rim_wys = [crossed(rim_ref[3 * pad + 8 * r : 3 * pad + 8 * r + 8, :]) for r in range(pad // 8)]
    copies = []
    for x in range(width_x):
        for r in range(pad // 8):
            rim_wy = rim_wys[r]
            values = second_transport(dims, at, rim_wy, far, inner_ref, ends_ref, ids, x, r)
            for a, value in enumerate(values):
                if x in (0, width_x - 1):
                    edge_ref[a, min(x, 1), 8 * r : 8 * r + 8, :] = value
                else:
                    field_ref[a, x, 8 * r : 8 * r + 8, :] = value
        for a in range(per_device if 0 < x < width_x - 1 else 0):
            source = field_ref.at[a, x, pl.ds(0, lev), :]
            copies.append(pltpu.make_async_copy(source, out_ref.at[a, :, x, 0, :], sem.at[len(copies)]))
            copies[-1].start()
    for copy in copies:
        copy.wait()


def quotient(value, count):
    if count & (count - 1) == 0:
        return value >> (count.bit_length() - 1), value & (count - 1)
    return lax.div(value, count), lax.rem(value, count)


def tables_kernel(dims, tiles, subs, n_rim, cell_ref, weight_ref, hot_ref, share_ref):
    _, width_x, width_y = dims
    slots, elements = cell_ref.shape
    tile_pos = lax.axis_index("tiles")
    cross = lax.axis_index("sub")
    column_x, row_y = quotient(cell_ref[...], width_y * subs)
    block_x, inner_x = quotient(column_x, width_x)
    block_y, lane_y = quotient(row_y, width_y)
    step = block_x - tile_pos
    step = jnp.where(step < -1, step + tiles, jnp.where(step > 1, step - tiles, step))
    if n_rim == 2:
        side = jnp.where(block_y == cross, 0, 1)
    else:
        side = block_y - cross + 1
    at_y = side * width_y + lane_y
    at_x = (step + 1) * width_x + inner_x
    weight = weight_ref[...]
    group = width_y
    rows = lax.broadcasted_iota(jnp.int32, (16, group), 0)
    for g in range(0, elements, group):
        lanes = slice(g, g + group)
        for k in range(slots):
            y = jnp.broadcast_to(at_y[k : k + 1, lanes], (16, group)) - rows
            for first in range(0, n_rim * width_y, 16):
                hot_ref[k, first : first + 16, lanes] = jnp.where(y == first, 1.0, 0.0).astype(BF16)
            x = jnp.broadcast_to(at_x[k : k + 1, lanes], (16, group)) - rows
            w = jnp.broadcast_to(weight[k : k + 1, lanes], (16, group))
            for first in range(0, 3 * width_x, 16):
                share_ref[k, first : first + 16, lanes] = jnp.where(x == first, w, 0.0)


def looked_up(dims, per_device, n_rim, blocks, hot_ref, share_ref, lanes):
    width_x = dims[1]
    rows = per_device * width_x
    surfaces = [split(jnp.concatenate(places, axis=1)) for _, places in blocks]
    lhs = jnp.concatenate([part for pair in surfaces for part in pair], axis=0)
    sums = [None] * per_device
    for k in range(hot_ref.shape[0]):
        found = jnp.dot(lhs, hot_ref[k, :, lanes], preferred_element_type=F32)
        for at, (step, _) in enumerate(blocks):
            share = share_ref[k, (step + 1) * width_x : (step + 2) * width_x, lanes]
            for a in range(per_device):
                high = 2 * at * rows + a * width_x
                low = high + rows
                value = (found[high : high + width_x] + found[low : low + width_x]) * share
                sums[a] = value if sums[a] is None else sums[a] + value
    return jnp.concatenate([jnp.sum(s, axis=0, keepdims=True) for s in sums], axis=0)


def wide_lanes(elements):
    wide = 256 if elements % 256 == 0 else 128
    return [slice(g, g + wide) for g in range(0, elements, wide)]


def sense_here_kernel(dims, per_device, n_rim, hot_ref, share_ref, here_ref, out_ref):
    rows = per_device * dims[1]
    blocks = [(0, [here_ref[k * rows : (k + 1) * rows, :] for k in range(n_rim)])]
    for lanes in wide_lanes(out_ref.shape[1]):
        out_ref[:, lanes] = looked_up(dims, per_device, n_rim, blocks, hot_ref, share_ref, lanes)


def sense_kernel(dims, per_device, n_rim, hot_ref, share_ref, partial_ref, before_ref, after_ref, out_ref, own_ref, sem):
    rows = per_device * dims[1]
    blocks = [
        (step, [ref[k * rows : (k + 1) * rows, :] for k in range(n_rim)])
        for step, ref in ((-1, before_ref), (1, after_ref))
    ]
    for lanes in wide_lanes(own_ref.shape[1]):
        value = looked_up(dims, per_device, n_rim, blocks, hot_ref, share_ref, lanes)
        own_ref[:, lanes] = partial_ref[:, lanes] + value
    copy = pltpu.make_async_copy(own_ref, out_ref, sem)
    copy.start()
    copy.wait()


class Seam:
    def __init__(self, dims, c, wy, wx, cluster, strength):
        _, self.width_x, lanes = dims
        self.lane = lane_of((1, lanes))
        self.place = self.lane % 4
        slot = self.lane // 4
        self.first, self.last = slot == 0, slot == self.width_x - 1
        self.beside = (slot == lanes // 4 - 1) | (slot == self.width_x)
        self.c, self.cluster, self.strength = c, cluster, strength
        self.east = jnp.maximum(wx, 0.0)
        self.west = jnp.maximum(-turn(wx, 4), 0.0)
        self.north = jnp.maximum(wy, 0.0)
        self.south = jnp.maximum(-turn(wy, 1), 0.0)

    def missing(self, lhs, ids):
        near = (self.place == 1) | (self.place == 2)
        wanted_slots = near & (self.beside | self.first | self.last)
        moved = [(turn(self.c, k), turn(self.cluster, k)) for k in (-1, 1, 4, -4)]
        fields = []
        for wanted in ids:
            own = jnp.where(self.cluster == wanted, self.c, 0.0)
            from_n, from_s, from_w, from_e = (jnp.where(row == wanted, c, 0.0) for c, row in moved)
            upright = jnp.where(self.place == 1, self.north * from_n, self.south * (from_s - own))
            level = jnp.where(self.first, self.west * (from_w - own), self.east * from_e)
            fields.append(jnp.where(wanted_slots, jnp.where(self.beside, upright, level), 0.0))
        return convect(lhs, fields, self.strength)


def seam_transport(dims, rates, missing):
    width_x = dims[1]
    east, west, north, south = rates
    lane = lane_of((1, missing.shape[1]))
    place, slot = lane % 4, lane // 4
    level = jnp.where(slot == 0, west * turn(missing, 4), east * turn(missing, -4))
    return level + jnp.where(place == 1, north * turn(missing, -1), south * turn(missing, 1))


def own_places(subs):
    cross = lax.axis_index("sub")
    if subs == 2:
        own_south = (cross == 0).astype(jnp.int32)
        return [own_south]
    return [jnp.int32(0), jnp.int32(1)]


def patch_kernel(dims, subs, per_device, n_rim, *refs):
    lev, width_x, lanes = dims
    rim_ref, full_ref, own_ref, south_ref, north_ref, lhs_ref, _, whole_ref, seam_ref = refs
    pad = round_up(lev, 8)
    half = 4 * width_x
    rows = per_device * width_x
    lane = lane_of((1, lanes))
    southern = lane % 4 < 2
    before_slot = lane >= lanes - 4
    after_slot = lane // 4 == width_x
    ids = adjoint_ids(per_device)
    lhs = lhs_ref[...]
    cross = lax.axis_index("sub")
    present = jnp.where(southern, cross, subs - 1 - cross) > 0

    def upright(ref):
        turned = ref[rows : rows + 8, :].T
        turned = jnp.concatenate([turned, jnp.zeros((lanes, lanes - 8), F32)], axis=1)
        return [turned[i * pad : (i + 1) * pad] for i in range(3)]

    def beyond(value, south, north, before, after):
        def placed(tile):
            moved = turn(tile[0], lanes - 4 - before)
            return moved if after is None else jnp.where(after_slot, turn(tile[1], half - after), moved)

        moved = placed(south) if south is north else jnp.where(southern, placed(south), placed(north))
        moved = jnp.where(present, moved, 0.0)
        slots = before_slot if after is None else before_slot | after_slot
        return jnp.where(slots, moved, value)

    south = upright(south_ref)
    north = south if subs == 2 else upright(north_ref)

    def pair(first, second):
        one = (south[first], south[second])
        return one, one if subs == 2 else (north[first], north[second])

    far_c, far_wy, far_wx = (rim_ref[i * pad : (i + 1) * pad, :] for i in (1, 3, 4))
    c_pair, wy_pair = pair(1, 0), pair(2, 0)
    if subs == 2:
        c_pair, wy_pair = (c_pair[0], c_pair[0]), (wy_pair[0], wy_pair[0])
    far_c = beyond(far_c, *c_pair, 4, 0)
    far_wx = beyond(far_wx, *wy_pair, 4, None)
    far_wy = beyond(far_wy, *wy_pair, 0, 4)
    base = RIM_TILES * pad

    def beyond_row(value, at_row):
        south_row = south_ref[rows + at_row : rows + at_row + 1, :]
        north_row = north_ref[rows + at_row : rows + at_row + 1, :]
        moved = jnp.where(present, jnp.where(southern, south_row, north_row), 0.0)
        return jnp.where(before_slot | after_slot, moved, value)

    far_cluster = beyond_row(rim_ref[base + 1 : base + 2, :], 8)
    far_strength = beyond_row(rim_ref[base + 2 : base + 3, :], 9)
    full_c, full_wy, full_wx = (full_ref[i * pad : (i + 1) * pad, :] for i in range(3))
    full_cluster = full_ref[3 * pad : 3 * pad + 1, :]
    full_strength = full_ref[3 * pad + 1 : 3 * pad + 2, :]
    surfaces = [own_ref, south_ref] if subs == 2 else [south_ref, own_ref, north_ref]
    for k, ref in enumerate(surfaces):
        whole_ref[k * rows : (k + 1) * rows, :] = ref[0:rows, :]
    for k, own_south in enumerate(own_places(subs)):
        mine = jnp.where(southern, own_south, 1 - own_south) > 0
        seam = Seam(
            dims,
            jnp.where(mine, full_c, far_c),
            jnp.where(mine, full_wy, far_wy),
            jnp.where(mine, full_wx, far_wx),
            jnp.where(mine, full_cluster, far_cluster),
            jnp.where(mine, full_strength, far_strength),
        )
        missing = seam.missing(lhs, ids)
        rates = (seam.east, seam.west, seam.north, seam.south)
        for i, value in enumerate(rates + tuple(missing)):
            seam_ref[k, i * pad : (i + 1) * pad, :] = value
        far_at = 1 if subs == 2 else 2 * k
        own_at = 0 if subs == 2 else 1
        own_lane = jnp.where(own_south > 0, lanes - 1, 0)
        for a, value in enumerate(missing):
            change = seam_transport(dims, [rate[0:8] for rate in rates], value[0:8])[0:1]
            for x in (0, width_x - 1):
                row = turn(change, -4 * x - 2)
                for block, at_lane in ((own_at, own_lane), (far_at, lanes - 1 - own_lane)):
                    at = block * rows + a * width_x + x
                    whole_ref[at : at + 1, :] = whole_ref[at : at + 1, :] + jnp.where(lane == at_lane, row, 0.0)


def output_ends_kernel(dims, subs, per_device, _, seam_ref, edge_ref, out_ref, done_ref, sem):
    lev, width_x, lanes = dims
    pad = round_up(lev, 8)
    lane = lane_of((1, lanes))
    copies = []
    for a in range(per_device):
        columns = [edge_ref[a, 0], edge_ref[a, 1]]
        for k, own_south in enumerate(own_places(subs)):
            rates = [seam_ref[k, i * pad : (i + 1) * pad, :] for i in range(4)]
            change = seam_transport(dims, rates, seam_ref[k, (4 + a) * pad : (5 + a) * pad, :])
            own = lane == jnp.where(own_south > 0, lanes - 1, 0)
            for i, x in enumerate((0, width_x - 1)):
                columns[i] = columns[i] + jnp.where(own, turn(change, -4 * x - 2), 0.0)
        for i, x in enumerate((0, width_x - 1)):
            done_ref[a, i, :, :] = columns[i]
            source = done_ref.at[a, i, pl.ds(0, lev), :]
            copies.append(pltpu.make_async_copy(source, out_ref.at[a, :, x, 0, :], sem.at[len(copies)]))
            copies[-1].start()
    for copy in copies:
        copy.wait()


def ring(value, axis, steps):
    count = lax.axis_size(axis)
    return lax.ppermute(value, axis, [(i, (i + steps) % count) for i in range(count)])


def across(value):
    count = lax.axis_size("sub")
    if count == 2:
        other = ring(value, "sub", 1)
        return other, other
    from_south = lax.ppermute(value, "sub", [(i, i + 1) for i in range(count - 1)])
    from_north = lax.ppermute(value, "sub", [(i + 1, i) for i in range(count - 1)])
    return from_south, from_north


def body(
    innovation,
    cluster,
    kernel,
    wind_x,
    wind_y,
    conv_strength,
    conv_matrix,
    margin_cell,
    margin_weight,
):
    dims = kernel.shape
    lev, width_x, width_y = dims
    tiles = lax.axis_size("tiles")
    subs = lax.axis_size("sub")
    per_device = ADJ // lax.axis_size("adj")
    pad = round_up(lev, 8)
    deep = round_up(lev, 16)
    flat = (lev * width_x, width_y)
    tall = (pad * width_x, width_y)
    small = innovation.shape
    sources = (
        kernel.reshape(flat),
        wind_x.reshape(flat),
        wind_y.reshape(flat),
        innovation,
        cluster,
        conv_strength,
        conv_matrix,
        margin_cell.T,
        margin_weight.T,
    )
    outs = [tall, tall, tall, small, (small, jnp.int32), small, conv_matrix.shape]
    outs += [(sources[7].shape, jnp.int32), sources[8].shape, ((pad, 3 * deep), BF16), (2 * pad + 8, width_y)]
    fetched = call(
        functools.partial(fetch_kernel, dims),
        outs,
        sources,
        scratch=(pltpu.SemaphoreType.DMA((len(sources),)),),
        far_in=True,
        name="fetch",
    )
    air, wx, wy, innov, group, strength, _, cell, weight, lhs, own_rim = fetched
    south_rim, north_rim = across(own_rim)
    first, to_east, to_west = call(
        functools.partial(first_mix_kernel, dims),
        [(width_x, pad, width_y), (5 * lev + 4, width_y), (4 * lev + 4, width_y)],
        (air, innov, strength, lhs, wx, wy, group),
        name="first_mix",
        cost=400000,
    )
    before = ring(to_east, "tiles", 1)
    after = ring(to_west, "tiles", -1)
    (rim,) = call(
        functools.partial(rim_kernel, dims, subs),
        [(RIM_TILES * pad + 8, width_y)],
        (own_rim, south_rim, north_rim, lhs),
        name="rim",
        cost=400000,
    )
    inner, ground = call(
        functools.partial(inner_kernel, dims, per_device),
        [(per_device, width_x - 2, pad, width_y), (per_device, width_x + 8, width_y)],
        (rim, first, wx, wy, group, strength, lhs),
        name="inner",
        cost=4000000,
    )
    ends, far, surface, full = call(
        functools.partial(ends_kernel, dims, subs, per_device),
        [
            (per_device, 4, pad, width_y),
            ((per_device + 1) // 2, pad + 8, width_y),
            (per_device * width_x + 16, width_y),
            (3 * pad + 8, width_y),
        ],
        (rim, before, after, ground, first, wx, wy, group, strength, lhs),
        scratch=(
            pltpu.VMEM((per_device, width_x + 8, width_y), F32),
            pltpu.VMEM((width_x + 8, width_y), F32),
            pltpu.VMEM((width_x * round_up(per_device + 1, 8), width_y), F32),
        ),
        name="ends",
    )
    south_surface, north_surface = across(surface)
    field, token, edge = call(
        functools.partial(output_kernel, dims, per_device),
        [(per_device, lev, width_x, 1, width_y), (8, width_y), (per_device, 2, pad, width_y)],
        (rim, before, inner, ends, far, wx, wy, group, strength),
        scratch=(
            pltpu.VMEM((per_device, width_x, pad, width_y), F32),
            pltpu.SemaphoreType.DMA((per_device * width_x,)),
        ),
        far_out=(0,),
        name="output",
        cost=4000000,
    )
    n_rim = min(subs, 3)
    rows = per_device * width_x
    seams = 1 if subs == 2 else 2
    whole, seam = call(
        functools.partial(patch_kernel, dims, subs, per_device, n_rim),
        [(n_rim * rows, width_y), (seams, (4 + per_device) * pad, width_y)],
        (rim, full, surface, south_surface, north_surface, lhs, token),
        name="patch",
    )
    surface_before = ring(whole, "tiles", 1)
    surface_after = ring(whole, "tiles", -1)
    near, hbm = pl.BlockSpec(memory_space=pltpu.VMEM), pl.BlockSpec(memory_space=pl.ANY)
    field = pl.pallas_call(
        functools.partial(output_ends_kernel, dims, subs, per_device),
        out_shape=jax.ShapeDtypeStruct(field.shape, F32),
        in_specs=[hbm, near, near],
        out_specs=hbm,
        scratch_shapes=[pltpu.VMEM((per_device, 2, pad, width_y), F32), pltpu.SemaphoreType.DMA((2 * per_device,))],
        input_output_aliases={0: 0},
        compiler_params=pltpu.CompilerParams(vmem_limit_bytes=VMEM_BYTES),
        cost_estimate=pl.CostEstimate(flops=1000000, bytes_accessed=1000000, transcendentals=0),
        name="output_ends",
    )(field, *[pltpu.with_memory_space_constraint(v, pltpu.VMEM) for v in (seam, edge)])
    slots, elements = cell.shape
    hot, share = call(
        functools.partial(tables_kernel, dims, tiles, subs, n_rim),
        [((slots, n_rim * width_y, elements), BF16), (slots, 3 * width_x, elements)],
        (cell, weight),
        name="tables",
        cost=2000000,
    )
    (partial,) = call(
        functools.partial(sense_here_kernel, dims, per_device, n_rim),
        [(per_device, elements)],
        (hot, share, whole),
        name="sense_here",
        cost=2000000,
    )
    (sensed,) = call(
        functools.partial(sense_kernel, dims, per_device, n_rim),
        [(per_device, elements)],
        (hot, share, partial, surface_before, surface_after),
        scratch=(pltpu.VMEM((per_device, elements), F32), pltpu.SemaphoreType.DMA),
        far_out=(0,),
        name="sense",
    )
    return (field.reshape(per_device, lev, width_x, width_y), sensed)


def solution(mesh):
    in_specs = (
        P(("groups", "tiles"), "sub"),
        P(("groups", "tiles"), "sub"),
        P(None, "tiles", "sub"),
        P(None, "tiles", "sub"),
        P(None, "tiles", "sub"),
        P("tiles", "sub"),
        P(),
        P(("tiles", "sub"), None),
        P(("tiles", "sub"), None),
    )
    out_specs = (P(("groups", "adj"), None, "tiles", "sub"), P(("groups", "adj"), ("tiles", "sub")))
    return jax.shard_map(body, mesh=mesh, in_specs=in_specs, out_specs=out_specs, check_vma=False)
```

```python
import functools

import jax
import jax.numpy as jnp
from jax import lax
from jax.experimental import pallas as pl
from jax.experimental.pallas import tpu as pltpu
from jax.sharding import PartitionSpec as P


ADJ = 8
F32 = jnp.float32
BF16 = jnp.bfloat16
VMEM_BYTES = 16 << 20
RIM_TILES = 6


def call(kernel, outs, args, scratch=(), far_in=False, far_out=(), cost=0):
    near = pl.BlockSpec(memory_space=pltpu.VMEM)
    far = pl.BlockSpec(memory_space=pl.ANY)
    outs = [out for out in outs]
    shapes = [(out, F32) if isinstance(out[-1], int) else out for out in outs]
    return pl.pallas_call(
        kernel,
        out_shape=[(jax.ShapeDtypeStruct if at in far_out else pltpu.VMEM)(*out) for at, out in enumerate(shapes)],
        in_specs=[far if far_in else near] * len(args),
        out_specs=[far if at in far_out else near for at in range(len(outs))],
        scratch_shapes=list(scratch),
        compiler_params=pltpu.CompilerParams(vmem_limit_bytes=VMEM_BYTES),
        cost_estimate=pl.CostEstimate(flops=cost, bytes_accessed=cost, transcendentals=0) if cost else None,
    )(*[pltpu.with_memory_space_constraint(arg, pltpu.HBM if far_in else pltpu.VMEM) for arg in args])


def round_up(count, unit):
    return count + -count % unit


def split(value):
    high = value.astype(BF16)
    return high, (value - high.astype(F32)).astype(BF16)


def mix(lhs, field):
    short = lhs.shape[1] // 3 - field.shape[0]
    if short:
        field = jnp.concatenate([field, jnp.zeros((short, field.shape[1]), F32)], axis=0)
    high, low = split(field)
    return jnp.dot(lhs, jnp.concatenate([high, high, low], axis=0), preferred_element_type=F32)


def lane_of(shape):
    return lax.broadcasted_iota(jnp.int32, shape, len(shape) - 1)


def turn(value, steps):
    steps = steps % value.shape[-1]
    return value if steps == 0 else pltpu.roll(value, steps, value.ndim - 1)


def total(parts):
    while len(parts) > 1:
        parts = [parts[i] + parts[i + 1] if i + 1 < len(parts) else parts[i] for i in range(0, len(parts), 2)]
    return parts[0]


def fetch_kernel(dims, *refs):
    lev, width_x, lanes = dims
    sources, (kernel, wx, wy, innov, cluster, strength, matrix, cell, weight, lhs, rim), scratch = (
        refs[:9],
        refs[9:20],
        refs[20:],
    )
    (sem,) = scratch
    pad = round_up(lev, 8)
    deep = lhs.shape[1] // 3
    half = 4 * width_x
    whole = lev * width_x
    copies = [pltpu.make_async_copy(s, t, sem.at[i]) for i, (s, t) in enumerate(zip(sources[3:], refs[12:18]))]
    targets = [ref.at[pl.ds(0, whole), :] for ref in (kernel, wx, wy)]
    large = [pltpu.make_async_copy(s, t, sem.at[6 + i]) for i, (s, t) in enumerate(zip(sources, targets))]
    for copy in copies[:4] + large + copies[4:]:
        copy.start()
    for ref in (kernel, wx, wy):
        ref[pl.ds(whole, (pad - lev) * width_x), :] = jnp.zeros(((pad - lev) * width_x, lanes), F32)
    slot = lane_of((1, lanes)) // 4

    def packed(ref, first, r):
        value = jnp.zeros((8, lanes), F32)
        for x in range(width_x):
            moved = turn(ref[pl.ds(8 * r * width_x + x, 8, stride=width_x), :], first + 4 * x + 2)
            value = jnp.where(slot == first // 4 + x, moved, value)
        return value

    def packed_row(value):
        moved = pltpu.roll(value, 2, 1, stride=4, stride_axis=0)
        own = lax.broadcasted_iota(jnp.int32, value.shape, 0) == slot
        return jnp.sum(jnp.where(own, moved, 0.0), axis=0, keepdims=True)

    for copy in copies[:4]:
        copy.wait()
    rim[2 * pad : 2 * pad + 1, :] = packed_row(innov[...])
    rim[2 * pad + 1 : 2 * pad + 2, :] = packed_row(cluster[...].astype(F32))
    rim[2 * pad + 2 : 2 * pad + 3, :] = packed_row(strength[...])
    rim[2 * pad + 3 : 2 * pad + 8, :] = jnp.zeros((5, lanes), F32)
    turned = matrix[...].T
    turned = jnp.concatenate([turned, jnp.zeros((pad - lev, lev), F32)], axis=0)
    turned = jnp.concatenate([turned, jnp.zeros((pad, deep - lev), F32)], axis=1)
    high = turned.astype(BF16).astype(F32)
    lhs[...] = jnp.concatenate([high, turned - high, high], axis=1).astype(BF16)
    groups = [slice(8 * r, 8 * r + 8) for r in range(pad // 8)]
    large[0].wait()
    lower = [packed(kernel, 0, r) for r in range(pad // 8)]
    large[2].wait()
    for r, rows in enumerate(groups):
        rim[rows, :] = jnp.where(slot * 4 >= half, packed(wy, half, r), lower[r])
    large[1].wait()
    for r in range(pad // 8):
        rim[pad + 8 * r : pad + 8 * r + 8, :] = packed(wx, 0, r)
    for copy in copies[4:]:
        copy.wait()


def first_mix_kernel(dims, *refs):
    lev, width_x, lanes = dims
    kernel_ref, innov_ref, strength_ref, lhs_ref, wx_ref, wy_ref, cluster_ref, out_ref, east_ref, west_ref = refs
    pad = round_up(lev, 8)
    lhs = lhs_ref[...]
    last = width_x - 1
    cluster = cluster_ref[...].astype(F32)
    held = {}
    order = [0, width_x - 2] + list(range(2, width_x - 2, 2))

    def column(ref, x):
        return ref[pl.ds(x, pad, stride=width_x), :]

    def put(ref, tiles, near, next_one):
        for at, value in enumerate(tiles):
            top = min(pad, ref.shape[0] - at * lev)
            ref[at * lev : at * lev + top, :] = value[:top]
        base = len(tiles) * lev
        ref[base : base + 1, :] = cluster[near : near + 1]
        ref[base + 1 : base + 2, :] = cluster[next_one : next_one + 1]
        ref[base + 2 : base + 3, :] = strength_ref[near : near + 1, :]
        ref[base + 3 : base + 4, :] = jnp.zeros((1, lanes), F32)

    for x in order:
        tiles = [column(kernel_ref, at) * innov_ref[at : at + 1, :] for at in (x, x + 1)]
        mixed = mix(lhs, jnp.concatenate(tiles, axis=1))
        for k, tile in enumerate(tiles):
            part = mixed[:, k * lanes : (k + 1) * lanes]
            held[x + k] = tile + strength_ref[x + k : x + k + 1, :] * (part - tile)
            out_ref[x + k, :, :] = held[x + k]
        if x == width_x - 2:
            ends = (held[last], held[last - 1], column(wx_ref, last), column(wy_ref, last), column(wx_ref, last - 1))
            put(east_ref, ends, last, last - 1)
            put(west_ref, (held[0], held[1], column(wx_ref, 0), column(wy_ref, 0)), 0, 1)


def rim_kernel(dims, subs, own_ref, south_ref, north_ref, lhs_ref, rim_ref):
    lev, width_x, lanes = dims
    pad = round_up(lev, 8)
    half = 4 * width_x
    cross = lax.axis_index("sub")
    lane = lane_of((1, lanes))
    lower = lane < half
    southern = lane % 4 < 2
    present = jnp.where(southern, cross, subs - 1 - cross) > 0

    def halo(rows):
        value = jnp.where(southern, south_ref[rows, :], north_ref[rows, :])
        return jnp.where(present, value, 0.0)

    own = own_ref[0:pad, :]
    far = halo(slice(0, pad))
    far_misc = halo(slice(2 * pad, 2 * pad + 8))
    own_misc = own_ref[2 * pad : 2 * pad + 8, :]
    sources = [
        jnp.where(lower, own, 0.0) * own_misc[0:1],
        jnp.where(lower, far, 0.0) * far_misc[0:1],
    ]
    mixed = mix(lhs_ref[...], jnp.concatenate(sources, axis=1))
    rim_c = sources[0] + own_misc[2:3] * (mixed[:, :lanes] - sources[0])
    far_c = sources[1] + far_misc[2:3] * (mixed[:, lanes:] - sources[1])
    own_wy = jnp.where(lower, turn(own, half), 0.0)
    far_wy = jnp.where(lower, turn(far, half), 0.0)
    far_wx = halo(slice(pad, 2 * pad))
    for at, value in enumerate((rim_c, far_c, own_wy, far_wy, far_wx, own_ref[pad : 2 * pad, :])):
        rim_ref[at * pad : (at + 1) * pad, :] = value
    base = RIM_TILES * pad
    rim_ref[base : base + 1, :] = own_misc[1:2]
    rim_ref[base + 1 : base + 3, :] = far_misc[1:3]
    rim_ref[base + 3 : base + 4, :] = own_misc[2:3]
    rim_ref[base + 4 : base + 8, :] = jnp.zeros((4, lanes), F32)


def rates_of(wx, wx_west, wy, wy_south):
    east = jnp.maximum(wx, 0.0)
    west = jnp.maximum(-wx_west, 0.0)
    north = jnp.maximum(wy, 0.0)
    south = jnp.maximum(-wy_south, 0.0)
    return (1.0 - east) - west - (north + south), east, west, north, south


def from_north(value, halo):
    lanes = value.shape[1]
    return jnp.where(lane_of((1, lanes)) == lanes - 1, halo, turn(value, -1))


def from_south(value, halo):
    return jnp.where(lane_of((1, value.shape[1])) == 0, halo, turn(value, 1))


def crossed(far):
    place = lane_of((1, far.shape[1])) % 4
    return jnp.where(place == 1, turn(far, -1), turn(far, 1))


def halo_of(far, x):
    return turn(far, -4 * x - 2)


def parted(terms, clusters, ids):
    return [total([jnp.where(c == wanted, t, 0.0) for t, c in zip(terms, clusters)]) for wanted in ids]


def convect(lhs, fields, strength):
    lanes = strength.shape[1]
    mixed = mix(lhs, jnp.concatenate(fields, axis=1))
    return [f + strength * (mixed[:, k * lanes : (k + 1) * lanes] - f) for k, f in enumerate(fields)]


def advance(dims, ids, lhs, x, at, rim):
    lev, _, lanes = dims
    pad = round_up(lev, 8)
    own_cluster = at.cluster(x)
    rim_row = halo_of(rim.cluster, x)
    clusters = (
        own_cluster,
        at.cluster(x + 1),
        at.cluster(x - 1),
        from_north(own_cluster, rim_row),
        from_south(own_cluster, rim_row),
    )
    clusters = [jnp.broadcast_to(c, (8, lanes)) for c in clusters]
    groups = []
    for r in range(pad // 8):
        wy, own = at.wy(x, r), at.c(x, r)
        south_wy = from_south(wy, halo_of(rim.wy(r), x))
        center, east, west, north, south = rates_of(at.wx(x, r), at.wx(x - 1, r), wy, south_wy)
        halo = halo_of(rim.c(r), x)
        terms = (
            center * own,
            east * at.c(x + 1, r),
            west * at.c(x - 1, r),
            north * from_north(own, halo),
            south * from_south(own, halo),
        )
        groups.append(parted(terms, clusters, ids))
    fields = [jnp.concatenate([group[a] for group in groups], axis=0) for a in range(len(ids))]
    return convect(lhs, fields, at.strength(x))


class Columns:
    def __init__(self, dims, c_ref, wx_ref, wy_ref, cluster_ref, strength_ref, before_ref=None, after_ref=None):
        self.lev, self.width_x, self.lanes = dims
        self.c_ref, self.wx_ref, self.wy_ref = c_ref, wx_ref, wy_ref
        self.cluster_rows = cluster_ref[...].astype(F32)
        self.strength_ref = strength_ref
        self.before_ref, self.after_ref = before_ref, after_ref

    def sent(self, ref, tile, r):
        first = tile * self.lev + 8 * r
        return ref[first : first + 8, :]

    def strided(self, ref, x, r):
        return ref[pl.ds(8 * r * self.width_x + x, 8, stride=self.width_x), :]

    def c(self, x, r):
        if x < 0:
            return self.sent(self.before_ref, -1 - x, r)
        if x >= self.width_x:
            return self.sent(self.after_ref, x - self.width_x, r)
        return self.c_ref[x, 8 * r : 8 * r + 8, :]

    def wx(self, x, r):
        if x < 0:
            return self.sent(self.before_ref, 2 if x == -1 else 4, r)
        return self.sent(self.after_ref, 2, r) if x >= self.width_x else self.strided(self.wx_ref, x, r)

    def wy(self, x, r):
        if x < 0:
            return self.sent(self.before_ref, 3, r)
        return self.sent(self.after_ref, 3, r) if x >= self.width_x else self.strided(self.wy_ref, x, r)

    def misc(self, ref, tiles, row):
        return ref[tiles * self.lev + row : tiles * self.lev + row + 1, :]

    def cluster(self, x):
        if x < 0:
            return self.misc(self.before_ref, 5, -1 - x)
        if x >= self.width_x:
            return self.misc(self.after_ref, 4, x - self.width_x)
        return self.cluster_rows[x : x + 1]

    def strength(self, x):
        if x < 0:
            return self.misc(self.before_ref, 5, 2)
        if x >= self.width_x:
            return self.misc(self.after_ref, 4, 2)
        return self.strength_ref[x : x + 1, :]


class Rim:
    def __init__(self, c, wy, cluster):
        self.c_tile, self.wy_tile, self.cluster = crossed(c), crossed(wy), crossed(cluster)

    def c(self, r):
        return self.c_tile[8 * r : 8 * r + 8]

    def wy(self, r):
        return self.wy_tile[8 * r : 8 * r + 8]


def adjoint_ids(per_device):
    first = (lax.axis_index("adj") * per_device).astype(F32)
    return [first + a for a in range(per_device)]


def inner_kernel(
    dims, per_device, rim_ref, c_ref, wx_ref, wy_ref, cluster_ref, strength_ref, lhs_ref, mixed_ref, ground_ref
):
    lev, width_x, _ = dims
    pad = round_up(lev, 8)
    at = Columns(dims, c_ref, wx_ref, wy_ref, cluster_ref, strength_ref)
    base = RIM_TILES * pad
    rim = Rim(rim_ref[pad : 2 * pad, :], rim_ref[3 * pad : 4 * pad, :], rim_ref[base + 1 : base + 2, :])
    ids = adjoint_ids(per_device)
    lhs = lhs_ref[...]
    for x in range(1, width_x - 1):
        for a, value in enumerate(advance(dims, ids, lhs, x, at, rim)):
            mixed_ref[a, x - 1, :, :] = value
            ground_ref[a, x + 1 : x + 2, :] = value[0:1]


def mixed_at(dims, inner_ref, ends_ref, a, x, r):
    width_x = dims[1]
    rows = slice(8 * r, 8 * r + 8)
    if 1 <= x < width_x - 1:
        return inner_ref[a, x - 1, rows, :]
    return ends_ref[a, x + 1 if x < 1 else x - width_x + 3, rows, :]


def second_transport(dims, at, rim_wy, far, inner_ref, ends_ref, ids, x, r):
    half = 4 * dims[1]
    wy = at.wy(x, r)
    south_wy = from_south(wy, halo_of(rim_wy, x))
    center, east, west, north, south = rates_of(at.wx(x, r), at.wx(x - 1, r), wy, south_wy)
    values = []
    for a in range(len(ids)):
        own = mixed_at(dims, inner_ref, ends_ref, a, x, r)
        halo = turn(far(a // 2, r), -4 * x - 2 - half * (a % 2))
        parts = [
            center * own,
            east * mixed_at(dims, inner_ref, ends_ref, a, x + 1, r),
            west * mixed_at(dims, inner_ref, ends_ref, a, x - 1, r),
            north * from_north(own, halo),
            south * from_south(own, halo),
        ]
        values.append(total(parts))
    return values


def ends_kernel(dims, subs, per_device, *refs):
    lev, width_x, lanes = dims
    rim_ref, before_ref, after_ref, inner_ground_ref, c_ref, wx_ref, wy_ref, cluster_ref, strength_ref, lhs_ref = refs[:10]
    ends_ref, far_ref, surface_ref, full_ref, ground_ref, west_ref, beside_ref = refs[10:]
    pad = round_up(lev, 8)
    half = 4 * width_x
    cross = lax.axis_index("sub")
    lane = lane_of((1, lanes))
    place = lane % 4
    after_slot = lane // 4 == width_x
    before_slot = lane >= lanes - 4
    at = Columns(dims, c_ref, wx_ref, wy_ref, cluster_ref, strength_ref, before_ref, after_ref)
    ids = adjoint_ids(per_device)
    lhs = lhs_ref[...]

    base = RIM_TILES * pad
    rim_c, far_c, rim_wy, far_wy, far_wx, rim_wx = (rim_ref[i * pad : (i + 1) * pad, :] for i in range(RIM_TILES))
    rim_cluster = rim_ref[base : base + 1, :]
    far_cluster = rim_ref[base + 1 : base + 2, :]
    far_strength = rim_ref[base + 2 : base + 3, :]
    rim = Rim(far_c, far_wy, far_cluster)

    def sent(ref, tile):
        return jnp.concatenate([at.sent(ref, tile, r) for r in range(pad // 8)], axis=0)

    def full(value, before, after):
        return jnp.where(before_slot, turn(before, -2), jnp.where(after_slot, turn(after, half + 2), value))

    full_c = full(rim_c, sent(before_ref, 0), sent(after_ref, 0))
    full_wy = full(rim_wy, sent(before_ref, 3), sent(after_ref, 3))
    full_wx = full(rim_wx, sent(before_ref, 2), rim_wx)
    for i, value in enumerate((full_c, full_wy, full_wx)):
        full_ref[i * pad : (i + 1) * pad, :] = value
    rows = [
        full(rim_cluster, at.cluster(-1), at.cluster(width_x)),
        full(rim_ref[base + 3 : base + 4, :], at.strength(-1), at.strength(width_x)),
    ]
    full_ref[3 * pad : 3 * pad + 2, :] = jnp.concatenate(rows, axis=0)
    full_ref[3 * pad + 2 : 3 * pad + 8, :] = jnp.zeros((6, lanes), F32)
    picked = jnp.where(before_slot | after_slot, full_c, 0.0)
    wy_slot = (lane < 4) | (lane // 4 == width_x + 1)
    wx_slot = lane // 4 == 1
    moved_wy = full(jnp.zeros_like(rim_wy), turn(sent(before_ref, 3), 0), turn(sent(after_ref, 3), 0))
    picked = jnp.where(wy_slot, turn(moved_wy, 4), picked)
    picked = jnp.where(wx_slot, turn(sent(before_ref, 2), 6), picked).T
    picked = jnp.concatenate([picked, jnp.zeros((lanes, lanes - pad), F32)], axis=1)
    packet = picked[half : half + 8] + turn(picked[lanes - 8 : lanes], pad) + turn(picked[0:8], 2 * pad)
    tail = per_device * width_x
    surface_ref[tail : tail + 8, :] = packet
    surface_ref[tail + 8 : tail + 10, :] = jnp.concatenate(rows, axis=0)
    surface_ref[tail + 10 : tail + 16, :] = jnp.zeros((6, lanes), F32)
    for k, x in ((1, 0), (2, width_x - 1), (0, -1), (3, width_x)):
        for a, value in enumerate(advance(dims, ids, lhs, x, at, rim)):
            ends_ref[a, k, :, :] = value
            ground_ref[a, x + 1 : x + 2, :] = value[0:1]

    def rim_north(far, own):
        return turn(jnp.where(place == 2, own, far), -1)

    def rim_south(far, own):
        return turn(jnp.where(place == 1, own, far), 1)

    center, east, west, north, south = rates_of(far_wx, turn(far_wx, 4), far_wy, rim_south(far_wy, rim_wy))
    terms = (
        center * far_c,
        east * turn(far_c, -4),
        west * turn(far_c, 4),
        north * rim_north(far_c, rim_c),
        south * rim_south(far_c, rim_c),
    )
    clusters = (
        far_cluster,
        turn(far_cluster, -4),
        turn(far_cluster, 4),
        rim_north(far_cluster, rim_cluster),
        rim_south(far_cluster, rim_cluster),
    )
    inside = jnp.where(lane < half, jnp.where(place < 2, cross, subs - 1 - cross), 0) > 0
    fields = [jnp.where(inside, f, 0.0) for f in parted(terms, clusters, ids)]
    joined = [fields[a] + turn(fields[a + 1], half) for a in range(0, per_device, 2)]
    far_mixed = [crossed(f) for f in convect(lhs, joined, far_strength + turn(far_strength, half))]
    for at_pair, value in enumerate(far_mixed):
        far_ref[at_pair, 0:pad, :] = value
    far_ref[0, pad : pad + 8, :] = jnp.zeros((8, lanes), F32)
    for pair in range(1, len(far_mixed)):
        far_ref[pair, pad : pad + 8, :] = jnp.zeros((8, lanes), F32)

    rows = [rim.wy_tile[0:1]] + [turn(far_mixed[a // 2][0:1], half * (a % 2)) for a in range(per_device)]
    tall = round_up(len(rows), 8)
    stack = jnp.concatenate(rows + [jnp.zeros((tall - len(rows), lanes), F32)], axis=0)
    for x in range(width_x):
        beside_ref[x * tall : (x + 1) * tall, :] = halo_of(stack, x)

    def beside(at_row):
        return beside_ref[pl.ds(at_row, width_x, stride=tall), :]

    west_ref[0:1, :] = at.sent(before_ref, 2, 0)[0:1]
    west_ref[1 : width_x + 1, :] = wx_ref[0:width_x, :]
    wx, wy = wx_ref[0:width_x, :], wy_ref[0:width_x, :]
    south_wy = from_south(wy, beside(0))
    center, east, west, north, south = rates_of(wx, west_ref[0:width_x, :], wy, south_wy)
    for a in range(per_device):
        ground_ref[a, 2:width_x, :] = inner_ground_ref[a, 2:width_x, :]
        own = ground_ref[a, 1 : width_x + 1, :]
        rim_rows = beside(1 + a)
        parts = [
            center * own,
            east * ground_ref[a, 2 : width_x + 2, :],
            west * ground_ref[a, 0:width_x, :],
            north * from_north(own, rim_rows),
            south * from_south(own, rim_rows),
        ]
        surface_ref[a * width_x : (a + 1) * width_x, :] = total(parts)


def output_kernel(dims, per_device, *refs):
    lev, width_x, _ = dims
    rim_ref, before_ref, inner_ref, ends_ref, far_ref, wx_ref, wy_ref, cluster_ref, strength_ref = refs[:9]
    out_ref, token_ref, edge_ref, field_ref, sem = refs[9:]
    token_ref[...] = jnp.zeros(token_ref.shape, F32)
    pad = round_up(lev, 8)
    at = Columns(dims, None, wx_ref, wy_ref, cluster_ref, strength_ref, before_ref)
    ids = range(per_device)

    def far(pair, r):
        return far_ref[pair, 8 * r : 8 * r + 8, :]

    rim_wys = [crossed(rim_ref[3 * pad + 8 * r : 3 * pad + 8 * r + 8, :]) for r in range(pad // 8)]
    copies = []
    for x in range(width_x):
        for r in range(pad // 8):
            rim_wy = rim_wys[r]
            values = second_transport(dims, at, rim_wy, far, inner_ref, ends_ref, ids, x, r)
            for a, value in enumerate(values):
                if x in (0, width_x - 1):
                    edge_ref[a, min(x, 1), 8 * r : 8 * r + 8, :] = value
                else:
                    field_ref[a, x, 8 * r : 8 * r + 8, :] = value
        for a in range(per_device if 0 < x < width_x - 1 else 0):
            source = field_ref.at[a, x, pl.ds(0, lev), :]
            copies.append(pltpu.make_async_copy(source, out_ref.at[a, :, x, 0, :], sem.at[len(copies)]))
            copies[-1].start()
    for copy in copies:
        copy.wait()


def quotient(value, count):
    if count & (count - 1) == 0:
        return value >> (count.bit_length() - 1), value & (count - 1)
    return lax.div(value, count), lax.rem(value, count)


def tables_kernel(dims, tiles, subs, n_rim, cell_ref, weight_ref, hot_ref, share_ref):
    _, width_x, width_y = dims
    slots, elements = cell_ref.shape
    tile_pos = lax.axis_index("tiles")
    cross = lax.axis_index("sub")
    column_x, row_y = quotient(cell_ref[...], width_y * subs)
    block_x, inner_x = quotient(column_x, width_x)
    block_y, lane_y = quotient(row_y, width_y)
    step = block_x - tile_pos
    step = jnp.where(step < -1, step + tiles, jnp.where(step > 1, step - tiles, step))
    if n_rim == 2:
        side = jnp.where(block_y == cross, 0, 1)
    else:
        side = block_y - cross + 1
    at_y = side * width_y + lane_y
    at_x = (step + 1) * width_x + inner_x
    weight = weight_ref[...]
    group = width_y
    rows = lax.broadcasted_iota(jnp.int32, (16, group), 0)
    for g in range(0, elements, group):
        lanes = slice(g, g + group)
        for k in range(slots):
            y = jnp.broadcast_to(at_y[k : k + 1, lanes], (16, group)) - rows
            for first in range(0, n_rim * width_y, 16):
                hot_ref[k, first : first + 16, lanes] = jnp.where(y == first, 1.0, 0.0).astype(BF16)
            x = jnp.broadcast_to(at_x[k : k + 1, lanes], (16, group)) - rows
            w = jnp.broadcast_to(weight[k : k + 1, lanes], (16, group))
            for first in range(0, 3 * width_x, 16):
                share_ref[k, first : first + 16, lanes] = jnp.where(x == first, w, 0.0)


def looked_up(dims, per_device, blocks, hot_ref, share_ref, lanes):
    width_x = dims[1]
    rows = per_device * width_x
    surfaces = [split(jnp.concatenate(places, axis=1)) for _, places in blocks]
    lhs = jnp.concatenate([part for pair in surfaces for part in pair], axis=0)
    sums = [None] * per_device
    for k in range(hot_ref.shape[0]):
        found = jnp.dot(lhs, hot_ref[k, :, lanes], preferred_element_type=F32)
        for at, (step, _) in enumerate(blocks):
            share = share_ref[k, (step + 1) * width_x : (step + 2) * width_x, lanes]
            for a in range(per_device):
                high = 2 * at * rows + a * width_x
                low = high + rows
                value = (found[high : high + width_x] + found[low : low + width_x]) * share
                sums[a] = value if sums[a] is None else sums[a] + value
    return jnp.concatenate([jnp.sum(s, axis=0, keepdims=True) for s in sums], axis=0)


def wide_lanes(elements):
    wide = 256 if elements % 256 == 0 else 128
    return [slice(g, g + wide) for g in range(0, elements, wide)]


def sense_here_kernel(dims, per_device, n_rim, hot_ref, share_ref, here_ref, out_ref):
    rows = per_device * dims[1]
    blocks = [(0, [here_ref[k * rows : (k + 1) * rows, :] for k in range(n_rim)])]
    for lanes in wide_lanes(out_ref.shape[1]):
        out_ref[:, lanes] = looked_up(dims, per_device, blocks, hot_ref, share_ref, lanes)


def sense_kernel(dims, per_device, n_rim, hot_ref, share_ref, partial_ref, before_ref, after_ref, out_ref, own_ref, sem):
    rows = per_device * dims[1]
    blocks = [
        (step, [ref[k * rows : (k + 1) * rows, :] for k in range(n_rim)])
        for step, ref in ((-1, before_ref), (1, after_ref))
    ]
    for lanes in wide_lanes(own_ref.shape[1]):
        value = looked_up(dims, per_device, blocks, hot_ref, share_ref, lanes)
        own_ref[:, lanes] = partial_ref[:, lanes] + value
    copy = pltpu.make_async_copy(own_ref, out_ref, sem)
    copy.start()
    copy.wait()


class Seam:
    def __init__(self, dims, c, wy, wx, cluster, strength):
        _, self.width_x, lanes = dims
        self.lane = lane_of((1, lanes))
        self.place = self.lane % 4
        slot = self.lane // 4
        self.first, self.last = slot == 0, slot == self.width_x - 1
        self.beside = (slot == lanes // 4 - 1) | (slot == self.width_x)
        self.c, self.cluster, self.strength = c, cluster, strength
        self.east = jnp.maximum(wx, 0.0)
        self.west = jnp.maximum(-turn(wx, 4), 0.0)
        self.north = jnp.maximum(wy, 0.0)
        self.south = jnp.maximum(-turn(wy, 1), 0.0)

    def missing(self, lhs, ids):
        near = (self.place == 1) | (self.place == 2)
        wanted_slots = near & (self.beside | self.first | self.last)
        moved = [(turn(self.c, k), turn(self.cluster, k)) for k in (-1, 1, 4, -4)]
        fields = []
        for wanted in ids:
            own = jnp.where(self.cluster == wanted, self.c, 0.0)
            from_n, from_s, from_w, from_e = (jnp.where(row == wanted, c, 0.0) for c, row in moved)
            upright = jnp.where(self.place == 1, self.north * from_n, self.south * (from_s - own))
            level = jnp.where(self.first, self.west * (from_w - own), self.east * from_e)
            fields.append(jnp.where(wanted_slots, jnp.where(self.beside, upright, level), 0.0))
        return convect(lhs, fields, self.strength)


def seam_transport(rates, missing):
    east, west, north, south = rates
    lane = lane_of((1, missing.shape[1]))
    place, slot = lane % 4, lane // 4
    level = jnp.where(slot == 0, west * turn(missing, 4), east * turn(missing, -4))
    return level + jnp.where(place == 1, north * turn(missing, -1), south * turn(missing, 1))


def own_places(subs):
    cross = lax.axis_index("sub")
    if subs == 2:
        own_south = (cross == 0).astype(jnp.int32)
        return [own_south]
    return [jnp.int32(0), jnp.int32(1)]


def patch_kernel(dims, subs, per_device, *refs):
    lev, width_x, lanes = dims
    rim_ref, full_ref, own_ref, south_ref, north_ref, lhs_ref, _, whole_ref, seam_ref = refs
    pad = round_up(lev, 8)
    half = 4 * width_x
    rows = per_device * width_x
    lane = lane_of((1, lanes))
    southern = lane % 4 < 2
    before_slot = lane >= lanes - 4
    after_slot = lane // 4 == width_x
    ids = adjoint_ids(per_device)
    lhs = lhs_ref[...]
    cross = lax.axis_index("sub")
    present = jnp.where(southern, cross, subs - 1 - cross) > 0

    def upright(ref):
        turned = ref[rows : rows + 8, :].T
        turned = jnp.concatenate([turned, jnp.zeros((lanes, lanes - 8), F32)], axis=1)
        return [turned[i * pad : (i + 1) * pad] for i in range(3)]

    def beyond(value, south, north, before, after):
        def placed(tile):
            moved = turn(tile[0], lanes - 4 - before)
            return moved if after is None else jnp.where(after_slot, turn(tile[1], half - after), moved)

        moved = placed(south) if south is north else jnp.where(southern, placed(south), placed(north))
        moved = jnp.where(present, moved, 0.0)
        slots = before_slot if after is None else before_slot | after_slot
        return jnp.where(slots, moved, value)

    south = upright(south_ref)
    north = south if subs == 2 else upright(north_ref)

    def pair(first, second):
        one = (south[first], south[second])
        return one, one if subs == 2 else (north[first], north[second])

    far_c, far_wy, far_wx = (rim_ref[i * pad : (i + 1) * pad, :] for i in (1, 3, 4))
    c_pair, wy_pair = pair(1, 0), pair(2, 0)
    if subs == 2:
        c_pair, wy_pair = (c_pair[0], c_pair[0]), (wy_pair[0], wy_pair[0])
    far_c = beyond(far_c, *c_pair, 4, 0)
    far_wx = beyond(far_wx, *wy_pair, 4, None)
    far_wy = beyond(far_wy, *wy_pair, 0, 4)
    base = RIM_TILES * pad

    def beyond_row(value, at_row):
        south_row = south_ref[rows + at_row : rows + at_row + 1, :]
        north_row = north_ref[rows + at_row : rows + at_row + 1, :]
        moved = jnp.where(present, jnp.where(southern, south_row, north_row), 0.0)
        return jnp.where(before_slot | after_slot, moved, value)

    far_cluster = beyond_row(rim_ref[base + 1 : base + 2, :], 8)
    far_strength = beyond_row(rim_ref[base + 2 : base + 3, :], 9)
    full_c, full_wy, full_wx = (full_ref[i * pad : (i + 1) * pad, :] for i in range(3))
    full_cluster = full_ref[3 * pad : 3 * pad + 1, :]
    full_strength = full_ref[3 * pad + 1 : 3 * pad + 2, :]
    surfaces = [own_ref, south_ref] if subs == 2 else [south_ref, own_ref, north_ref]
    for k, ref in enumerate(surfaces):
        whole_ref[k * rows : (k + 1) * rows, :] = ref[0:rows, :]
    for k, own_south in enumerate(own_places(subs)):
        mine = jnp.where(southern, own_south, 1 - own_south) > 0
        seam = Seam(
            dims,
            jnp.where(mine, full_c, far_c),
            jnp.where(mine, full_wy, far_wy),
            jnp.where(mine, full_wx, far_wx),
            jnp.where(mine, full_cluster, far_cluster),
            jnp.where(mine, full_strength, far_strength),
        )
        missing = seam.missing(lhs, ids)
        rates = (seam.east, seam.west, seam.north, seam.south)
        for i, value in enumerate(rates + tuple(missing)):
            seam_ref[k, i * pad : (i + 1) * pad, :] = value
        far_at = 1 if subs == 2 else 2 * k
        own_at = 0 if subs == 2 else 1
        own_lane = jnp.where(own_south > 0, lanes - 1, 0)
        for a, value in enumerate(missing):
            change = seam_transport([rate[0:8] for rate in rates], value[0:8])[0:1]
            for x in (0, width_x - 1):
                row = turn(change, -4 * x - 2)
                for block, at_lane in ((own_at, own_lane), (far_at, lanes - 1 - own_lane)):
                    at = block * rows + a * width_x + x
                    whole_ref[at : at + 1, :] = whole_ref[at : at + 1, :] + jnp.where(lane == at_lane, row, 0.0)


def output_ends_kernel(dims, subs, per_device, _, seam_ref, edge_ref, out_ref, done_ref, sem):
    lev, width_x, lanes = dims
    pad = round_up(lev, 8)
    lane = lane_of((1, lanes))
    copies = []
    for a in range(per_device):
        columns = [edge_ref[a, 0], edge_ref[a, 1]]
        for k, own_south in enumerate(own_places(subs)):
            rates = [seam_ref[k, i * pad : (i + 1) * pad, :] for i in range(4)]
            change = seam_transport(rates, seam_ref[k, (4 + a) * pad : (5 + a) * pad, :])
            own = lane == jnp.where(own_south > 0, lanes - 1, 0)
            for i, x in enumerate((0, width_x - 1)):
                columns[i] = columns[i] + jnp.where(own, turn(change, -4 * x - 2), 0.0)
        for i, x in enumerate((0, width_x - 1)):
            done_ref[a, i, :, :] = columns[i]
            source = done_ref.at[a, i, pl.ds(0, lev), :]
            copies.append(pltpu.make_async_copy(source, out_ref.at[a, :, x, 0, :], sem.at[len(copies)]))
            copies[-1].start()
    for copy in copies:
        copy.wait()


def ring(value, axis, steps):
    count = lax.axis_size(axis)
    return lax.ppermute(value, axis, [(i, (i + steps) % count) for i in range(count)])


def across(value):
    count = lax.axis_size("sub")
    if count == 2:
        other = ring(value, "sub", 1)
        return other, other
    from_south = lax.ppermute(value, "sub", [(i, i + 1) for i in range(count - 1)])
    from_north = lax.ppermute(value, "sub", [(i + 1, i) for i in range(count - 1)])
    return from_south, from_north


def body(
    innovation,
    cluster,
    kernel,
    wind_x,
    wind_y,
    conv_strength,
    conv_matrix,
    margin_cell,
    margin_weight,
):
    dims = kernel.shape
    lev, width_x, width_y = dims
    tiles = lax.axis_size("tiles")
    subs = lax.axis_size("sub")
    per_device = ADJ // lax.axis_size("adj")
    pad = round_up(lev, 8)
    deep = round_up(lev, 16)
    flat = (lev * width_x, width_y)
    tall = (pad * width_x, width_y)
    small = innovation.shape
    sources = (
        kernel.reshape(flat),
        wind_x.reshape(flat),
        wind_y.reshape(flat),
        innovation,
        cluster,
        conv_strength,
        conv_matrix,
        margin_cell.T,
        margin_weight.T,
    )
    outs = [tall, tall, tall, small, (small, jnp.int32), small, conv_matrix.shape]
    outs += [(sources[7].shape, jnp.int32), sources[8].shape, ((pad, 3 * deep), BF16), (2 * pad + 8, width_y)]
    fetched = call(
        functools.partial(fetch_kernel, dims),
        outs,
        sources,
        scratch=(pltpu.SemaphoreType.DMA((len(sources),)),),
        far_in=True,
    )
    air, wx, wy, innov, group, strength, _, cell, weight, lhs, own_rim = fetched
    south_rim, north_rim = across(own_rim)
    first, to_east, to_west = call(
        functools.partial(first_mix_kernel, dims),
        [(width_x, pad, width_y), (5 * lev + 4, width_y), (4 * lev + 4, width_y)],
        (air, innov, strength, lhs, wx, wy, group),
        cost=400000,
    )
    before = ring(to_east, "tiles", 1)
    after = ring(to_west, "tiles", -1)
    (rim,) = call(
        functools.partial(rim_kernel, dims, subs),
        [(RIM_TILES * pad + 8, width_y)],
        (own_rim, south_rim, north_rim, lhs),
        cost=400000,
    )
    inner, ground = call(
        functools.partial(inner_kernel, dims, per_device),
        [(per_device, width_x - 2, pad, width_y), (per_device, width_x + 8, width_y)],
        (rim, first, wx, wy, group, strength, lhs),
        cost=4000000,
    )
    ends, far, surface, full = call(
        functools.partial(ends_kernel, dims, subs, per_device),
        [
            (per_device, 4, pad, width_y),
            ((per_device + 1) // 2, pad + 8, width_y),
            (per_device * width_x + 16, width_y),
            (3 * pad + 8, width_y),
        ],
        (rim, before, after, ground, first, wx, wy, group, strength, lhs),
        scratch=(
            pltpu.VMEM((per_device, width_x + 8, width_y), F32),
            pltpu.VMEM((width_x + 8, width_y), F32),
            pltpu.VMEM((width_x * round_up(per_device + 1, 8), width_y), F32),
        ),
    )
    south_surface, north_surface = across(surface)
    field, token, edge = call(
        functools.partial(output_kernel, dims, per_device),
        [(per_device, lev, width_x, 1, width_y), (8, width_y), (per_device, 2, pad, width_y)],
        (rim, before, inner, ends, far, wx, wy, group, strength),
        scratch=(
            pltpu.VMEM((per_device, width_x, pad, width_y), F32),
            pltpu.SemaphoreType.DMA((per_device * width_x,)),
        ),
        far_out=(0,),
        cost=4000000,
    )
    n_rim = min(subs, 3)
    rows = per_device * width_x
    seams = 1 if subs == 2 else 2
    whole, seam = call(
        functools.partial(patch_kernel, dims, subs, per_device),
        [(n_rim * rows, width_y), (seams, (4 + per_device) * pad, width_y)],
        (rim, full, surface, south_surface, north_surface, lhs, token),
    )
    surface_before = ring(whole, "tiles", 1)
    surface_after = ring(whole, "tiles", -1)
    near, hbm = pl.BlockSpec(memory_space=pltpu.VMEM), pl.BlockSpec(memory_space=pl.ANY)
    field = pl.pallas_call(
        functools.partial(output_ends_kernel, dims, subs, per_device),
        out_shape=jax.ShapeDtypeStruct(field.shape, F32),
        in_specs=[hbm, near, near],
        out_specs=hbm,
        scratch_shapes=[pltpu.VMEM((per_device, 2, pad, width_y), F32), pltpu.SemaphoreType.DMA((2 * per_device,))],
        input_output_aliases={0: 0},
        compiler_params=pltpu.CompilerParams(vmem_limit_bytes=VMEM_BYTES),
        cost_estimate=pl.CostEstimate(flops=1000000, bytes_accessed=1000000, transcendentals=0),
        name="output_ends",
    )(field, *[pltpu.with_memory_space_constraint(v, pltpu.VMEM) for v in (seam, edge)])
    slots, elements = cell.shape
    hot, share = call(
        functools.partial(tables_kernel, dims, tiles, subs, n_rim),
        [((slots, n_rim * width_y, elements), BF16), (slots, 3 * width_x, elements)],
        (cell, weight),
        cost=2000000,
    )
    (partial,) = call(
        functools.partial(sense_here_kernel, dims, per_device, n_rim),
        [(per_device, elements)],
        (hot, share, whole),
        cost=2000000,
    )
    (sensed,) = call(
        functools.partial(sense_kernel, dims, per_device, n_rim),
        [(per_device, elements)],
        (hot, share, partial, surface_before, surface_after),
        scratch=(pltpu.VMEM((per_device, elements), F32), pltpu.SemaphoreType.DMA),
        far_out=(0,),
    )
    return (field.reshape(per_device, lev, width_x, width_y), sensed)


def solution(mesh):
    in_specs = (
        P(("groups", "tiles"), "sub"),
        P(("groups", "tiles"), "sub"),
        P(None, "tiles", "sub"),
        P(None, "tiles", "sub"),
        P(None, "tiles", "sub"),
        P("tiles", "sub"),
        P(),
        P(("tiles", "sub"), None),
        P(("tiles", "sub"), None),
    )
    out_specs = (P(("groups", "adj"), None, "tiles", "sub"), P(("groups", "adj"), ("tiles", "sub")))
    return jax.shard_map(body, mesh=mesh, in_specs=in_specs, out_specs=out_specs, check_vma=False)
```

```python
import functools

import jax
import jax.numpy as jnp
from jax import lax
from jax.experimental import pallas as pl
from jax.experimental.pallas import tpu as pltpu
from jax.sharding import PartitionSpec as P


ADJ = 8
F32 = jnp.float32
BF16 = jnp.bfloat16
VMEM_BYTES = 16 << 20
RIM_TILES = 6


def call(kernel, outs, args, scratch=(), far_in=False, far_out=(), cost=0):
    near = pl.BlockSpec(memory_space=pltpu.VMEM)
    far = pl.BlockSpec(memory_space=pl.ANY)
    outs = [out for out in outs]
    shapes = [(out, F32) if isinstance(out[-1], int) else out for out in outs]
    return pl.pallas_call(
        kernel,
        out_shape=[(jax.ShapeDtypeStruct if at in far_out else pltpu.VMEM)(*out) for at, out in enumerate(shapes)],
        in_specs=[far if far_in else near] * len(args),
        out_specs=[far if at in far_out else near for at in range(len(outs))],
        scratch_shapes=list(scratch),
        compiler_params=pltpu.CompilerParams(vmem_limit_bytes=VMEM_BYTES),
        cost_estimate=pl.CostEstimate(flops=cost, bytes_accessed=cost, transcendentals=0) if cost else None,
    )(*[pltpu.with_memory_space_constraint(arg, pltpu.HBM if far_in else pltpu.VMEM) for arg in args])


def round_up(count, unit):
    return count + -count % unit


def split(value):
    high = value.astype(BF16)
    return high, (value - high.astype(F32)).astype(BF16)


def mix(lhs, field):
    short = lhs.shape[1] // 3 - field.shape[0]
    if short:
        field = jnp.concatenate([field, jnp.zeros((short, field.shape[1]), F32)], axis=0)
    high, low = split(field)
    return jnp.dot(lhs, jnp.concatenate([high, high, low], axis=0), preferred_element_type=F32)


def lane_of(shape):
    return lax.broadcasted_iota(jnp.int32, shape, len(shape) - 1)


def turn(value, steps):
    steps = steps % value.shape[-1]
    return value if steps == 0 else pltpu.roll(value, steps, value.ndim - 1)


def total(parts):
    while len(parts) > 1:
        parts = [parts[i] + parts[i + 1] if i + 1 < len(parts) else parts[i] for i in range(0, len(parts), 2)]
    return parts[0]


def fetch_kernel(dims, *refs):
    lev, width_x, lanes = dims
    sources, (kernel, wx, wy, innov, cluster, strength, matrix, cell, weight, lhs, rim), scratch = (
        refs[:9],
        refs[9:20],
        refs[20:],
    )
    (sem,) = scratch
    pad = round_up(lev, 8)
    deep = lhs.shape[1] // 3
    half = 4 * width_x
    whole = lev * width_x
    copies = [pltpu.make_async_copy(s, t, sem.at[i]) for i, (s, t) in enumerate(zip(sources[3:], refs[12:18]))]
    targets = [ref.at[pl.ds(0, whole), :] for ref in (kernel, wx, wy)]
    large = [pltpu.make_async_copy(s, t, sem.at[6 + i]) for i, (s, t) in enumerate(zip(sources, targets))]
    for copy in copies[:4] + large + copies[4:]:
        copy.start()
    for ref in (kernel, wx, wy):
        ref[pl.ds(whole, (pad - lev) * width_x), :] = jnp.zeros(((pad - lev) * width_x, lanes), F32)
    slot = lane_of((1, lanes)) // 4

    def packed(ref, first, r):
        value = jnp.zeros((8, lanes), F32)
        for x in range(width_x):
            moved = turn(ref[pl.ds(8 * r * width_x + x, 8, stride=width_x), :], first + 4 * x + 2)
            value = jnp.where(slot == first // 4 + x, moved, value)
        return value

    def packed_row(value):
        moved = pltpu.roll(value, 2, 1, stride=4, stride_axis=0)
        own = lax.broadcasted_iota(jnp.int32, value.shape, 0) == slot
        return jnp.sum(jnp.where(own, moved, 0.0), axis=0, keepdims=True)

    for copy in copies[:4]:
        copy.wait()
    rim[2 * pad : 2 * pad + 1, :] = packed_row(innov[...])
    rim[2 * pad + 1 : 2 * pad + 2, :] = packed_row(cluster[...].astype(F32))
    rim[2 * pad + 2 : 2 * pad + 3, :] = packed_row(strength[...])
    rim[2 * pad + 3 : 2 * pad + 8, :] = jnp.zeros((5, lanes), F32)
    turned = matrix[...].T
    turned = jnp.concatenate([turned, jnp.zeros((pad - lev, lev), F32)], axis=0)
    turned = jnp.concatenate([turned, jnp.zeros((pad, deep - lev), F32)], axis=1)
    high = turned.astype(BF16).astype(F32)
    lhs[...] = jnp.concatenate([high, turned - high, high], axis=1).astype(BF16)
    groups = [slice(8 * r, 8 * r + 8) for r in range(pad // 8)]
    large[0].wait()
    lower = [packed(kernel, 0, r) for r in range(pad // 8)]
    large[2].wait()
    for r, rows in enumerate(groups):
        rim[rows, :] = jnp.where(slot * 4 >= half, packed(wy, half, r), lower[r])
    large[1].wait()
    for r in range(pad // 8):
        rim[pad + 8 * r : pad + 8 * r + 8, :] = packed(wx, 0, r)
    for copy in copies[4:]:
        copy.wait()


def first_columns(dims, kernel_ref, innov_ref, strength_ref, lhs, x):
    lev, width_x, lanes = dims
    pad = round_up(lev, 8)
    tiles = [kernel_ref[pl.ds(at, pad, stride=width_x), :] * innov_ref[at : at + 1, :] for at in (x, x + 1)]
    mixed = mix(lhs, jnp.concatenate(tiles, axis=1))
    parts = [mixed[:, k * lanes : (k + 1) * lanes] for k in (0, 1)]
    return [t + strength_ref[x + k : x + k + 1, :] * (p - t) for k, (t, p) in enumerate(zip(tiles, parts))]


def first_ends_kernel(dims, *refs):
    lev, width_x, lanes = dims
    kernel_ref, innov_ref, strength_ref, lhs_ref, wx_ref, wy_ref, cluster_ref, east_ref, west_ref = refs
    pad = round_up(lev, 8)
    lhs = lhs_ref[...]
    last = width_x - 1
    cluster = cluster_ref[...].astype(F32)

    def column(ref, x):
        return ref[pl.ds(x, pad, stride=width_x), :]

    def put(ref, tiles, near, next_one):
        for at, value in enumerate(tiles):
            top = min(pad, ref.shape[0] - at * lev)
            ref[at * lev : at * lev + top, :] = value[:top]
        base = len(tiles) * lev
        ref[base : base + 1, :] = cluster[near : near + 1]
        ref[base + 1 : base + 2, :] = cluster[next_one : next_one + 1]
        ref[base + 2 : base + 3, :] = strength_ref[near : near + 1, :]
        ref[base + 3 : base + 4, :] = jnp.zeros((1, lanes), F32)

    inside, outer = first_columns(dims, kernel_ref, innov_ref, strength_ref, lhs, last - 1)
    put(
        east_ref,
        (outer, inside, column(wx_ref, last), column(wy_ref, last), column(wx_ref, last - 1)),
        last,
        last - 1,
    )
    outer, inside = first_columns(dims, kernel_ref, innov_ref, strength_ref, lhs, 0)
    put(west_ref, (outer, inside, column(wx_ref, 0), column(wy_ref, 0)), 0, 1)


def first_mix_kernel(dims, kernel_ref, innov_ref, strength_ref, lhs_ref, out_ref):
    lhs = lhs_ref[...]
    for x in range(0, dims[1], 2):
        for k, value in enumerate(first_columns(dims, kernel_ref, innov_ref, strength_ref, lhs, x)):
            out_ref[x + k, :, :] = value


def rim_kernel(dims, subs, own_ref, south_ref, north_ref, lhs_ref, rim_ref):
    lev, width_x, lanes = dims
    pad = round_up(lev, 8)
    half = 4 * width_x
    cross = lax.axis_index("sub")
    lane = lane_of((1, lanes))
    lower = lane < half
    southern = lane % 4 < 2
    present = jnp.where(southern, cross, subs - 1 - cross) > 0

    def halo(rows):
        value = jnp.where(southern, south_ref[rows, :], north_ref[rows, :])
        return jnp.where(present, value, 0.0)

    own = own_ref[0:pad, :]
    far = halo(slice(0, pad))
    far_misc = halo(slice(2 * pad, 2 * pad + 8))
    own_misc = own_ref[2 * pad : 2 * pad + 8, :]
    sources = [
        jnp.where(lower, own, 0.0) * own_misc[0:1],
        jnp.where(lower, far, 0.0) * far_misc[0:1],
    ]
    mixed = mix(lhs_ref[...], jnp.concatenate(sources, axis=1))
    rim_c = sources[0] + own_misc[2:3] * (mixed[:, :lanes] - sources[0])
    far_c = sources[1] + far_misc[2:3] * (mixed[:, lanes:] - sources[1])
    own_wy = jnp.where(lower, turn(own, half), 0.0)
    far_wy = jnp.where(lower, turn(far, half), 0.0)
    far_wx = halo(slice(pad, 2 * pad))
    for at, value in enumerate((rim_c, far_c, own_wy, far_wy, far_wx, own_ref[pad : 2 * pad, :])):
        rim_ref[at * pad : (at + 1) * pad, :] = value
    base = RIM_TILES * pad
    rim_ref[base : base + 1, :] = own_misc[1:2]
    rim_ref[base + 1 : base + 3, :] = far_misc[1:3]
    rim_ref[base + 3 : base + 4, :] = own_misc[2:3]
    rim_ref[base + 4 : base + 8, :] = jnp.zeros((4, lanes), F32)


def rates_of(wx, wx_west, wy, wy_south):
    east = jnp.maximum(wx, 0.0)
    west = jnp.maximum(-wx_west, 0.0)
    north = jnp.maximum(wy, 0.0)
    south = jnp.maximum(-wy_south, 0.0)
    return (1.0 - east) - west - (north + south), east, west, north, south


def from_north(value, halo):
    lanes = value.shape[1]
    return jnp.where(lane_of((1, lanes)) == lanes - 1, halo, turn(value, -1))


def from_south(value, halo):
    return jnp.where(lane_of((1, value.shape[1])) == 0, halo, turn(value, 1))


def crossed(far):
    place = lane_of((1, far.shape[1])) % 4
    return jnp.where(place == 1, turn(far, -1), turn(far, 1))


def halo_of(far, x):
    return turn(far, -4 * x - 2)


def parted(terms, clusters, ids):
    return [total([jnp.where(c == wanted, t, 0.0) for t, c in zip(terms, clusters)]) for wanted in ids]


def convect(lhs, fields, strength):
    lanes = strength.shape[1]
    mixed = mix(lhs, jnp.concatenate(fields, axis=1))
    return [f + strength * (mixed[:, k * lanes : (k + 1) * lanes] - f) for k, f in enumerate(fields)]


def advance(dims, ids, lhs, x, at, rim):
    lev, _, lanes = dims
    pad = round_up(lev, 8)
    own_cluster = at.cluster(x)
    rim_row = halo_of(rim.cluster, x)
    clusters = (
        own_cluster,
        at.cluster(x + 1),
        at.cluster(x - 1),
        from_north(own_cluster, rim_row),
        from_south(own_cluster, rim_row),
    )
    clusters = [jnp.broadcast_to(c, (8, lanes)) for c in clusters]
    groups = []
    for r in range(pad // 8):
        wy, own = at.wy(x, r), at.c(x, r)
        south_wy = from_south(wy, halo_of(rim.wy(r), x))
        center, east, west, north, south = rates_of(at.wx(x, r), at.wx(x - 1, r), wy, south_wy)
        halo = halo_of(rim.c(r), x)
        terms = (
            center * own,
            east * at.c(x + 1, r),
            west * at.c(x - 1, r),
            north * from_north(own, halo),
            south * from_south(own, halo),
        )
        groups.append(parted(terms, clusters, ids))
    fields = [jnp.concatenate([group[a] for group in groups], axis=0) for a in range(len(ids))]
    return convect(lhs, fields, at.strength(x))


class Columns:
    def __init__(self, dims, c_ref, wx_ref, wy_ref, cluster_ref, strength_ref, before_ref=None, after_ref=None):
        self.lev, self.width_x, self.lanes = dims
        self.c_ref, self.wx_ref, self.wy_ref = c_ref, wx_ref, wy_ref
        self.cluster_rows = cluster_ref[...].astype(F32)
        self.strength_ref = strength_ref
        self.before_ref, self.after_ref = before_ref, after_ref

    def sent(self, ref, tile, r):
        first = tile * self.lev + 8 * r
        return ref[first : first + 8, :]

    def strided(self, ref, x, r):
        return ref[pl.ds(8 * r * self.width_x + x, 8, stride=self.width_x), :]

    def c(self, x, r):
        if x < 0:
            return self.sent(self.before_ref, -1 - x, r)
        if x >= self.width_x:
            return self.sent(self.after_ref, x - self.width_x, r)
        return self.c_ref[x, 8 * r : 8 * r + 8, :]

    def wx(self, x, r):
        if x < 0:
            return self.sent(self.before_ref, 2 if x == -1 else 4, r)
        return self.sent(self.after_ref, 2, r) if x >= self.width_x else self.strided(self.wx_ref, x, r)

    def wy(self, x, r):
        if x < 0:
            return self.sent(self.before_ref, 3, r)
        return self.sent(self.after_ref, 3, r) if x >= self.width_x else self.strided(self.wy_ref, x, r)

    def misc(self, ref, tiles, row):
        return ref[tiles * self.lev + row : tiles * self.lev + row + 1, :]

    def cluster(self, x):
        if x < 0:
            return self.misc(self.before_ref, 5, -1 - x)
        if x >= self.width_x:
            return self.misc(self.after_ref, 4, x - self.width_x)
        return self.cluster_rows[x : x + 1]

    def strength(self, x):
        if x < 0:
            return self.misc(self.before_ref, 5, 2)
        if x >= self.width_x:
            return self.misc(self.after_ref, 4, 2)
        return self.strength_ref[x : x + 1, :]


class Rim:
    def __init__(self, c, wy, cluster):
        self.c_tile, self.wy_tile, self.cluster = crossed(c), crossed(wy), crossed(cluster)

    def c(self, r):
        return self.c_tile[8 * r : 8 * r + 8]

    def wy(self, r):
        return self.wy_tile[8 * r : 8 * r + 8]


def adjoint_ids(per_device):
    first = (lax.axis_index("adj") * per_device).astype(F32)
    return [first + a for a in range(per_device)]


def inner_kernel(
    dims, per_device, rim_ref, c_ref, wx_ref, wy_ref, cluster_ref, strength_ref, lhs_ref, mixed_ref, ground_ref
):
    lev, width_x, _ = dims
    pad = round_up(lev, 8)
    at = Columns(dims, c_ref, wx_ref, wy_ref, cluster_ref, strength_ref)
    base = RIM_TILES * pad
    rim = Rim(rim_ref[pad : 2 * pad, :], rim_ref[3 * pad : 4 * pad, :], rim_ref[base + 1 : base + 2, :])
    ids = adjoint_ids(per_device)
    lhs = lhs_ref[...]
    for x in range(1, width_x - 1):
        for a, value in enumerate(advance(dims, ids, lhs, x, at, rim)):
            mixed_ref[a, x - 1, :, :] = value
            ground_ref[a, x + 1 : x + 2, :] = value[0:1]


def mixed_at(dims, inner_ref, ends_ref, a, x, r):
    width_x = dims[1]
    rows = slice(8 * r, 8 * r + 8)
    if 1 <= x < width_x - 1:
        return inner_ref[a, x - 1, rows, :]
    return ends_ref[a, x + 1 if x < 1 else x - width_x + 3, rows, :]


def second_transport(dims, at, rim_wy, far, inner_ref, ends_ref, ids, x, r):
    half = 4 * dims[1]
    wy = at.wy(x, r)
    south_wy = from_south(wy, halo_of(rim_wy, x))
    center, east, west, north, south = rates_of(at.wx(x, r), at.wx(x - 1, r), wy, south_wy)
    values = []
    for a in range(len(ids)):
        own = mixed_at(dims, inner_ref, ends_ref, a, x, r)
        halo = turn(far(a // 2, r), -4 * x - 2 - half * (a % 2))
        parts = [
            center * own,
            east * mixed_at(dims, inner_ref, ends_ref, a, x + 1, r),
            west * mixed_at(dims, inner_ref, ends_ref, a, x - 1, r),
            north * from_north(own, halo),
            south * from_south(own, halo),
        ]
        values.append(total(parts))
    return values


def ends_kernel(dims, subs, per_device, *refs):
    lev, width_x, lanes = dims
    rim_ref, before_ref, after_ref, inner_ground_ref, c_ref, wx_ref, wy_ref, cluster_ref, strength_ref, lhs_ref = refs[:10]
    ends_ref, far_ref, surface_ref, full_ref, ground_ref, west_ref, beside_ref = refs[10:]
    pad = round_up(lev, 8)
    half = 4 * width_x
    cross = lax.axis_index("sub")
    lane = lane_of((1, lanes))
    place = lane % 4
    after_slot = lane // 4 == width_x
    before_slot = lane >= lanes - 4
    at = Columns(dims, c_ref, wx_ref, wy_ref, cluster_ref, strength_ref, before_ref, after_ref)
    ids = adjoint_ids(per_device)
    lhs = lhs_ref[...]

    base = RIM_TILES * pad
    rim_c, far_c, rim_wy, far_wy, far_wx, rim_wx = (rim_ref[i * pad : (i + 1) * pad, :] for i in range(RIM_TILES))
    rim_cluster = rim_ref[base : base + 1, :]
    far_cluster = rim_ref[base + 1 : base + 2, :]
    far_strength = rim_ref[base + 2 : base + 3, :]
    rim = Rim(far_c, far_wy, far_cluster)

    def sent(ref, tile):
        return jnp.concatenate([at.sent(ref, tile, r) for r in range(pad // 8)], axis=0)

    def full(value, before, after):
        return jnp.where(before_slot, turn(before, -2), jnp.where(after_slot, turn(after, half + 2), value))

    full_c = full(rim_c, sent(before_ref, 0), sent(after_ref, 0))
    full_wy = full(rim_wy, sent(before_ref, 3), sent(after_ref, 3))
    full_wx = full(rim_wx, sent(before_ref, 2), rim_wx)
    for i, value in enumerate((full_c, full_wy, full_wx)):
        full_ref[i * pad : (i + 1) * pad, :] = value
    rows = [
        full(rim_cluster, at.cluster(-1), at.cluster(width_x)),
        full(rim_ref[base + 3 : base + 4, :], at.strength(-1), at.strength(width_x)),
    ]
    full_ref[3 * pad : 3 * pad + 2, :] = jnp.concatenate(rows, axis=0)
    full_ref[3 * pad + 2 : 3 * pad + 8, :] = jnp.zeros((6, lanes), F32)
    picked = jnp.where(before_slot | after_slot, full_c, 0.0)
    wy_slot = (lane < 4) | (lane // 4 == width_x + 1)
    wx_slot = lane // 4 == 1
    moved_wy = full(jnp.zeros_like(rim_wy), turn(sent(before_ref, 3), 0), turn(sent(after_ref, 3), 0))
    picked = jnp.where(wy_slot, turn(moved_wy, 4), picked)
    picked = jnp.where(wx_slot, turn(sent(before_ref, 2), 6), picked).T
    picked = jnp.concatenate([picked, jnp.zeros((lanes, lanes - pad), F32)], axis=1)
    packet = picked[half : half + 8] + turn(picked[lanes - 8 : lanes], pad) + turn(picked[0:8], 2 * pad)
    tail = per_device * width_x
    surface_ref[tail : tail + 8, :] = packet
    surface_ref[tail + 8 : tail + 10, :] = jnp.concatenate(rows, axis=0)
    surface_ref[tail + 10 : tail + 16, :] = jnp.zeros((6, lanes), F32)
    for k, x in ((1, 0), (2, width_x - 1), (0, -1), (3, width_x)):
        for a, value in enumerate(advance(dims, ids, lhs, x, at, rim)):
            ends_ref[a, k, :, :] = value
            ground_ref[a, x + 1 : x + 2, :] = value[0:1]

    def rim_north(far, own):
        return turn(jnp.where(place == 2, own, far), -1)

    def rim_south(far, own):
        return turn(jnp.where(place == 1, own, far), 1)

    center, east, west, north, south = rates_of(far_wx, turn(far_wx, 4), far_wy, rim_south(far_wy, rim_wy))
    terms = (
        center * far_c,
        east * turn(far_c, -4),
        west * turn(far_c, 4),
        north * rim_north(far_c, rim_c),
        south * rim_south(far_c, rim_c),
    )
    clusters = (
        far_cluster,
        turn(far_cluster, -4),
        turn(far_cluster, 4),
        rim_north(far_cluster, rim_cluster),
        rim_south(far_cluster, rim_cluster),
    )
    inside = jnp.where(lane < half, jnp.where(place < 2, cross, subs - 1 - cross), 0) > 0
    fields = [jnp.where(inside, f, 0.0) for f in parted(terms, clusters, ids)]
    joined = [fields[a] + turn(fields[a + 1], half) for a in range(0, per_device, 2)]
    far_mixed = [crossed(f) for f in convect(lhs, joined, far_strength + turn(far_strength, half))]
    for at_pair, value in enumerate(far_mixed):
        far_ref[at_pair, 0:pad, :] = value
    far_ref[0, pad : pad + 8, :] = jnp.zeros((8, lanes), F32)
    for pair in range(1, len(far_mixed)):
        far_ref[pair, pad : pad + 8, :] = jnp.zeros((8, lanes), F32)

    rows = [rim.wy_tile[0:1]] + [turn(far_mixed[a // 2][0:1], half * (a % 2)) for a in range(per_device)]
    tall = round_up(len(rows), 8)
    stack = jnp.concatenate(rows + [jnp.zeros((tall - len(rows), lanes), F32)], axis=0)
    for x in range(width_x):
        beside_ref[x * tall : (x + 1) * tall, :] = halo_of(stack, x)

    def beside(at_row):
        return beside_ref[pl.ds(at_row, width_x, stride=tall), :]

    west_ref[0:1, :] = at.sent(before_ref, 2, 0)[0:1]
    west_ref[1 : width_x + 1, :] = wx_ref[0:width_x, :]
    wx, wy = wx_ref[0:width_x, :], wy_ref[0:width_x, :]
    south_wy = from_south(wy, beside(0))
    center, east, west, north, south = rates_of(wx, west_ref[0:width_x, :], wy, south_wy)
    for a in range(per_device):
        ground_ref[a, 2:width_x, :] = inner_ground_ref[a, 2:width_x, :]
        own = ground_ref[a, 1 : width_x + 1, :]
        rim_rows = beside(1 + a)
        parts = [
            center * own,
            east * ground_ref[a, 2 : width_x + 2, :],
            west * ground_ref[a, 0:width_x, :],
            north * from_north(own, rim_rows),
            south * from_south(own, rim_rows),
        ]
        surface_ref[a * width_x : (a + 1) * width_x, :] = total(parts)


def output_kernel(dims, per_device, *refs):
    lev, width_x, _ = dims
    rim_ref, before_ref, inner_ref, ends_ref, far_ref, wx_ref, wy_ref, cluster_ref, strength_ref = refs[:9]
    out_ref, token_ref, edge_ref, field_ref, sem = refs[9:]
    token_ref[...] = jnp.zeros(token_ref.shape, F32)
    pad = round_up(lev, 8)
    at = Columns(dims, None, wx_ref, wy_ref, cluster_ref, strength_ref, before_ref)
    ids = range(per_device)

    def far(pair, r):
        return far_ref[pair, 8 * r : 8 * r + 8, :]

    rim_wys = [crossed(rim_ref[3 * pad + 8 * r : 3 * pad + 8 * r + 8, :]) for r in range(pad // 8)]
    copies = []
    for x in range(width_x):
        for r in range(pad // 8):
            rim_wy = rim_wys[r]
            values = second_transport(dims, at, rim_wy, far, inner_ref, ends_ref, ids, x, r)
            for a, value in enumerate(values):
                if x in (0, width_x - 1):
                    edge_ref[a, min(x, 1), 8 * r : 8 * r + 8, :] = value
                else:
                    field_ref[a, x, 8 * r : 8 * r + 8, :] = value
        for a in range(per_device if 0 < x < width_x - 1 else 0):
            source = field_ref.at[a, x, pl.ds(0, lev), :]
            copies.append(pltpu.make_async_copy(source, out_ref.at[a, :, x, 0, :], sem.at[len(copies)]))
            copies[-1].start()
    for copy in copies:
        copy.wait()


def quotient(value, count):
    if count & (count - 1) == 0:
        return value >> (count.bit_length() - 1), value & (count - 1)
    return lax.div(value, count), lax.rem(value, count)


def tables_kernel(dims, tiles, subs, n_rim, cell_ref, weight_ref, hot_ref, share_ref):
    _, width_x, width_y = dims
    slots, elements = cell_ref.shape
    tile_pos = lax.axis_index("tiles")
    cross = lax.axis_index("sub")
    column_x, row_y = quotient(cell_ref[...], width_y * subs)
    block_x, inner_x = quotient(column_x, width_x)
    block_y, lane_y = quotient(row_y, width_y)
    step = block_x - tile_pos
    step = jnp.where(step < -1, step + tiles, jnp.where(step > 1, step - tiles, step))
    if n_rim == 2:
        side = jnp.where(block_y == cross, 0, 1)
    else:
        side = block_y - cross + 1
    at_y = side * width_y + lane_y
    at_x = (step + 1) * width_x + inner_x
    weight = weight_ref[...]
    group = width_y
    rows = lax.broadcasted_iota(jnp.int32, (16, group), 0)
    for g in range(0, elements, group):
        lanes = slice(g, g + group)
        for k in range(slots):
            y = jnp.broadcast_to(at_y[k : k + 1, lanes], (16, group)) - rows
            for first in range(0, n_rim * width_y, 16):
                hot_ref[k, first : first + 16, lanes] = jnp.where(y == first, 1.0, 0.0).astype(BF16)
            x = jnp.broadcast_to(at_x[k : k + 1, lanes], (16, group)) - rows
            w = jnp.broadcast_to(weight[k : k + 1, lanes], (16, group))
            for first in range(0, 3 * width_x, 16):
                share_ref[k, first : first + 16, lanes] = jnp.where(x == first, w, 0.0)


def looked_up(dims, per_device, blocks, hot_ref, share_ref, lanes):
    width_x = dims[1]
    rows = per_device * width_x
    surfaces = [split(jnp.concatenate(places, axis=1)) for _, places in blocks]
    lhs = jnp.concatenate([part for pair in surfaces for part in pair], axis=0)
    sums = [None] * per_device
    for k in range(hot_ref.shape[0]):
        found = jnp.dot(lhs, hot_ref[k, :, lanes], preferred_element_type=F32)
        for at, (step, _) in enumerate(blocks):
            share = share_ref[k, (step + 1) * width_x : (step + 2) * width_x, lanes]
            for a in range(per_device):
                high = 2 * at * rows + a * width_x
                low = high + rows
                value = (found[high : high + width_x] + found[low : low + width_x]) * share
                sums[a] = value if sums[a] is None else sums[a] + value
    return jnp.concatenate([jnp.sum(s, axis=0, keepdims=True) for s in sums], axis=0)


def wide_lanes(elements):
    wide = 256 if elements % 256 == 0 else 128
    return [slice(g, g + wide) for g in range(0, elements, wide)]


def sense_part_kernel(dims, per_device, n_rim, step, hot_ref, share_ref, block_ref, *refs):
    *found, out_ref = refs
    rows = per_device * dims[1]
    blocks = [(step, [block_ref[k * rows : (k + 1) * rows, :] for k in range(n_rim)])]
    for lanes in wide_lanes(out_ref.shape[1]):
        value = looked_up(dims, per_device, blocks, hot_ref, share_ref, lanes)
        out_ref[:, lanes] = total([ref[:, lanes] for ref in found] + [value])


def sense_last_kernel(*refs):
    *inputs, out_ref, own_ref, sem = refs
    sense_part_kernel(*inputs, own_ref)
    copy = pltpu.make_async_copy(own_ref, out_ref, sem)
    copy.start()
    copy.wait()


class Seam:
    def __init__(self, dims, c, wy, wx, cluster, strength):
        _, self.width_x, lanes = dims
        self.lane = lane_of((1, lanes))
        self.place = self.lane % 4
        slot = self.lane // 4
        self.first, self.last = slot == 0, slot == self.width_x - 1
        self.beside = (slot == lanes // 4 - 1) | (slot == self.width_x)
        self.c, self.cluster, self.strength = c, cluster, strength
        self.east = jnp.maximum(wx, 0.0)
        self.west = jnp.maximum(-turn(wx, 4), 0.0)
        self.north = jnp.maximum(wy, 0.0)
        self.south = jnp.maximum(-turn(wy, 1), 0.0)

    def missing(self, lhs, ids):
        near = (self.place == 1) | (self.place == 2)
        wanted_slots = near & (self.beside | self.first | self.last)
        moved = [(turn(self.c, k), turn(self.cluster, k)) for k in (-1, 1, 4, -4)]
        fields = []
        for wanted in ids:
            own = jnp.where(self.cluster == wanted, self.c, 0.0)
            from_n, from_s, from_w, from_e = (jnp.where(row == wanted, c, 0.0) for c, row in moved)
            upright = jnp.where(self.place == 1, self.north * from_n, self.south * (from_s - own))
            level = jnp.where(self.first, self.west * (from_w - own), self.east * from_e)
            fields.append(jnp.where(wanted_slots, jnp.where(self.beside, upright, level), 0.0))
        return convect(lhs, fields, self.strength)


def seam_transport(rates, missing):
    east, west, north, south = rates
    lane = lane_of((1, missing.shape[1]))
    place, slot = lane % 4, lane // 4
    level = jnp.where(slot == 0, west * turn(missing, 4), east * turn(missing, -4))
    return level + jnp.where(place == 1, north * turn(missing, -1), south * turn(missing, 1))


def own_places(subs):
    cross = lax.axis_index("sub")
    if subs == 2:
        own_south = (cross == 0).astype(jnp.int32)
        return [own_south]
    return [jnp.int32(0), jnp.int32(1)]


def patch_kernel(dims, subs, per_device, *refs):
    lev, width_x, lanes = dims
    rim_ref, full_ref, own_ref, south_ref, north_ref, lhs_ref, _, whole_ref, seam_ref = refs
    pad = round_up(lev, 8)
    half = 4 * width_x
    rows = per_device * width_x
    lane = lane_of((1, lanes))
    southern = lane % 4 < 2
    before_slot = lane >= lanes - 4
    after_slot = lane // 4 == width_x
    ids = adjoint_ids(per_device)
    lhs = lhs_ref[...]
    cross = lax.axis_index("sub")
    present = jnp.where(southern, cross, subs - 1 - cross) > 0

    def upright(ref):
        turned = ref[rows : rows + 8, :].T
        turned = jnp.concatenate([turned, jnp.zeros((lanes, lanes - 8), F32)], axis=1)
        return [turned[i * pad : (i + 1) * pad] for i in range(3)]

    def beyond(value, south, north, before, after):
        def placed(tile):
            moved = turn(tile[0], lanes - 4 - before)
            return moved if after is None else jnp.where(after_slot, turn(tile[1], half - after), moved)

        moved = placed(south) if south is north else jnp.where(southern, placed(south), placed(north))
        moved = jnp.where(present, moved, 0.0)
        slots = before_slot if after is None else before_slot | after_slot
        return jnp.where(slots, moved, value)

    south = upright(south_ref)
    north = south if subs == 2 else upright(north_ref)

    def pair(first, second):
        one = (south[first], south[second])
        return one, one if subs == 2 else (north[first], north[second])

    far_c, far_wy, far_wx = (rim_ref[i * pad : (i + 1) * pad, :] for i in (1, 3, 4))
    c_pair, wy_pair = pair(1, 0), pair(2, 0)
    if subs == 2:
        c_pair, wy_pair = (c_pair[0], c_pair[0]), (wy_pair[0], wy_pair[0])
    far_c = beyond(far_c, *c_pair, 4, 0)
    far_wx = beyond(far_wx, *wy_pair, 4, None)
    far_wy = beyond(far_wy, *wy_pair, 0, 4)
    base = RIM_TILES * pad

    def beyond_row(value, at_row):
        south_row = south_ref[rows + at_row : rows + at_row + 1, :]
        north_row = north_ref[rows + at_row : rows + at_row + 1, :]
        moved = jnp.where(present, jnp.where(southern, south_row, north_row), 0.0)
        return jnp.where(before_slot | after_slot, moved, value)

    far_cluster = beyond_row(rim_ref[base + 1 : base + 2, :], 8)
    far_strength = beyond_row(rim_ref[base + 2 : base + 3, :], 9)
    full_c, full_wy, full_wx = (full_ref[i * pad : (i + 1) * pad, :] for i in range(3))
    full_cluster = full_ref[3 * pad : 3 * pad + 1, :]
    full_strength = full_ref[3 * pad + 1 : 3 * pad + 2, :]
    surfaces = [own_ref, south_ref] if subs == 2 else [south_ref, own_ref, north_ref]
    for k, ref in enumerate(surfaces):
        whole_ref[k * rows : (k + 1) * rows, :] = ref[0:rows, :]
    for k, own_south in enumerate(own_places(subs)):
        mine = jnp.where(southern, own_south, 1 - own_south) > 0
        seam = Seam(
            dims,
            jnp.where(mine, full_c, far_c),
            jnp.where(mine, full_wy, far_wy),
            jnp.where(mine, full_wx, far_wx),
            jnp.where(mine, full_cluster, far_cluster),
            jnp.where(mine, full_strength, far_strength),
        )
        missing = seam.missing(lhs, ids)
        rates = (seam.east, seam.west, seam.north, seam.south)
        for i, value in enumerate(rates + tuple(missing)):
            seam_ref[k, i * pad : (i + 1) * pad, :] = value
        far_at = 1 if subs == 2 else 2 * k
        own_at = 0 if subs == 2 else 1
        own_lane = jnp.where(own_south > 0, lanes - 1, 0)
        for a, value in enumerate(missing):
            change = seam_transport([rate[0:8] for rate in rates], value[0:8])[0:1]
            for x in (0, width_x - 1):
                row = turn(change, -4 * x - 2)
                for block, at_lane in ((own_at, own_lane), (far_at, lanes - 1 - own_lane)):
                    at = block * rows + a * width_x + x
                    whole_ref[at : at + 1, :] = whole_ref[at : at + 1, :] + jnp.where(lane == at_lane, row, 0.0)


def output_ends_kernel(dims, subs, per_device, _, seam_ref, edge_ref, out_ref, done_ref, sem):
    lev, width_x, lanes = dims
    pad = round_up(lev, 8)
    lane = lane_of((1, lanes))
    copies = []
    for a in range(per_device):
        columns = [edge_ref[a, 0], edge_ref[a, 1]]
        for k, own_south in enumerate(own_places(subs)):
            rates = [seam_ref[k, i * pad : (i + 1) * pad, :] for i in range(4)]
            change = seam_transport(rates, seam_ref[k, (4 + a) * pad : (5 + a) * pad, :])
            own = lane == jnp.where(own_south > 0, lanes - 1, 0)
            for i, x in enumerate((0, width_x - 1)):
                columns[i] = columns[i] + jnp.where(own, turn(change, -4 * x - 2), 0.0)
        for i, x in enumerate((0, width_x - 1)):
            done_ref[a, i, :, :] = columns[i]
            source = done_ref.at[a, i, pl.ds(0, lev), :]
            copies.append(pltpu.make_async_copy(source, out_ref.at[a, :, x, 0, :], sem.at[len(copies)]))
            copies[-1].start()
    for copy in copies:
        copy.wait()


def ring(value, axis, steps):
    count = lax.axis_size(axis)
    return lax.ppermute(value, axis, [(i, (i + steps) % count) for i in range(count)])


def across(value):
    count = lax.axis_size("sub")
    if count == 2:
        other = ring(value, "sub", 1)
        return other, other
    from_south = lax.ppermute(value, "sub", [(i, i + 1) for i in range(count - 1)])
    from_north = lax.ppermute(value, "sub", [(i + 1, i) for i in range(count - 1)])
    return from_south, from_north


def body(
    innovation,
    cluster,
    kernel,
    wind_x,
    wind_y,
    conv_strength,
    conv_matrix,
    margin_cell,
    margin_weight,
):
    dims = kernel.shape
    lev, width_x, width_y = dims
    tiles = lax.axis_size("tiles")
    subs = lax.axis_size("sub")
    per_device = ADJ // lax.axis_size("adj")
    pad = round_up(lev, 8)
    deep = round_up(lev, 16)
    flat = (lev * width_x, width_y)
    tall = (pad * width_x, width_y)
    small = innovation.shape
    sources = (
        kernel.reshape(flat),
        wind_x.reshape(flat),
        wind_y.reshape(flat),
        innovation,
        cluster,
        conv_strength,
        conv_matrix,
        margin_cell.T,
        margin_weight.T,
    )
    outs = [tall, tall, tall, small, (small, jnp.int32), small, conv_matrix.shape]
    outs += [(sources[7].shape, jnp.int32), sources[8].shape, ((pad, 3 * deep), BF16), (2 * pad + 8, width_y)]
    fetched = call(
        functools.partial(fetch_kernel, dims),
        outs,
        sources,
        scratch=(pltpu.SemaphoreType.DMA((len(sources),)),),
        far_in=True,
    )
    air, wx, wy, innov, group, strength, _, cell, weight, lhs, own_rim = fetched
    south_rim, north_rim = across(own_rim)
    to_east, to_west = call(
        functools.partial(first_ends_kernel, dims),
        [(5 * lev + 4, width_y), (4 * lev + 4, width_y)],
        (air, innov, strength, lhs, wx, wy, group),
    )
    before = ring(to_east, "tiles", 1)
    after = ring(to_west, "tiles", -1)
    (first,) = call(
        functools.partial(first_mix_kernel, dims), [(width_x, pad, width_y)], (air, innov, strength, lhs), cost=400000
    )
    (rim,) = call(
        functools.partial(rim_kernel, dims, subs),
        [(RIM_TILES * pad + 8, width_y)],
        (own_rim, south_rim, north_rim, lhs),
        cost=400000,
    )
    inner, ground = call(
        functools.partial(inner_kernel, dims, per_device),
        [(per_device, width_x - 2, pad, width_y), (per_device, width_x + 8, width_y)],
        (rim, first, wx, wy, group, strength, lhs),
        cost=4000000,
    )
    ends, far, surface, full = call(
        functools.partial(ends_kernel, dims, subs, per_device),
        [
            (per_device, 4, pad, width_y),
            ((per_device + 1) // 2, pad + 8, width_y),
            (per_device * width_x + 16, width_y),
            (3 * pad + 8, width_y),
        ],
        (rim, before, after, ground, first, wx, wy, group, strength, lhs),
        scratch=(
            pltpu.VMEM((per_device, width_x + 8, width_y), F32),
            pltpu.VMEM((width_x + 8, width_y), F32),
            pltpu.VMEM((width_x * round_up(per_device + 1, 8), width_y), F32),
        ),
    )
    south_surface, north_surface = across(surface)
    field, token, edge = call(
        functools.partial(output_kernel, dims, per_device),
        [(per_device, lev, width_x, 1, width_y), (8, width_y), (per_device, 2, pad, width_y)],
        (rim, before, inner, ends, far, wx, wy, group, strength),
        scratch=(
            pltpu.VMEM((per_device, width_x, pad, width_y), F32),
            pltpu.SemaphoreType.DMA((per_device * width_x,)),
        ),
        far_out=(0,),
        cost=4000000,
    )
    n_rim = min(subs, 3)
    rows = per_device * width_x
    seams = 1 if subs == 2 else 2
    whole, seam = call(
        functools.partial(patch_kernel, dims, subs, per_device),
        [(n_rim * rows, width_y), (seams, (4 + per_device) * pad, width_y)],
        (rim, full, surface, south_surface, north_surface, lhs, token),
    )
    if subs > 2:
        own = whole[rows : 2 * rows]
        south_surface, north_surface = across(own)
        whole = jnp.concatenate([south_surface, own, north_surface], axis=0)
    surface_before = ring(whole, "tiles", 1)
    surface_after = ring(whole, "tiles", -1)
    near, hbm = pl.BlockSpec(memory_space=pltpu.VMEM), pl.BlockSpec(memory_space=pl.ANY)
    field = pl.pallas_call(
        functools.partial(output_ends_kernel, dims, subs, per_device),
        out_shape=jax.ShapeDtypeStruct(field.shape, F32),
        in_specs=[hbm, near, near],
        out_specs=hbm,
        scratch_shapes=[pltpu.VMEM((per_device, 2, pad, width_y), F32), pltpu.SemaphoreType.DMA((2 * per_device,))],
        input_output_aliases={0: 0},
        compiler_params=pltpu.CompilerParams(vmem_limit_bytes=VMEM_BYTES),
        cost_estimate=pl.CostEstimate(flops=1000000, bytes_accessed=1000000, transcendentals=0),
        name="output_ends",
    )(field, *[pltpu.with_memory_space_constraint(v, pltpu.VMEM) for v in (seam, edge)])
    slots, elements = cell.shape
    hot, share = call(
        functools.partial(tables_kernel, dims, tiles, subs, n_rim),
        [((slots, n_rim * width_y, elements), BF16), (slots, 3 * width_x, elements)],
        (cell, weight),
        cost=2000000,
    )
    part = functools.partial(sense_part_kernel, dims, per_device, n_rim)
    found = [(per_device, elements)]
    (sensed,) = call(functools.partial(part, 0), found, (hot, share, whole), cost=2000000)
    (sensed,) = call(functools.partial(part, 1), found, (hot, share, surface_after, sensed), cost=2000000)
    (sensed,) = call(
        functools.partial(sense_last_kernel, dims, per_device, n_rim, -1),
        found,
        (hot, share, surface_before, sensed),
        scratch=(pltpu.VMEM((per_device, elements), F32), pltpu.SemaphoreType.DMA),
        far_out=(0,),
    )
    return (field.reshape(per_device, lev, width_x, width_y), sensed)


def solution(mesh):
    in_specs = (
        P(("groups", "tiles"), "sub"),
        P(("groups", "tiles"), "sub"),
        P(None, "tiles", "sub"),
        P(None, "tiles", "sub"),
        P(None, "tiles", "sub"),
        P("tiles", "sub"),
        P(),
        P(("tiles", "sub"), None),
        P(("tiles", "sub"), None),
    )
    out_specs = (P(("groups", "adj"), None, "tiles", "sub"), P(("groups", "adj"), ("tiles", "sub")))
    return jax.shard_map(body, mesh=mesh, in_specs=in_specs, out_specs=out_specs, check_vma=False)
```

```python
import functools

import jax
import jax.numpy as jnp
from jax import lax
from jax.experimental import pallas as pl
from jax.experimental.pallas import tpu as pltpu
from jax.sharding import PartitionSpec as P


ADJ = 8
F32 = jnp.float32
BF16 = jnp.bfloat16
VMEM_BYTES = 16 << 20
RIM_TILES = 6


def call(kernel, outs, args, scratch=(), far_in=False, far_out=(), cost=0):
    near = pl.BlockSpec(memory_space=pltpu.VMEM)
    far = pl.BlockSpec(memory_space=pl.ANY)
    outs = [out for out in outs]
    shapes = [(out, F32) if isinstance(out[-1], int) else out for out in outs]
    return pl.pallas_call(
        kernel,
        out_shape=[(jax.ShapeDtypeStruct if at in far_out else pltpu.VMEM)(*out) for at, out in enumerate(shapes)],
        in_specs=[far if far_in else near] * len(args),
        out_specs=[far if at in far_out else near for at in range(len(outs))],
        scratch_shapes=list(scratch),
        compiler_params=pltpu.CompilerParams(vmem_limit_bytes=VMEM_BYTES),
        cost_estimate=pl.CostEstimate(flops=cost, bytes_accessed=cost, transcendentals=0) if cost else None,
    )(*[pltpu.with_memory_space_constraint(arg, pltpu.HBM if far_in else pltpu.VMEM) for arg in args])


def round_up(count, unit):
    return count + -count % unit


def split(value):
    high = value.astype(BF16)
    return high, (value - high.astype(F32)).astype(BF16)


def mix(lhs, field):
    short = lhs.shape[1] // 3 - field.shape[0]
    if short:
        field = jnp.concatenate([field, jnp.zeros((short, field.shape[1]), F32)], axis=0)
    high, low = split(field)
    return jnp.dot(lhs, jnp.concatenate([high, high, low], axis=0), preferred_element_type=F32)


def lane_of(shape):
    return lax.broadcasted_iota(jnp.int32, shape, len(shape) - 1)


def turn(value, steps):
    steps = steps % value.shape[-1]
    return value if steps == 0 else pltpu.roll(value, steps, value.ndim - 1)


def total(parts):
    while len(parts) > 1:
        parts = [parts[i] + parts[i + 1] if i + 1 < len(parts) else parts[i] for i in range(0, len(parts), 2)]
    return parts[0]


def fetch_kernel(dims, *refs):
    lev, width_x, lanes = dims
    sources, (kernel, wx, wy, innov, cluster, strength, matrix, cell, weight, lhs, rim), scratch = (
        refs[:9],
        refs[9:20],
        refs[20:],
    )
    (sem,) = scratch
    pad = round_up(lev, 8)
    deep = lhs.shape[1] // 3
    half = 4 * width_x
    whole = lev * width_x
    copies = [pltpu.make_async_copy(s, t, sem.at[i]) for i, (s, t) in enumerate(zip(sources[3:], refs[12:18]))]
    targets = [ref.at[pl.ds(0, whole), :] for ref in (kernel, wx, wy)]
    large = [pltpu.make_async_copy(s, t, sem.at[6 + i]) for i, (s, t) in enumerate(zip(sources, targets))]
    for copy in copies[:4] + large + copies[4:]:
        copy.start()
    for ref in (kernel, wx, wy):
        ref[pl.ds(whole, (pad - lev) * width_x), :] = jnp.zeros(((pad - lev) * width_x, lanes), F32)
    slot = lane_of((1, lanes)) // 4

    def packed(ref, first, r):
        value = jnp.zeros((8, lanes), F32)
        for x in range(width_x):
            moved = turn(ref[pl.ds(8 * r * width_x + x, 8, stride=width_x), :], first + 4 * x + 2)
            value = jnp.where(slot == first // 4 + x, moved, value)
        return value

    def packed_row(value):
        moved = pltpu.roll(value, 2, 1, stride=4, stride_axis=0)
        own = lax.broadcasted_iota(jnp.int32, value.shape, 0) == slot
        return jnp.sum(jnp.where(own, moved, 0.0), axis=0, keepdims=True)

    for copy in copies[:4]:
        copy.wait()
    rim[2 * pad : 2 * pad + 1, :] = packed_row(innov[...])
    rim[2 * pad + 1 : 2 * pad + 2, :] = packed_row(cluster[...].astype(F32))
    rim[2 * pad + 2 : 2 * pad + 3, :] = packed_row(strength[...])
    rim[2 * pad + 3 : 2 * pad + 8, :] = jnp.zeros((5, lanes), F32)
    square = [lax.broadcasted_iota(jnp.int32, (lev, lev), axis) for axis in (0, 1)]
    turned = matrix[...].T - jnp.where(square[0] == square[1], 1.0, 0.0)
    turned = jnp.concatenate([turned, jnp.zeros((pad - lev, lev), F32)], axis=0)
    turned = jnp.concatenate([turned, jnp.zeros((pad, deep - lev), F32)], axis=1)
    high = turned.astype(BF16).astype(F32)
    lhs[...] = jnp.concatenate([high, turned - high, high], axis=1).astype(BF16)
    groups = [slice(8 * r, 8 * r + 8) for r in range(pad // 8)]
    large[0].wait()
    lower = [packed(kernel, 0, r) for r in range(pad // 8)]
    large[2].wait()
    for r, rows in enumerate(groups):
        rim[rows, :] = jnp.where(slot * 4 >= half, packed(wy, half, r), lower[r])
    large[1].wait()
    for r in range(pad // 8):
        rim[pad + 8 * r : pad + 8 * r + 8, :] = packed(wx, 0, r)
    for copy in copies[4:]:
        copy.wait()


def first_columns(dims, kernel_ref, innov_ref, strength_ref, lhs, x):
    lev, width_x, lanes = dims
    pad = round_up(lev, 8)
    tiles = [kernel_ref[pl.ds(at, pad, stride=width_x), :] * innov_ref[at : at + 1, :] for at in (x, x + 1)]
    moved = mix(lhs, jnp.concatenate([strength_ref[x + k : x + k + 1, :] * t for k, t in enumerate(tiles)], axis=1))
    return [t + moved[:, k * lanes : (k + 1) * lanes] for k, t in enumerate(tiles)]


def first_ends_kernel(dims, *refs):
    lev, width_x, lanes = dims
    kernel_ref, innov_ref, strength_ref, lhs_ref, wx_ref, wy_ref, cluster_ref, east_ref, west_ref = refs
    pad = round_up(lev, 8)
    lhs = lhs_ref[...]
    last = width_x - 1
    cluster = cluster_ref[...].astype(F32)

    def column(ref, x):
        return ref[pl.ds(x, pad, stride=width_x), :]

    def put(ref, tiles, near, next_one):
        for at, value in enumerate(tiles):
            top = min(pad, ref.shape[0] - at * lev)
            ref[at * lev : at * lev + top, :] = value[:top]
        base = len(tiles) * lev
        ref[base : base + 1, :] = cluster[near : near + 1]
        ref[base + 1 : base + 2, :] = cluster[next_one : next_one + 1]
        ref[base + 2 : base + 3, :] = strength_ref[near : near + 1, :]
        ref[base + 3 : base + 4, :] = jnp.zeros((1, lanes), F32)

    inside, outer = first_columns(dims, kernel_ref, innov_ref, strength_ref, lhs, last - 1)
    put(
        east_ref,
        (outer, inside, column(wx_ref, last), column(wy_ref, last), column(wx_ref, last - 1)),
        last,
        last - 1,
    )
    outer, inside = first_columns(dims, kernel_ref, innov_ref, strength_ref, lhs, 0)
    put(west_ref, (outer, inside, column(wx_ref, 0), column(wy_ref, 0)), 0, 1)


def first_mix_kernel(dims, kernel_ref, innov_ref, strength_ref, lhs_ref, out_ref):
    lhs = lhs_ref[...]
    for x in range(0, dims[1], 2):
        for k, value in enumerate(first_columns(dims, kernel_ref, innov_ref, strength_ref, lhs, x)):
            out_ref[x + k, :, :] = value


def rim_kernel(dims, subs, own_ref, south_ref, north_ref, lhs_ref, rim_ref):
    lev, width_x, lanes = dims
    pad = round_up(lev, 8)
    half = 4 * width_x
    cross = lax.axis_index("sub")
    lane = lane_of((1, lanes))
    lower = lane < half
    southern = lane % 4 < 2
    present = jnp.where(southern, cross, subs - 1 - cross) > 0

    def halo(rows):
        value = jnp.where(southern, south_ref[rows, :], north_ref[rows, :])
        return jnp.where(present, value, 0.0)

    own = own_ref[0:pad, :]
    far = halo(slice(0, pad))
    far_misc = halo(slice(2 * pad, 2 * pad + 8))
    own_misc = own_ref[2 * pad : 2 * pad + 8, :]
    sources = [
        jnp.where(lower, own, 0.0) * own_misc[0:1],
        jnp.where(lower, far, 0.0) * far_misc[0:1],
    ]
    lifted = [sources[0] * own_misc[2:3], sources[1] * far_misc[2:3]]
    moved = mix(lhs_ref[...], jnp.concatenate(lifted, axis=1))
    rim_c = sources[0] + moved[:, :lanes]
    far_c = sources[1] + moved[:, lanes:]
    own_wy = jnp.where(lower, turn(own, half), 0.0)
    far_wy = jnp.where(lower, turn(far, half), 0.0)
    far_wx = halo(slice(pad, 2 * pad))
    for at, value in enumerate((rim_c, far_c, own_wy, far_wy, far_wx, own_ref[pad : 2 * pad, :])):
        rim_ref[at * pad : (at + 1) * pad, :] = value
    base = RIM_TILES * pad
    rim_ref[base : base + 1, :] = own_misc[1:2]
    rim_ref[base + 1 : base + 3, :] = far_misc[1:3]
    rim_ref[base + 3 : base + 4, :] = own_misc[2:3]
    rim_ref[base + 4 : base + 8, :] = jnp.zeros((4, lanes), F32)


def rates_of(wx, wx_west, wy, wy_south):
    east = jnp.maximum(wx, 0.0)
    west = jnp.maximum(-wx_west, 0.0)
    north = jnp.maximum(wy, 0.0)
    south = jnp.maximum(-wy_south, 0.0)
    return (1.0 - east) - west - (north + south), east, west, north, south


def from_north(value, halo):
    lanes = value.shape[1]
    return jnp.where(lane_of((1, lanes)) == lanes - 1, halo, turn(value, -1))


def from_south(value, halo):
    return jnp.where(lane_of((1, value.shape[1])) == 0, halo, turn(value, 1))


def crossed(far):
    place = lane_of((1, far.shape[1])) % 4
    return jnp.where(place == 1, turn(far, -1), turn(far, 1))


def halo_of(far, x):
    return turn(far, -4 * x - 2)


def parted(terms, clusters, ids):
    return [total([jnp.where(c == wanted, t, 0.0) for t, c in zip(terms, clusters)]) for wanted in ids]


def convect(lhs, fields, strength):
    lanes = strength.shape[1]
    moved = mix(lhs, jnp.concatenate([strength * f for f in fields], axis=1))
    return [f + moved[:, k * lanes : (k + 1) * lanes] for k, f in enumerate(fields)]


def advance(dims, ids, lhs, x, at, rim):
    lev, _, lanes = dims
    pad = round_up(lev, 8)
    own_cluster = at.cluster(x)
    rim_row = halo_of(rim.cluster, x)
    clusters = (
        own_cluster,
        at.cluster(x + 1),
        at.cluster(x - 1),
        from_north(own_cluster, rim_row),
        from_south(own_cluster, rim_row),
    )
    clusters = [jnp.broadcast_to(c, (8, lanes)) for c in clusters]
    groups = []
    for r in range(pad // 8):
        wy, own = at.wy(x, r), at.c(x, r)
        south_wy = from_south(wy, halo_of(rim.wy(r), x))
        center, east, west, north, south = rates_of(at.wx(x, r), at.wx(x - 1, r), wy, south_wy)
        halo = halo_of(rim.c(r), x)
        terms = (
            center * own,
            east * at.c(x + 1, r),
            west * at.c(x - 1, r),
            north * from_north(own, halo),
            south * from_south(own, halo),
        )
        groups.append(parted(terms, clusters, ids))
    fields = [jnp.concatenate([group[a] for group in groups], axis=0) for a in range(len(ids))]
    return convect(lhs, fields, at.strength(x))


class Columns:
    def __init__(self, dims, c_ref, wx_ref, wy_ref, cluster_ref, strength_ref, before_ref=None, after_ref=None):
        self.lev, self.width_x, self.lanes = dims
        self.c_ref, self.wx_ref, self.wy_ref = c_ref, wx_ref, wy_ref
        self.cluster_rows = cluster_ref[...].astype(F32)
        self.strength_ref = strength_ref
        self.before_ref, self.after_ref = before_ref, after_ref

    def sent(self, ref, tile, r):
        first = tile * self.lev + 8 * r
        return ref[first : first + 8, :]

    def strided(self, ref, x, r):
        return ref[pl.ds(8 * r * self.width_x + x, 8, stride=self.width_x), :]

    def c(self, x, r):
        if x < 0:
            return self.sent(self.before_ref, -1 - x, r)
        if x >= self.width_x:
            return self.sent(self.after_ref, x - self.width_x, r)
        return self.c_ref[x, 8 * r : 8 * r + 8, :]

    def wx(self, x, r):
        if x < 0:
            return self.sent(self.before_ref, 2 if x == -1 else 4, r)
        return self.sent(self.after_ref, 2, r) if x >= self.width_x else self.strided(self.wx_ref, x, r)

    def wy(self, x, r):
        if x < 0:
            return self.sent(self.before_ref, 3, r)
        return self.sent(self.after_ref, 3, r) if x >= self.width_x else self.strided(self.wy_ref, x, r)

    def misc(self, ref, tiles, row):
        return ref[tiles * self.lev + row : tiles * self.lev + row + 1, :]

    def cluster(self, x):
        if x < 0:
            return self.misc(self.before_ref, 5, -1 - x)
        if x >= self.width_x:
            return self.misc(self.after_ref, 4, x - self.width_x)
        return self.cluster_rows[x : x + 1]

    def strength(self, x):
        if x < 0:
            return self.misc(self.before_ref, 5, 2)
        if x >= self.width_x:
            return self.misc(self.after_ref, 4, 2)
        return self.strength_ref[x : x + 1, :]


class Rim:
    def __init__(self, c, wy, cluster):
        self.c_tile, self.wy_tile, self.cluster = crossed(c), crossed(wy), crossed(cluster)

    def c(self, r):
        return self.c_tile[8 * r : 8 * r + 8]

    def wy(self, r):
        return self.wy_tile[8 * r : 8 * r + 8]


def adjoint_ids(per_device):
    first = (lax.axis_index("adj") * per_device).astype(F32)
    return [first + a for a in range(per_device)]


def inner_kernel(
    dims, per_device, rim_ref, c_ref, wx_ref, wy_ref, cluster_ref, strength_ref, lhs_ref, mixed_ref, ground_ref
):
    lev, width_x, _ = dims
    pad = round_up(lev, 8)
    at = Columns(dims, c_ref, wx_ref, wy_ref, cluster_ref, strength_ref)
    base = RIM_TILES * pad
    rim = Rim(rim_ref[pad : 2 * pad, :], rim_ref[3 * pad : 4 * pad, :], rim_ref[base + 1 : base + 2, :])
    ids = adjoint_ids(per_device)
    lhs = lhs_ref[...]
    for x in range(1, width_x - 1):
        for a, value in enumerate(advance(dims, ids, lhs, x, at, rim)):
            mixed_ref[a, x - 1, :, :] = value
            ground_ref[a, x + 1 : x + 2, :] = value[0:1]


def mixed_at(dims, inner_ref, ends_ref, a, x, r):
    width_x = dims[1]
    rows = slice(8 * r, 8 * r + 8)
    if 1 <= x < width_x - 1:
        return inner_ref[a, x - 1, rows, :]
    return ends_ref[a, x + 1 if x < 1 else x - width_x + 3, rows, :]


def second_transport(dims, at, rim_wy, far, inner_ref, ends_ref, ids, x, r):
    half = 4 * dims[1]
    wy = at.wy(x, r)
    south_wy = from_south(wy, halo_of(rim_wy, x))
    center, east, west, north, south = rates_of(at.wx(x, r), at.wx(x - 1, r), wy, south_wy)
    values = []
    for a in range(len(ids)):
        own = mixed_at(dims, inner_ref, ends_ref, a, x, r)
        halo = turn(far(a // 2, r), -4 * x - 2 - half * (a % 2))
        parts = [
            center * own,
            east * mixed_at(dims, inner_ref, ends_ref, a, x + 1, r),
            west * mixed_at(dims, inner_ref, ends_ref, a, x - 1, r),
            north * from_north(own, halo),
            south * from_south(own, halo),
        ]
        values.append(total(parts))
    return values


def ends_kernel(dims, subs, per_device, *refs):
    lev, width_x, lanes = dims
    rim_ref, before_ref, after_ref, inner_ground_ref, c_ref, wx_ref, wy_ref, cluster_ref, strength_ref, lhs_ref = refs[:10]
    ends_ref, far_ref, surface_ref, full_ref, ground_ref, west_ref, beside_ref = refs[10:]
    pad = round_up(lev, 8)
    half = 4 * width_x
    cross = lax.axis_index("sub")
    lane = lane_of((1, lanes))
    place = lane % 4
    after_slot = lane // 4 == width_x
    before_slot = lane >= lanes - 4
    at = Columns(dims, c_ref, wx_ref, wy_ref, cluster_ref, strength_ref, before_ref, after_ref)
    ids = adjoint_ids(per_device)
    lhs = lhs_ref[...]

    base = RIM_TILES * pad
    rim_c, far_c, rim_wy, far_wy, far_wx, rim_wx = (rim_ref[i * pad : (i + 1) * pad, :] for i in range(RIM_TILES))
    rim_cluster = rim_ref[base : base + 1, :]
    far_cluster = rim_ref[base + 1 : base + 2, :]
    far_strength = rim_ref[base + 2 : base + 3, :]
    rim = Rim(far_c, far_wy, far_cluster)

    def sent(ref, tile):
        return jnp.concatenate([at.sent(ref, tile, r) for r in range(pad // 8)], axis=0)

    def full(value, before, after):
        return jnp.where(before_slot, turn(before, -2), jnp.where(after_slot, turn(after, half + 2), value))

    full_c = full(rim_c, sent(before_ref, 0), sent(after_ref, 0))
    full_wy = full(rim_wy, sent(before_ref, 3), sent(after_ref, 3))
    full_wx = full(rim_wx, sent(before_ref, 2), rim_wx)
    for i, value in enumerate((full_c, full_wy, full_wx)):
        full_ref[i * pad : (i + 1) * pad, :] = value
    rows = [
        full(rim_cluster, at.cluster(-1), at.cluster(width_x)),
        full(rim_ref[base + 3 : base + 4, :], at.strength(-1), at.strength(width_x)),
    ]
    full_ref[3 * pad : 3 * pad + 2, :] = jnp.concatenate(rows, axis=0)
    full_ref[3 * pad + 2 : 3 * pad + 8, :] = jnp.zeros((6, lanes), F32)
    picked = jnp.where(before_slot | after_slot, full_c, 0.0)
    wy_slot = (lane < 4) | (lane // 4 == width_x + 1)
    wx_slot = lane // 4 == 1
    moved_wy = full(jnp.zeros_like(rim_wy), turn(sent(before_ref, 3), 0), turn(sent(after_ref, 3), 0))
    picked = jnp.where(wy_slot, turn(moved_wy, 4), picked)
    picked = jnp.where(wx_slot, turn(sent(before_ref, 2), 6), picked).T
    picked = jnp.concatenate([picked, jnp.zeros((lanes, lanes - pad), F32)], axis=1)
    packet = picked[half : half + 8] + turn(picked[lanes - 8 : lanes], pad) + turn(picked[0:8], 2 * pad)
    tail = per_device * width_x
    surface_ref[tail : tail + 8, :] = packet
    surface_ref[tail + 8 : tail + 10, :] = jnp.concatenate(rows, axis=0)
    surface_ref[tail + 10 : tail + 16, :] = jnp.zeros((6, lanes), F32)
    for k, x in ((1, 0), (2, width_x - 1), (0, -1), (3, width_x)):
        for a, value in enumerate(advance(dims, ids, lhs, x, at, rim)):
            ends_ref[a, k, :, :] = value
            ground_ref[a, x + 1 : x + 2, :] = value[0:1]

    def rim_north(far, own):
        return turn(jnp.where(place == 2, own, far), -1)

    def rim_south(far, own):
        return turn(jnp.where(place == 1, own, far), 1)

    center, east, west, north, south = rates_of(far_wx, turn(far_wx, 4), far_wy, rim_south(far_wy, rim_wy))
    terms = (
        center * far_c,
        east * turn(far_c, -4),
        west * turn(far_c, 4),
        north * rim_north(far_c, rim_c),
        south * rim_south(far_c, rim_c),
    )
    clusters = (
        far_cluster,
        turn(far_cluster, -4),
        turn(far_cluster, 4),
        rim_north(far_cluster, rim_cluster),
        rim_south(far_cluster, rim_cluster),
    )
    inside = jnp.where(lane < half, jnp.where(place < 2, cross, subs - 1 - cross), 0) > 0
    fields = [jnp.where(inside, f, 0.0) for f in parted(terms, clusters, ids)]
    joined = [fields[a] + turn(fields[a + 1], half) for a in range(0, per_device, 2)]
    far_mixed = [crossed(f) for f in convect(lhs, joined, far_strength + turn(far_strength, half))]
    for at_pair, value in enumerate(far_mixed):
        far_ref[at_pair, 0:pad, :] = value
    far_ref[0, pad : pad + 8, :] = jnp.zeros((8, lanes), F32)
    for pair in range(1, len(far_mixed)):
        far_ref[pair, pad : pad + 8, :] = jnp.zeros((8, lanes), F32)

    rows = [rim.wy_tile[0:1]] + [turn(far_mixed[a // 2][0:1], half * (a % 2)) for a in range(per_device)]
    tall = round_up(len(rows), 8)
    stack = jnp.concatenate(rows + [jnp.zeros((tall - len(rows), lanes), F32)], axis=0)
    for x in range(width_x):
        beside_ref[x * tall : (x + 1) * tall, :] = halo_of(stack, x)

    def beside(at_row):
        return beside_ref[pl.ds(at_row, width_x, stride=tall), :]

    west_ref[0:1, :] = at.sent(before_ref, 2, 0)[0:1]
    west_ref[1 : width_x + 1, :] = wx_ref[0:width_x, :]
    wx, wy = wx_ref[0:width_x, :], wy_ref[0:width_x, :]
    south_wy = from_south(wy, beside(0))
    center, east, west, north, south = rates_of(wx, west_ref[0:width_x, :], wy, south_wy)
    for a in range(per_device):
        ground_ref[a, 2:width_x, :] = inner_ground_ref[a, 2:width_x, :]
        own = ground_ref[a, 1 : width_x + 1, :]
        rim_rows = beside(1 + a)
        parts = [
            center * own,
            east * ground_ref[a, 2 : width_x + 2, :],
            west * ground_ref[a, 0:width_x, :],
            north * from_north(own, rim_rows),
            south * from_south(own, rim_rows),
        ]
        surface_ref[a * width_x : (a + 1) * width_x, :] = total(parts)


def output_kernel(dims, per_device, *refs):
    lev, width_x, _ = dims
    rim_ref, before_ref, inner_ref, ends_ref, far_ref, wx_ref, wy_ref, cluster_ref, strength_ref = refs[:9]
    out_ref, token_ref, edge_ref, field_ref, sem = refs[9:]
    token_ref[...] = jnp.zeros(token_ref.shape, F32)
    pad = round_up(lev, 8)
    at = Columns(dims, None, wx_ref, wy_ref, cluster_ref, strength_ref, before_ref)
    ids = range(per_device)

    def far(pair, r):
        return far_ref[pair, 8 * r : 8 * r + 8, :]

    rim_wys = [crossed(rim_ref[3 * pad + 8 * r : 3 * pad + 8 * r + 8, :]) for r in range(pad // 8)]
    copies = []
    for x in range(width_x):
        for r in range(pad // 8):
            rim_wy = rim_wys[r]
            values = second_transport(dims, at, rim_wy, far, inner_ref, ends_ref, ids, x, r)
            for a, value in enumerate(values):
                if x in (0, width_x - 1):
                    edge_ref[a, min(x, 1), 8 * r : 8 * r + 8, :] = value
                else:
                    field_ref[a, x, 8 * r : 8 * r + 8, :] = value
        for a in range(per_device if 0 < x < width_x - 1 else 0):
            source = field_ref.at[a, x, pl.ds(0, lev), :]
            copies.append(pltpu.make_async_copy(source, out_ref.at[a, :, x, 0, :], sem.at[len(copies)]))
            copies[-1].start()
    for copy in copies:
        copy.wait()


def quotient(value, count):
    if count & (count - 1) == 0:
        return value >> (count.bit_length() - 1), value & (count - 1)
    return lax.div(value, count), lax.rem(value, count)


def tables_kernel(dims, tiles, subs, n_rim, cell_ref, weight_ref, hot_ref, share_ref):
    _, width_x, width_y = dims
    slots, elements = cell_ref.shape
    tile_pos = lax.axis_index("tiles")
    cross = lax.axis_index("sub")
    column_x, row_y = quotient(cell_ref[...], width_y * subs)
    block_x, inner_x = quotient(column_x, width_x)
    block_y, lane_y = quotient(row_y, width_y)
    step = block_x - tile_pos
    step = jnp.where(step < -1, step + tiles, jnp.where(step > 1, step - tiles, step))
    if n_rim == 2:
        side = jnp.where(block_y == cross, 0, 1)
    else:
        side = block_y - cross + 1
    at_y = side * width_y + lane_y
    at_x = (step + 1) * width_x + inner_x
    weight = weight_ref[...]
    group = width_y
    rows = lax.broadcasted_iota(jnp.int32, (16, group), 0)
    for g in range(0, elements, group):
        lanes = slice(g, g + group)
        for k in range(slots):
            y = jnp.broadcast_to(at_y[k : k + 1, lanes], (16, group)) - rows
            for first in range(0, n_rim * width_y, 16):
                hot_ref[k, first : first + 16, lanes] = jnp.where(y == first, 1.0, 0.0).astype(BF16)
            x = jnp.broadcast_to(at_x[k : k + 1, lanes], (16, group)) - rows
            w = jnp.broadcast_to(weight[k : k + 1, lanes], (16, group))
            for first in range(0, 3 * width_x, 16):
                share_ref[k, first : first + 16, lanes] = jnp.where(x == first, w, 0.0)


def looked_up(dims, per_device, blocks, hot_ref, share_ref, lanes):
    width_x = dims[1]
    rows = per_device * width_x
    surfaces = [split(jnp.concatenate(places, axis=1)) for _, places in blocks]
    lhs = jnp.concatenate([part for pair in surfaces for part in pair], axis=0)
    sums = [None] * per_device
    for k in range(hot_ref.shape[0]):
        found = jnp.dot(lhs, hot_ref[k, :, lanes], preferred_element_type=F32)
        for at, (step, _) in enumerate(blocks):
            share = share_ref[k, (step + 1) * width_x : (step + 2) * width_x, lanes]
            for a in range(per_device):
                high = 2 * at * rows + a * width_x
                low = high + rows
                value = (found[high : high + width_x] + found[low : low + width_x]) * share
                sums[a] = value if sums[a] is None else sums[a] + value
    return jnp.concatenate([jnp.sum(s, axis=0, keepdims=True) for s in sums], axis=0)


def wide_lanes(elements):
    wide = 256 if elements % 256 == 0 else 128
    return [slice(g, g + wide) for g in range(0, elements, wide)]


def sense_part_kernel(dims, per_device, n_rim, step, hot_ref, share_ref, block_ref, *refs):
    *found, out_ref = refs
    rows = per_device * dims[1]
    blocks = [(step, [block_ref[k * rows : (k + 1) * rows, :] for k in range(n_rim)])]
    for lanes in wide_lanes(out_ref.shape[1]):
        value = looked_up(dims, per_device, blocks, hot_ref, share_ref, lanes)
        out_ref[:, lanes] = total([ref[:, lanes] for ref in found] + [value])


def sense_last_kernel(*refs):
    *inputs, out_ref, own_ref, sem = refs
    sense_part_kernel(*inputs, own_ref)
    copy = pltpu.make_async_copy(own_ref, out_ref, sem)
    copy.start()
    copy.wait()


class Seam:
    def __init__(self, dims, c, wy, wx, cluster, strength):
        _, self.width_x, lanes = dims
        self.lane = lane_of((1, lanes))
        self.place = self.lane % 4
        slot = self.lane // 4
        self.first, self.last = slot == 0, slot == self.width_x - 1
        self.beside = (slot == lanes // 4 - 1) | (slot == self.width_x)
        self.c, self.cluster, self.strength = c, cluster, strength
        self.east = jnp.maximum(wx, 0.0)
        self.west = jnp.maximum(-turn(wx, 4), 0.0)
        self.north = jnp.maximum(wy, 0.0)
        self.south = jnp.maximum(-turn(wy, 1), 0.0)

    def missing(self, lhs, ids):
        near = (self.place == 1) | (self.place == 2)
        wanted_slots = near & (self.beside | self.first | self.last)
        moved = [(turn(self.c, k), turn(self.cluster, k)) for k in (-1, 1, 4, -4)]
        fields = []
        for wanted in ids:
            own = jnp.where(self.cluster == wanted, self.c, 0.0)
            from_n, from_s, from_w, from_e = (jnp.where(row == wanted, c, 0.0) for c, row in moved)
            upright = jnp.where(self.place == 1, self.north * from_n, self.south * (from_s - own))
            level = jnp.where(self.first, self.west * (from_w - own), self.east * from_e)
            fields.append(jnp.where(wanted_slots, jnp.where(self.beside, upright, level), 0.0))
        return convect(lhs, fields, self.strength)


def seam_transport(rates, missing):
    east, west, north, south = rates
    lane = lane_of((1, missing.shape[1]))
    place, slot = lane % 4, lane // 4
    level = jnp.where(slot == 0, west * turn(missing, 4), east * turn(missing, -4))
    return level + jnp.where(place == 1, north * turn(missing, -1), south * turn(missing, 1))


def own_places(subs):
    cross = lax.axis_index("sub")
    if subs == 2:
        own_south = (cross == 0).astype(jnp.int32)
        return [own_south]
    return [jnp.int32(0), jnp.int32(1)]


def patch_kernel(dims, subs, per_device, *refs):
    lev, width_x, lanes = dims
    rim_ref, full_ref, own_ref, south_ref, north_ref, lhs_ref, _, whole_ref, seam_ref = refs
    pad = round_up(lev, 8)
    half = 4 * width_x
    rows = per_device * width_x
    lane = lane_of((1, lanes))
    southern = lane % 4 < 2
    before_slot = lane >= lanes - 4
    after_slot = lane // 4 == width_x
    ids = adjoint_ids(per_device)
    lhs = lhs_ref[...]
    cross = lax.axis_index("sub")
    present = jnp.where(southern, cross, subs - 1 - cross) > 0

    def upright(ref):
        turned = ref[rows : rows + 8, :].T
        turned = jnp.concatenate([turned, jnp.zeros((lanes, lanes - 8), F32)], axis=1)
        return [turned[i * pad : (i + 1) * pad] for i in range(3)]

    def beyond(value, south, north, before, after):
        def placed(tile):
            moved = turn(tile[0], lanes - 4 - before)
            return moved if after is None else jnp.where(after_slot, turn(tile[1], half - after), moved)

        moved = placed(south) if south is north else jnp.where(southern, placed(south), placed(north))
        moved = jnp.where(present, moved, 0.0)
        slots = before_slot if after is None else before_slot | after_slot
        return jnp.where(slots, moved, value)

    south = upright(south_ref)
    north = south if subs == 2 else upright(north_ref)

    def pair(first, second):
        one = (south[first], south[second])
        return one, one if subs == 2 else (north[first], north[second])

    far_c, far_wy, far_wx = (rim_ref[i * pad : (i + 1) * pad, :] for i in (1, 3, 4))
    c_pair, wy_pair = pair(1, 0), pair(2, 0)
    if subs == 2:
        c_pair, wy_pair = (c_pair[0], c_pair[0]), (wy_pair[0], wy_pair[0])
    far_c = beyond(far_c, *c_pair, 4, 0)
    far_wx = beyond(far_wx, *wy_pair, 4, None)
    far_wy = beyond(far_wy, *wy_pair, 0, 4)
    base = RIM_TILES * pad

    def beyond_row(value, at_row):
        south_row = south_ref[rows + at_row : rows + at_row + 1, :]
        north_row = north_ref[rows + at_row : rows + at_row + 1, :]
        moved = jnp.where(present, jnp.where(southern, south_row, north_row), 0.0)
        return jnp.where(before_slot | after_slot, moved, value)

    far_cluster = beyond_row(rim_ref[base + 1 : base + 2, :], 8)
    far_strength = beyond_row(rim_ref[base + 2 : base + 3, :], 9)
    full_c, full_wy, full_wx = (full_ref[i * pad : (i + 1) * pad, :] for i in range(3))
    full_cluster = full_ref[3 * pad : 3 * pad + 1, :]
    full_strength = full_ref[3 * pad + 1 : 3 * pad + 2, :]
    surfaces = [own_ref, south_ref] if subs == 2 else [south_ref, own_ref, north_ref]
    for k, ref in enumerate(surfaces):
        whole_ref[k * rows : (k + 1) * rows, :] = ref[0:rows, :]
    for k, own_south in enumerate(own_places(subs)):
        mine = jnp.where(southern, own_south, 1 - own_south) > 0
        seam = Seam(
            dims,
            jnp.where(mine, full_c, far_c),
            jnp.where(mine, full_wy, far_wy),
            jnp.where(mine, full_wx, far_wx),
            jnp.where(mine, full_cluster, far_cluster),
            jnp.where(mine, full_strength, far_strength),
        )
        missing = seam.missing(lhs, ids)
        rates = (seam.east, seam.west, seam.north, seam.south)
        for i, value in enumerate(rates + tuple(missing)):
            seam_ref[k, i * pad : (i + 1) * pad, :] = value
        far_at = 1 if subs == 2 else 2 * k
        own_at = 0 if subs == 2 else 1
        own_lane = jnp.where(own_south > 0, lanes - 1, 0)
        for a, value in enumerate(missing):
            change = seam_transport([rate[0:8] for rate in rates], value[0:8])[0:1]
            for x in (0, width_x - 1):
                row = turn(change, -4 * x - 2)
                for block, at_lane in ((own_at, own_lane), (far_at, lanes - 1 - own_lane)):
                    at = block * rows + a * width_x + x
                    whole_ref[at : at + 1, :] = whole_ref[at : at + 1, :] + jnp.where(lane == at_lane, row, 0.0)


def output_ends_kernel(dims, subs, per_device, _, seam_ref, edge_ref, out_ref, done_ref, sem):
    lev, width_x, lanes = dims
    pad = round_up(lev, 8)
    lane = lane_of((1, lanes))
    copies = []
    for a in range(per_device):
        columns = [edge_ref[a, 0], edge_ref[a, 1]]
        for k, own_south in enumerate(own_places(subs)):
            rates = [seam_ref[k, i * pad : (i + 1) * pad, :] for i in range(4)]
            change = seam_transport(rates, seam_ref[k, (4 + a) * pad : (5 + a) * pad, :])
            own = lane == jnp.where(own_south > 0, lanes - 1, 0)
            for i, x in enumerate((0, width_x - 1)):
                columns[i] = columns[i] + jnp.where(own, turn(change, -4 * x - 2), 0.0)
        for i, x in enumerate((0, width_x - 1)):
            done_ref[a, i, :, :] = columns[i]
            source = done_ref.at[a, i, pl.ds(0, lev), :]
            copies.append(pltpu.make_async_copy(source, out_ref.at[a, :, x, 0, :], sem.at[len(copies)]))
            copies[-1].start()
    for copy in copies:
        copy.wait()


def ring(value, axis, steps):
    count = lax.axis_size(axis)
    return lax.ppermute(value, axis, [(i, (i + steps) % count) for i in range(count)])


def across(value):
    count = lax.axis_size("sub")
    if count == 2:
        other = ring(value, "sub", 1)
        return other, other
    from_south = lax.ppermute(value, "sub", [(i, i + 1) for i in range(count - 1)])
    from_north = lax.ppermute(value, "sub", [(i + 1, i) for i in range(count - 1)])
    return from_south, from_north


def body(
    innovation,
    cluster,
    kernel,
    wind_x,
    wind_y,
    conv_strength,
    conv_matrix,
    margin_cell,
    margin_weight,
):
    dims = kernel.shape
    lev, width_x, width_y = dims
    tiles = lax.axis_size("tiles")
    subs = lax.axis_size("sub")
    per_device = ADJ // lax.axis_size("adj")
    pad = round_up(lev, 8)
    deep = round_up(lev, 16)
    flat = (lev * width_x, width_y)
    tall = (pad * width_x, width_y)
    small = innovation.shape
    sources = (
        kernel.reshape(flat),
        wind_x.reshape(flat),
        wind_y.reshape(flat),
        innovation,
        cluster,
        conv_strength,
        conv_matrix,
        margin_cell.T,
        margin_weight.T,
    )
    outs = [tall, tall, tall, small, (small, jnp.int32), small, conv_matrix.shape]
    outs += [(sources[7].shape, jnp.int32), sources[8].shape, ((pad, 3 * deep), BF16), (2 * pad + 8, width_y)]
    fetched = call(
        functools.partial(fetch_kernel, dims),
        outs,
        sources,
        scratch=(pltpu.SemaphoreType.DMA((len(sources),)),),
        far_in=True,
    )
    air, wx, wy, innov, group, strength, _, cell, weight, lhs, own_rim = fetched
    south_rim, north_rim = across(own_rim)
    to_east, to_west = call(
        functools.partial(first_ends_kernel, dims),
        [(5 * lev + 4, width_y), (4 * lev + 4, width_y)],
        (air, innov, strength, lhs, wx, wy, group),
    )
    before = ring(to_east, "tiles", 1)
    after = ring(to_west, "tiles", -1)
    (first,) = call(
        functools.partial(first_mix_kernel, dims), [(width_x, pad, width_y)], (air, innov, strength, lhs), cost=400000
    )
    (rim,) = call(
        functools.partial(rim_kernel, dims, subs),
        [(RIM_TILES * pad + 8, width_y)],
        (own_rim, south_rim, north_rim, lhs),
        cost=400000,
    )
    inner, ground = call(
        functools.partial(inner_kernel, dims, per_device),
        [(per_device, width_x - 2, pad, width_y), (per_device, width_x + 8, width_y)],
        (rim, first, wx, wy, group, strength, lhs),
        cost=4000000,
    )
    ends, far, surface, full = call(
        functools.partial(ends_kernel, dims, subs, per_device),
        [
            (per_device, 4, pad, width_y),
            ((per_device + 1) // 2, pad + 8, width_y),
            (per_device * width_x + 16, width_y),
            (3 * pad + 8, width_y),
        ],
        (rim, before, after, ground, first, wx, wy, group, strength, lhs),
        scratch=(
            pltpu.VMEM((per_device, width_x + 8, width_y), F32),
            pltpu.VMEM((width_x + 8, width_y), F32),
            pltpu.VMEM((width_x * round_up(per_device + 1, 8), width_y), F32),
        ),
    )
    south_surface, north_surface = across(surface)
    field, token, edge = call(
        functools.partial(output_kernel, dims, per_device),
        [(per_device, lev, width_x, 1, width_y), (8, width_y), (per_device, 2, pad, width_y)],
        (rim, before, inner, ends, far, wx, wy, group, strength),
        scratch=(
            pltpu.VMEM((per_device, width_x, pad, width_y), F32),
            pltpu.SemaphoreType.DMA((per_device * width_x,)),
        ),
        far_out=(0,),
        cost=4000000,
    )
    n_rim = min(subs, 3)
    rows = per_device * width_x
    seams = 1 if subs == 2 else 2
    whole, seam = call(
        functools.partial(patch_kernel, dims, subs, per_device),
        [(n_rim * rows, width_y), (seams, (4 + per_device) * pad, width_y)],
        (rim, full, surface, south_surface, north_surface, lhs, token),
    )
    if subs > 2:
        own = whole[rows : 2 * rows]
        south_surface, north_surface = across(own)
        whole = jnp.concatenate([south_surface, own, north_surface], axis=0)
    surface_before = ring(whole, "tiles", 1)
    surface_after = ring(whole, "tiles", -1)
    near, hbm = pl.BlockSpec(memory_space=pltpu.VMEM), pl.BlockSpec(memory_space=pl.ANY)
    field = pl.pallas_call(
        functools.partial(output_ends_kernel, dims, subs, per_device),
        out_shape=jax.ShapeDtypeStruct(field.shape, F32),
        in_specs=[hbm, near, near],
        out_specs=hbm,
        scratch_shapes=[pltpu.VMEM((per_device, 2, pad, width_y), F32), pltpu.SemaphoreType.DMA((2 * per_device,))],
        input_output_aliases={0: 0},
        compiler_params=pltpu.CompilerParams(vmem_limit_bytes=VMEM_BYTES),
        cost_estimate=pl.CostEstimate(flops=1000000, bytes_accessed=1000000, transcendentals=0),
        name="output_ends",
    )(field, *[pltpu.with_memory_space_constraint(v, pltpu.VMEM) for v in (seam, edge)])
    slots, elements = cell.shape
    hot, share = call(
        functools.partial(tables_kernel, dims, tiles, subs, n_rim),
        [((slots, n_rim * width_y, elements), BF16), (slots, 3 * width_x, elements)],
        (cell, weight),
        cost=2000000,
    )
    part = functools.partial(sense_part_kernel, dims, per_device, n_rim)
    found = [(per_device, elements)]
    (sensed,) = call(functools.partial(part, 0), found, (hot, share, whole), cost=2000000)
    (sensed,) = call(functools.partial(part, 1), found, (hot, share, surface_after, sensed), cost=2000000)
    (sensed,) = call(
        functools.partial(sense_last_kernel, dims, per_device, n_rim, -1),
        found,
        (hot, share, surface_before, sensed),
        scratch=(pltpu.VMEM((per_device, elements), F32), pltpu.SemaphoreType.DMA),
        far_out=(0,),
    )
    return (field.reshape(per_device, lev, width_x, width_y), sensed)


def solution(mesh):
    in_specs = (
        P(("groups", "tiles"), "sub"),
        P(("groups", "tiles"), "sub"),
        P(None, "tiles", "sub"),
        P(None, "tiles", "sub"),
        P(None, "tiles", "sub"),
        P("tiles", "sub"),
        P(),
        P(("tiles", "sub"), None),
        P(("tiles", "sub"), None),
    )
    out_specs = (P(("groups", "adj"), None, "tiles", "sub"), P(("groups", "adj"), ("tiles", "sub")))
    return jax.shard_map(body, mesh=mesh, in_specs=in_specs, out_specs=out_specs, check_vma=False)
```

```python
import functools

import jax
import jax.numpy as jnp
from jax import lax
from jax.experimental import pallas as pl
from jax.experimental.pallas import tpu as pltpu
from jax.sharding import PartitionSpec as P


ADJ = 8
F32 = jnp.float32
BF16 = jnp.bfloat16
VMEM_BYTES = 16 << 20
RIM_TILES = 6


def call(kernel, outs, args, scratch=(), far_in=False, far_out=(), cost=0):
    near = pl.BlockSpec(memory_space=pltpu.VMEM)
    far = pl.BlockSpec(memory_space=pl.ANY)
    outs = [out for out in outs]
    shapes = [(out, F32) if isinstance(out[-1], int) else out for out in outs]
    return pl.pallas_call(
        kernel,
        out_shape=[(jax.ShapeDtypeStruct if at in far_out else pltpu.VMEM)(*out) for at, out in enumerate(shapes)],
        in_specs=[far if far_in else near] * len(args),
        out_specs=[far if at in far_out else near for at in range(len(outs))],
        scratch_shapes=list(scratch),
        compiler_params=pltpu.CompilerParams(vmem_limit_bytes=VMEM_BYTES),
        cost_estimate=pl.CostEstimate(flops=cost, bytes_accessed=cost, transcendentals=0) if cost else None,
    )(*[pltpu.with_memory_space_constraint(arg, pltpu.HBM if far_in else pltpu.VMEM) for arg in args])


def round_up(count, unit):
    return count + -count % unit


def split(value):
    high = value.astype(BF16)
    return high, (value - high.astype(F32)).astype(BF16)


def mix(lhs, field):
    short = lhs.shape[1] // 3 - field.shape[0]
    if short:
        field = jnp.concatenate([field, jnp.zeros((short, field.shape[1]), F32)], axis=0)
    high, low = split(field)
    return jnp.dot(lhs, jnp.concatenate([high, high, low], axis=0), preferred_element_type=F32)


def lane_of(shape):
    return lax.broadcasted_iota(jnp.int32, shape, len(shape) - 1)


def turn(value, steps):
    steps = steps % value.shape[-1]
    return value if steps == 0 else pltpu.roll(value, steps, value.ndim - 1)


def total(parts):
    while len(parts) > 1:
        parts = [parts[i] + parts[i + 1] if i + 1 < len(parts) else parts[i] for i in range(0, len(parts), 2)]
    return parts[0]


def fetch_kernel(dims, *refs):
    lev, width_x, lanes = dims
    sources, (kernel, wx, wy, innov, cluster, strength, matrix, lhs, rim), scratch = (
        refs[:7],
        refs[7:16],
        refs[16:],
    )
    (sem,) = scratch
    pad = round_up(lev, 8)
    deep = lhs.shape[1] // 3
    half = 4 * width_x
    whole = lev * width_x
    copies = [pltpu.make_async_copy(s, t, sem.at[i]) for i, (s, t) in enumerate(zip(sources[3:], refs[10:14]))]
    targets = [ref.at[pl.ds(0, whole), :] for ref in (kernel, wx, wy)]
    large = [pltpu.make_async_copy(s, t, sem.at[4 + i]) for i, (s, t) in enumerate(zip(sources, targets))]
    for copy in copies + large:
        copy.start()
    for ref in (kernel, wx, wy):
        ref[pl.ds(whole, (pad - lev) * width_x), :] = jnp.zeros(((pad - lev) * width_x, lanes), F32)
    slot = lane_of((1, lanes)) // 4

    def packed(ref, first, r):
        value = jnp.zeros((8, lanes), F32)
        for x in range(width_x):
            moved = turn(ref[pl.ds(8 * r * width_x + x, 8, stride=width_x), :], first + 4 * x + 2)
            value = jnp.where(slot == first // 4 + x, moved, value)
        return value

    def packed_row(value):
        moved = pltpu.roll(value, 2, 1, stride=4, stride_axis=0)
        own = lax.broadcasted_iota(jnp.int32, value.shape, 0) == slot
        return jnp.sum(jnp.where(own, moved, 0.0), axis=0, keepdims=True)

    for copy in copies[:4]:
        copy.wait()
    rim[2 * pad : 2 * pad + 1, :] = packed_row(innov[...])
    rim[2 * pad + 1 : 2 * pad + 2, :] = packed_row(cluster[...].astype(F32))
    rim[2 * pad + 2 : 2 * pad + 3, :] = packed_row(strength[...])
    rim[2 * pad + 3 : 2 * pad + 8, :] = jnp.zeros((5, lanes), F32)
    square = [lax.broadcasted_iota(jnp.int32, (lev, lev), axis) for axis in (0, 1)]
    turned = matrix[...].T - jnp.where(square[0] == square[1], 1.0, 0.0)
    turned = jnp.concatenate([turned, jnp.zeros((pad - lev, lev), F32)], axis=0)
    turned = jnp.concatenate([turned, jnp.zeros((pad, deep - lev), F32)], axis=1)
    high = turned.astype(BF16).astype(F32)
    lhs[...] = jnp.concatenate([high, turned - high, high], axis=1).astype(BF16)
    groups = [slice(8 * r, 8 * r + 8) for r in range(pad // 8)]
    large[0].wait()
    lower = [packed(kernel, 0, r) for r in range(pad // 8)]
    large[2].wait()
    for r, rows in enumerate(groups):
        rim[rows, :] = jnp.where(slot * 4 >= half, packed(wy, half, r), lower[r])
    large[1].wait()
    for r in range(pad // 8):
        rim[pad + 8 * r : pad + 8 * r + 8, :] = packed(wx, 0, r)


def first_columns(dims, kernel_ref, innov_ref, strength_ref, lhs, x):
    lev, width_x, lanes = dims
    pad = round_up(lev, 8)
    tiles = [kernel_ref[pl.ds(at, pad, stride=width_x), :] * innov_ref[at : at + 1, :] for at in (x, x + 1)]
    moved = mix(lhs, jnp.concatenate([strength_ref[x + k : x + k + 1, :] * t for k, t in enumerate(tiles)], axis=1))
    return [t + moved[:, k * lanes : (k + 1) * lanes] for k, t in enumerate(tiles)]


def first_ends_kernel(dims, *refs):
    lev, width_x, lanes = dims
    kernel_ref, innov_ref, strength_ref, lhs_ref, wx_ref, wy_ref, cluster_ref, east_ref, west_ref = refs
    pad = round_up(lev, 8)
    lhs = lhs_ref[...]
    last = width_x - 1
    cluster = cluster_ref[...].astype(F32)

    def column(ref, x):
        return ref[pl.ds(x, pad, stride=width_x), :]

    def put(ref, tiles, near, next_one):
        for at, value in enumerate(tiles):
            top = min(pad, ref.shape[0] - at * lev)
            ref[at * lev : at * lev + top, :] = value[:top]
        base = len(tiles) * lev
        ref[base : base + 1, :] = cluster[near : near + 1]
        ref[base + 1 : base + 2, :] = cluster[next_one : next_one + 1]
        ref[base + 2 : base + 3, :] = strength_ref[near : near + 1, :]
        ref[base + 3 : base + 4, :] = jnp.zeros((1, lanes), F32)

    inside, outer = first_columns(dims, kernel_ref, innov_ref, strength_ref, lhs, last - 1)
    put(
        east_ref,
        (outer, inside, column(wx_ref, last), column(wy_ref, last), column(wx_ref, last - 1)),
        last,
        last - 1,
    )
    outer, inside = first_columns(dims, kernel_ref, innov_ref, strength_ref, lhs, 0)
    put(west_ref, (outer, inside, column(wx_ref, 0), column(wy_ref, 0)), 0, 1)


def first_mix_kernel(dims, kernel_ref, innov_ref, strength_ref, lhs_ref, out_ref):
    lhs = lhs_ref[...]
    for x in range(0, dims[1], 2):
        for k, value in enumerate(first_columns(dims, kernel_ref, innov_ref, strength_ref, lhs, x)):
            out_ref[x + k, :, :] = value


def rim_kernel(dims, subs, own_ref, south_ref, north_ref, lhs_ref, rim_ref):
    lev, width_x, lanes = dims
    pad = round_up(lev, 8)
    half = 4 * width_x
    cross = lax.axis_index("sub")
    lane = lane_of((1, lanes))
    lower = lane < half
    southern = lane % 4 < 2
    present = jnp.where(southern, cross, subs - 1 - cross) > 0

    def halo(rows):
        value = jnp.where(southern, south_ref[rows, :], north_ref[rows, :])
        return jnp.where(present, value, 0.0)

    own = own_ref[0:pad, :]
    far = halo(slice(0, pad))
    far_misc = halo(slice(2 * pad, 2 * pad + 8))
    own_misc = own_ref[2 * pad : 2 * pad + 8, :]
    sources = [
        jnp.where(lower, own, 0.0) * own_misc[0:1],
        jnp.where(lower, far, 0.0) * far_misc[0:1],
    ]
    lifted = [sources[0] * own_misc[2:3], sources[1] * far_misc[2:3]]
    moved = mix(lhs_ref[...], jnp.concatenate(lifted, axis=1))
    rim_c = sources[0] + moved[:, :lanes]
    far_c = sources[1] + moved[:, lanes:]
    own_wy = jnp.where(lower, turn(own, half), 0.0)
    far_wy = jnp.where(lower, turn(far, half), 0.0)
    far_wx = halo(slice(pad, 2 * pad))
    for at, value in enumerate((rim_c, far_c, own_wy, far_wy, far_wx, own_ref[pad : 2 * pad, :])):
        rim_ref[at * pad : (at + 1) * pad, :] = value
    base = RIM_TILES * pad
    rim_ref[base : base + 1, :] = own_misc[1:2]
    rim_ref[base + 1 : base + 3, :] = far_misc[1:3]
    rim_ref[base + 3 : base + 4, :] = own_misc[2:3]
    rim_ref[base + 4 : base + 8, :] = jnp.zeros((4, lanes), F32)


def rates_of(wx, wx_west, wy, wy_south):
    east = jnp.maximum(wx, 0.0)
    west = jnp.maximum(-wx_west, 0.0)
    north = jnp.maximum(wy, 0.0)
    south = jnp.maximum(-wy_south, 0.0)
    return (1.0 - east) - west - (north + south), east, west, north, south


def from_north(value, halo):
    lanes = value.shape[1]
    return jnp.where(lane_of((1, lanes)) == lanes - 1, halo, turn(value, -1))


def from_south(value, halo):
    return jnp.where(lane_of((1, value.shape[1])) == 0, halo, turn(value, 1))


def crossed(far):
    place = lane_of((1, far.shape[1])) % 4
    return jnp.where(place == 1, turn(far, -1), turn(far, 1))


def halo_of(far, x):
    return turn(far, -4 * x - 2)


def parted(terms, clusters, ids):
    return [total([jnp.where(c == wanted, t, 0.0) for t, c in zip(terms, clusters)]) for wanted in ids]


def convect(lhs, fields, strength):
    lanes = strength.shape[1]
    moved = mix(lhs, jnp.concatenate([strength * f for f in fields], axis=1))
    return [f + moved[:, k * lanes : (k + 1) * lanes] for k, f in enumerate(fields)]


def advance(dims, ids, lhs, x, at, rim):
    lev, _, lanes = dims
    pad = round_up(lev, 8)
    own_cluster = at.cluster(x)
    rim_row = halo_of(rim.cluster, x)
    clusters = (
        own_cluster,
        at.cluster(x + 1),
        at.cluster(x - 1),
        from_north(own_cluster, rim_row),
        from_south(own_cluster, rim_row),
    )
    clusters = [jnp.broadcast_to(c, (8, lanes)) for c in clusters]
    groups = []
    for r in range(pad // 8):
        wy, own = at.wy(x, r), at.c(x, r)
        south_wy = from_south(wy, halo_of(rim.wy(r), x))
        center, east, west, north, south = rates_of(at.wx(x, r), at.wx(x - 1, r), wy, south_wy)
        halo = halo_of(rim.c(r), x)
        terms = (
            center * own,
            east * at.c(x + 1, r),
            west * at.c(x - 1, r),
            north * from_north(own, halo),
            south * from_south(own, halo),
        )
        groups.append(parted(terms, clusters, ids))
    fields = [jnp.concatenate([group[a] for group in groups], axis=0) for a in range(len(ids))]
    return convect(lhs, fields, at.strength(x))


class Columns:
    def __init__(self, dims, c_ref, wx_ref, wy_ref, cluster_ref, strength_ref, before_ref=None, after_ref=None):
        self.lev, self.width_x, self.lanes = dims
        self.c_ref, self.wx_ref, self.wy_ref = c_ref, wx_ref, wy_ref
        self.cluster_rows = cluster_ref[...].astype(F32)
        self.strength_ref = strength_ref
        self.before_ref, self.after_ref = before_ref, after_ref

    def sent(self, ref, tile, r):
        first = tile * self.lev + 8 * r
        return ref[first : first + 8, :]

    def strided(self, ref, x, r):
        return ref[pl.ds(8 * r * self.width_x + x, 8, stride=self.width_x), :]

    def c(self, x, r):
        if x < 0:
            return self.sent(self.before_ref, -1 - x, r)
        if x >= self.width_x:
            return self.sent(self.after_ref, x - self.width_x, r)
        return self.c_ref[x, 8 * r : 8 * r + 8, :]

    def wx(self, x, r):
        if x < 0:
            return self.sent(self.before_ref, 2 if x == -1 else 4, r)
        return self.sent(self.after_ref, 2, r) if x >= self.width_x else self.strided(self.wx_ref, x, r)

    def wy(self, x, r):
        if x < 0:
            return self.sent(self.before_ref, 3, r)
        return self.sent(self.after_ref, 3, r) if x >= self.width_x else self.strided(self.wy_ref, x, r)

    def misc(self, ref, tiles, row):
        return ref[tiles * self.lev + row : tiles * self.lev + row + 1, :]

    def cluster(self, x):
        if x < 0:
            return self.misc(self.before_ref, 5, -1 - x)
        if x >= self.width_x:
            return self.misc(self.after_ref, 4, x - self.width_x)
        return self.cluster_rows[x : x + 1]

    def strength(self, x):
        if x < 0:
            return self.misc(self.before_ref, 5, 2)
        if x >= self.width_x:
            return self.misc(self.after_ref, 4, 2)
        return self.strength_ref[x : x + 1, :]


class Rim:
    def __init__(self, c, wy, cluster):
        self.c_tile, self.wy_tile, self.cluster = crossed(c), crossed(wy), crossed(cluster)

    def c(self, r):
        return self.c_tile[8 * r : 8 * r + 8]

    def wy(self, r):
        return self.wy_tile[8 * r : 8 * r + 8]


def adjoint_ids(per_device):
    first = (lax.axis_index("adj") * per_device).astype(F32)
    return [first + a for a in range(per_device)]


def inner_kernel(
    dims, per_device, rim_ref, c_ref, wx_ref, wy_ref, cluster_ref, strength_ref, lhs_ref, mixed_ref, ground_ref
):
    lev, width_x, _ = dims
    pad = round_up(lev, 8)
    at = Columns(dims, c_ref, wx_ref, wy_ref, cluster_ref, strength_ref)
    base = RIM_TILES * pad
    rim = Rim(rim_ref[pad : 2 * pad, :], rim_ref[3 * pad : 4 * pad, :], rim_ref[base + 1 : base + 2, :])
    ids = adjoint_ids(per_device)
    lhs = lhs_ref[...]
    for x in range(1, width_x - 1):
        for a, value in enumerate(advance(dims, ids, lhs, x, at, rim)):
            mixed_ref[a, x - 1, :, :] = value
            ground_ref[a, x + 1 : x + 2, :] = value[0:1]


def mixed_at(dims, inner_ref, ends_ref, a, x, r):
    width_x = dims[1]
    rows = slice(8 * r, 8 * r + 8)
    if 1 <= x < width_x - 1:
        return inner_ref[a, x - 1, rows, :]
    return ends_ref[a, x + 1 if x < 1 else x - width_x + 3, rows, :]


def second_transport(dims, at, rim_wy, far, inner_ref, ends_ref, ids, x, r):
    half = 4 * dims[1]
    wy = at.wy(x, r)
    south_wy = from_south(wy, halo_of(rim_wy, x))
    center, east, west, north, south = rates_of(at.wx(x, r), at.wx(x - 1, r), wy, south_wy)
    values = []
    for a in range(len(ids)):
        own = mixed_at(dims, inner_ref, ends_ref, a, x, r)
        halo = turn(far(a // 2, r), -4 * x - 2 - half * (a % 2))
        parts = [
            center * own,
            east * mixed_at(dims, inner_ref, ends_ref, a, x + 1, r),
            west * mixed_at(dims, inner_ref, ends_ref, a, x - 1, r),
            north * from_north(own, halo),
            south * from_south(own, halo),
        ]
        values.append(total(parts))
    return values


def ends_kernel(dims, subs, per_device, *refs):
    lev, width_x, lanes = dims
    rim_ref, before_ref, after_ref, inner_ground_ref, c_ref, wx_ref, wy_ref, cluster_ref, strength_ref, lhs_ref = refs[:10]
    ends_ref, far_ref, surface_ref, full_ref, ground_ref, west_ref, beside_ref = refs[10:]
    pad = round_up(lev, 8)
    half = 4 * width_x
    cross = lax.axis_index("sub")
    lane = lane_of((1, lanes))
    place = lane % 4
    after_slot = lane // 4 == width_x
    before_slot = lane >= lanes - 4
    at = Columns(dims, c_ref, wx_ref, wy_ref, cluster_ref, strength_ref, before_ref, after_ref)
    ids = adjoint_ids(per_device)
    lhs = lhs_ref[...]

    base = RIM_TILES * pad
    rim_c, far_c, rim_wy, far_wy, far_wx, rim_wx = (rim_ref[i * pad : (i + 1) * pad, :] for i in range(RIM_TILES))
    rim_cluster = rim_ref[base : base + 1, :]
    far_cluster = rim_ref[base + 1 : base + 2, :]
    far_strength = rim_ref[base + 2 : base + 3, :]
    rim = Rim(far_c, far_wy, far_cluster)

    def sent(ref, tile):
        return jnp.concatenate([at.sent(ref, tile, r) for r in range(pad // 8)], axis=0)

    def full(value, before, after):
        return jnp.where(before_slot, turn(before, -2), jnp.where(after_slot, turn(after, half + 2), value))

    full_c = full(rim_c, sent(before_ref, 0), sent(after_ref, 0))
    full_wy = full(rim_wy, sent(before_ref, 3), sent(after_ref, 3))
    full_wx = full(rim_wx, sent(before_ref, 2), rim_wx)
    for i, value in enumerate((full_c, full_wy, full_wx)):
        full_ref[i * pad : (i + 1) * pad, :] = value
    rows = [
        full(rim_cluster, at.cluster(-1), at.cluster(width_x)),
        full(rim_ref[base + 3 : base + 4, :], at.strength(-1), at.strength(width_x)),
    ]
    full_ref[3 * pad : 3 * pad + 2, :] = jnp.concatenate(rows, axis=0)
    full_ref[3 * pad + 2 : 3 * pad + 8, :] = jnp.zeros((6, lanes), F32)
    picked = jnp.where(before_slot | after_slot, full_c, 0.0)
    wy_slot = (lane < 4) | (lane // 4 == width_x + 1)
    wx_slot = lane // 4 == 1
    moved_wy = full(jnp.zeros_like(rim_wy), turn(sent(before_ref, 3), 0), turn(sent(after_ref, 3), 0))
    picked = jnp.where(wy_slot, turn(moved_wy, 4), picked)
    picked = jnp.where(wx_slot, turn(sent(before_ref, 2), 6), picked).T
    picked = jnp.concatenate([picked, jnp.zeros((lanes, lanes - pad), F32)], axis=1)
    packet = picked[half : half + 8] + turn(picked[lanes - 8 : lanes], pad) + turn(picked[0:8], 2 * pad)
    tail = per_device * width_x
    surface_ref[tail : tail + 8, :] = packet
    surface_ref[tail + 8 : tail + 10, :] = jnp.concatenate(rows, axis=0)
    surface_ref[tail + 10 : tail + 16, :] = jnp.zeros((6, lanes), F32)
    for k, x in ((1, 0), (2, width_x - 1), (0, -1), (3, width_x)):
        for a, value in enumerate(advance(dims, ids, lhs, x, at, rim)):
            ends_ref[a, k, :, :] = value
            ground_ref[a, x + 1 : x + 2, :] = value[0:1]

    def rim_north(far, own):
        return turn(jnp.where(place == 2, own, far), -1)

    def rim_south(far, own):
        return turn(jnp.where(place == 1, own, far), 1)

    center, east, west, north, south = rates_of(far_wx, turn(far_wx, 4), far_wy, rim_south(far_wy, rim_wy))
    terms = (
        center * far_c,
        east * turn(far_c, -4),
        west * turn(far_c, 4),
        north * rim_north(far_c, rim_c),
        south * rim_south(far_c, rim_c),
    )
    clusters = (
        far_cluster,
        turn(far_cluster, -4),
        turn(far_cluster, 4),
        rim_north(far_cluster, rim_cluster),
        rim_south(far_cluster, rim_cluster),
    )
    inside = jnp.where(lane < half, jnp.where(place < 2, cross, subs - 1 - cross), 0) > 0
    fields = [jnp.where(inside, f, 0.0) for f in parted(terms, clusters, ids)]
    joined = [fields[a] + turn(fields[a + 1], half) for a in range(0, per_device, 2)]
    far_mixed = [crossed(f) for f in convect(lhs, joined, far_strength + turn(far_strength, half))]
    for at_pair, value in enumerate(far_mixed):
        far_ref[at_pair, 0:pad, :] = value
    far_ref[0, pad : pad + 8, :] = jnp.zeros((8, lanes), F32)
    for pair in range(1, len(far_mixed)):
        far_ref[pair, pad : pad + 8, :] = jnp.zeros((8, lanes), F32)

    rows = [rim.wy_tile[0:1]] + [turn(far_mixed[a // 2][0:1], half * (a % 2)) for a in range(per_device)]
    tall = round_up(len(rows), 8)
    stack = jnp.concatenate(rows + [jnp.zeros((tall - len(rows), lanes), F32)], axis=0)
    for x in range(width_x):
        beside_ref[x * tall : (x + 1) * tall, :] = halo_of(stack, x)

    def beside(at_row):
        return beside_ref[pl.ds(at_row, width_x, stride=tall), :]

    west_ref[0:1, :] = at.sent(before_ref, 2, 0)[0:1]
    west_ref[1 : width_x + 1, :] = wx_ref[0:width_x, :]
    wx, wy = wx_ref[0:width_x, :], wy_ref[0:width_x, :]
    south_wy = from_south(wy, beside(0))
    center, east, west, north, south = rates_of(wx, west_ref[0:width_x, :], wy, south_wy)
    for a in range(per_device):
        ground_ref[a, 2:width_x, :] = inner_ground_ref[a, 2:width_x, :]
        own = ground_ref[a, 1 : width_x + 1, :]
        rim_rows = beside(1 + a)
        parts = [
            center * own,
            east * ground_ref[a, 2 : width_x + 2, :],
            west * ground_ref[a, 0:width_x, :],
            north * from_north(own, rim_rows),
            south * from_south(own, rim_rows),
        ]
        surface_ref[a * width_x : (a + 1) * width_x, :] = total(parts)


def output_kernel(dims, per_device, *refs):
    lev, width_x, _ = dims
    rim_ref, before_ref, inner_ref, ends_ref, far_ref, wx_ref, wy_ref, cluster_ref, strength_ref = refs[:9]
    out_ref, token_ref, edge_ref, field_ref, sem = refs[9:]
    token_ref[...] = jnp.zeros(token_ref.shape, F32)
    pad = round_up(lev, 8)
    at = Columns(dims, None, wx_ref, wy_ref, cluster_ref, strength_ref, before_ref)
    ids = range(per_device)

    def far(pair, r):
        return far_ref[pair, 8 * r : 8 * r + 8, :]

    rim_wys = [crossed(rim_ref[3 * pad + 8 * r : 3 * pad + 8 * r + 8, :]) for r in range(pad // 8)]
    copies = []
    for x in range(width_x):
        for r in range(pad // 8):
            rim_wy = rim_wys[r]
            values = second_transport(dims, at, rim_wy, far, inner_ref, ends_ref, ids, x, r)
            for a, value in enumerate(values):
                if x in (0, width_x - 1):
                    edge_ref[a, min(x, 1), 8 * r : 8 * r + 8, :] = value
                else:
                    field_ref[a, x, 8 * r : 8 * r + 8, :] = value
        for a in range(per_device if 0 < x < width_x - 1 else 0):
            source = field_ref.at[a, x, pl.ds(0, lev), :]
            copies.append(pltpu.make_async_copy(source, out_ref.at[a, :, x, 0, :], sem.at[len(copies)]))
            copies[-1].start()
    for copy in copies:
        copy.wait()


def quotient(value, count):
    if count & (count - 1) == 0:
        return value >> (count.bit_length() - 1), value & (count - 1)
    return lax.div(value, count), lax.rem(value, count)


def tables_kernel(dims, tiles, subs, n_rim, cell_ref, weight_ref, hot_ref, share_ref):
    _, width_x, width_y = dims
    slots, elements = cell_ref.shape
    tile_pos = lax.axis_index("tiles")
    cross = lax.axis_index("sub")
    column_x, row_y = quotient(cell_ref[...], width_y * subs)
    block_x, inner_x = quotient(column_x, width_x)
    block_y, lane_y = quotient(row_y, width_y)
    step = block_x - tile_pos
    step = jnp.where(step < -1, step + tiles, jnp.where(step > 1, step - tiles, step))
    if n_rim == 2:
        side = jnp.where(block_y == cross, 0, 1)
    else:
        side = block_y - cross + 1
    at_y = side * width_y + lane_y
    at_x = (step + 1) * width_x + inner_x
    weight = weight_ref[...]
    group = width_y
    rows = lax.broadcasted_iota(jnp.int32, (16, group), 0)
    for g in range(0, elements, group):
        lanes = slice(g, g + group)
        for k in range(slots):
            y = jnp.broadcast_to(at_y[k : k + 1, lanes], (16, group)) - rows
            for first in range(0, n_rim * width_y, 16):
                hot_ref[k, first : first + 16, lanes] = jnp.where(y == first, 1.0, 0.0).astype(BF16)
            x = jnp.broadcast_to(at_x[k : k + 1, lanes], (16, group)) - rows
            w = jnp.broadcast_to(weight[k : k + 1, lanes], (16, group))
            for first in range(0, 3 * width_x, 16):
                share_ref[k, first : first + 16, lanes] = jnp.where(x == first, w, 0.0)


def looked_up(dims, per_device, blocks, hot_ref, share_ref, lanes):
    width_x = dims[1]
    rows = per_device * width_x
    surfaces = [split(jnp.concatenate(places, axis=1)) for _, places in blocks]
    lhs = jnp.concatenate([part for pair in surfaces for part in pair], axis=0)
    sums = [None] * per_device
    for k in range(hot_ref.shape[0]):
        found = jnp.dot(lhs, hot_ref[k, :, lanes], preferred_element_type=F32)
        for at, (step, _) in enumerate(blocks):
            share = share_ref[k, (step + 1) * width_x : (step + 2) * width_x, lanes]
            for a in range(per_device):
                high = 2 * at * rows + a * width_x
                low = high + rows
                value = (found[high : high + width_x] + found[low : low + width_x]) * share
                sums[a] = value if sums[a] is None else sums[a] + value
    return jnp.concatenate([jnp.sum(s, axis=0, keepdims=True) for s in sums], axis=0)


def wide_lanes(elements):
    wide = 256 if elements % 256 == 0 else 128
    return [slice(g, g + wide) for g in range(0, elements, wide)]


def sense_part_kernel(dims, per_device, n_rim, step, hot_ref, share_ref, block_ref, *refs):
    *found, out_ref = refs
    rows = per_device * dims[1]
    blocks = [(step, [block_ref[k * rows : (k + 1) * rows, :] for k in range(n_rim)])]
    for lanes in wide_lanes(out_ref.shape[1]):
        value = looked_up(dims, per_device, blocks, hot_ref, share_ref, lanes)
        out_ref[:, lanes] = total([ref[:, lanes] for ref in found] + [value])


def sense_last_kernel(*refs):
    *inputs, out_ref, own_ref, sem = refs
    sense_part_kernel(*inputs, own_ref)
    copy = pltpu.make_async_copy(own_ref, out_ref, sem)
    copy.start()
    copy.wait()


class Seam:
    def __init__(self, dims, c, wy, wx, cluster, strength):
        _, self.width_x, lanes = dims
        self.lane = lane_of((1, lanes))
        self.place = self.lane % 4
        slot = self.lane // 4
        self.first, self.last = slot == 0, slot == self.width_x - 1
        self.beside = (slot == lanes // 4 - 1) | (slot == self.width_x)
        self.c, self.cluster, self.strength = c, cluster, strength
        self.east = jnp.maximum(wx, 0.0)
        self.west = jnp.maximum(-turn(wx, 4), 0.0)
        self.north = jnp.maximum(wy, 0.0)
        self.south = jnp.maximum(-turn(wy, 1), 0.0)

    def missing(self, lhs, ids):
        near = (self.place == 1) | (self.place == 2)
        wanted_slots = near & (self.beside | self.first | self.last)
        moved = [(turn(self.c, k), turn(self.cluster, k)) for k in (-1, 1, 4, -4)]
        fields = []
        for wanted in ids:
            own = jnp.where(self.cluster == wanted, self.c, 0.0)
            from_n, from_s, from_w, from_e = (jnp.where(row == wanted, c, 0.0) for c, row in moved)
            upright = jnp.where(self.place == 1, self.north * from_n, self.south * (from_s - own))
            level = jnp.where(self.first, self.west * (from_w - own), self.east * from_e)
            fields.append(jnp.where(wanted_slots, jnp.where(self.beside, upright, level), 0.0))
        return convect(lhs, fields, self.strength)


def seam_transport(rates, missing):
    east, west, north, south = rates
    lane = lane_of((1, missing.shape[1]))
    place, slot = lane % 4, lane // 4
    level = jnp.where(slot == 0, west * turn(missing, 4), east * turn(missing, -4))
    return level + jnp.where(place == 1, north * turn(missing, -1), south * turn(missing, 1))


def own_places(subs):
    cross = lax.axis_index("sub")
    if subs == 2:
        own_south = (cross == 0).astype(jnp.int32)
        return [own_south]
    return [jnp.int32(0), jnp.int32(1)]


def patch_kernel(dims, subs, per_device, *refs):
    lev, width_x, lanes = dims
    rim_ref, full_ref, own_ref, south_ref, north_ref, lhs_ref, _, whole_ref, seam_ref = refs
    pad = round_up(lev, 8)
    half = 4 * width_x
    rows = per_device * width_x
    lane = lane_of((1, lanes))
    southern = lane % 4 < 2
    before_slot = lane >= lanes - 4
    after_slot = lane // 4 == width_x
    ids = adjoint_ids(per_device)
    lhs = lhs_ref[...]
    cross = lax.axis_index("sub")
    present = jnp.where(southern, cross, subs - 1 - cross) > 0

    def upright(ref):
        turned = ref[rows : rows + 8, :].T
        turned = jnp.concatenate([turned, jnp.zeros((lanes, lanes - 8), F32)], axis=1)
        return [turned[i * pad : (i + 1) * pad] for i in range(3)]

    def beyond(value, south, north, before, after):
        def placed(tile):
            moved = turn(tile[0], lanes - 4 - before)
            return moved if after is None else jnp.where(after_slot, turn(tile[1], half - after), moved)

        moved = placed(south) if south is north else jnp.where(southern, placed(south), placed(north))
        moved = jnp.where(present, moved, 0.0)
        slots = before_slot if after is None else before_slot | after_slot
        return jnp.where(slots, moved, value)

    south = upright(south_ref)
    north = south if subs == 2 else upright(north_ref)

    def pair(first, second):
        one = (south[first], south[second])
        return one, one if subs == 2 else (north[first], north[second])

    far_c, far_wy, far_wx = (rim_ref[i * pad : (i + 1) * pad, :] for i in (1, 3, 4))
    c_pair, wy_pair = pair(1, 0), pair(2, 0)
    if subs == 2:
        c_pair, wy_pair = (c_pair[0], c_pair[0]), (wy_pair[0], wy_pair[0])
    far_c = beyond(far_c, *c_pair, 4, 0)
    far_wx = beyond(far_wx, *wy_pair, 4, None)
    far_wy = beyond(far_wy, *wy_pair, 0, 4)
    base = RIM_TILES * pad

    def beyond_row(value, at_row):
        south_row = south_ref[rows + at_row : rows + at_row + 1, :]
        north_row = north_ref[rows + at_row : rows + at_row + 1, :]
        moved = jnp.where(present, jnp.where(southern, south_row, north_row), 0.0)
        return jnp.where(before_slot | after_slot, moved, value)

    far_cluster = beyond_row(rim_ref[base + 1 : base + 2, :], 8)
    far_strength = beyond_row(rim_ref[base + 2 : base + 3, :], 9)
    full_c, full_wy, full_wx = (full_ref[i * pad : (i + 1) * pad, :] for i in range(3))
    full_cluster = full_ref[3 * pad : 3 * pad + 1, :]
    full_strength = full_ref[3 * pad + 1 : 3 * pad + 2, :]
    surfaces = [own_ref, south_ref] if subs == 2 else [south_ref, own_ref, north_ref]
    for k, ref in enumerate(surfaces):
        whole_ref[k * rows : (k + 1) * rows, :] = ref[0:rows, :]
    for k, own_south in enumerate(own_places(subs)):
        mine = jnp.where(southern, own_south, 1 - own_south) > 0
        seam = Seam(
            dims,
            jnp.where(mine, full_c, far_c),
            jnp.where(mine, full_wy, far_wy),
            jnp.where(mine, full_wx, far_wx),
            jnp.where(mine, full_cluster, far_cluster),
            jnp.where(mine, full_strength, far_strength),
        )
        missing = seam.missing(lhs, ids)
        rates = (seam.east, seam.west, seam.north, seam.south)
        for i, value in enumerate(rates + tuple(missing)):
            seam_ref[k, i * pad : (i + 1) * pad, :] = value
        far_at = 1 if subs == 2 else 2 * k
        own_at = 0 if subs == 2 else 1
        own_lane = jnp.where(own_south > 0, lanes - 1, 0)
        for a, value in enumerate(missing):
            change = seam_transport([rate[0:8] for rate in rates], value[0:8])[0:1]
            for x in (0, width_x - 1):
                row = turn(change, -4 * x - 2)
                for block, at_lane in ((own_at, own_lane), (far_at, lanes - 1 - own_lane)):
                    at = block * rows + a * width_x + x
                    whole_ref[at : at + 1, :] = whole_ref[at : at + 1, :] + jnp.where(lane == at_lane, row, 0.0)


def output_ends_kernel(dims, subs, per_device, _, seam_ref, edge_ref, out_ref, done_ref, sem):
    lev, width_x, lanes = dims
    pad = round_up(lev, 8)
    lane = lane_of((1, lanes))
    copies = []
    for a in range(per_device):
        columns = [edge_ref[a, 0], edge_ref[a, 1]]
        for k, own_south in enumerate(own_places(subs)):
            rates = [seam_ref[k, i * pad : (i + 1) * pad, :] for i in range(4)]
            change = seam_transport(rates, seam_ref[k, (4 + a) * pad : (5 + a) * pad, :])
            own = lane == jnp.where(own_south > 0, lanes - 1, 0)
            for i, x in enumerate((0, width_x - 1)):
                columns[i] = columns[i] + jnp.where(own, turn(change, -4 * x - 2), 0.0)
        for i, x in enumerate((0, width_x - 1)):
            done_ref[a, i, :, :] = columns[i]
            source = done_ref.at[a, i, pl.ds(0, lev), :]
            copies.append(pltpu.make_async_copy(source, out_ref.at[a, :, x, 0, :], sem.at[len(copies)]))
            copies[-1].start()
    for copy in copies:
        copy.wait()


def ring(value, axis, steps):
    count = lax.axis_size(axis)
    return lax.ppermute(value, axis, [(i, (i + steps) % count) for i in range(count)])


def across(value):
    count = lax.axis_size("sub")
    if count == 2:
        other = ring(value, "sub", 1)
        return other, other
    from_south = lax.ppermute(value, "sub", [(i, i + 1) for i in range(count - 1)])
    from_north = lax.ppermute(value, "sub", [(i + 1, i) for i in range(count - 1)])
    return from_south, from_north


def body(
    innovation,
    cluster,
    kernel,
    wind_x,
    wind_y,
    conv_strength,
    conv_matrix,
    margin_cell,
    margin_weight,
):
    dims = kernel.shape
    lev, width_x, width_y = dims
    tiles = lax.axis_size("tiles")
    subs = lax.axis_size("sub")
    per_device = ADJ // lax.axis_size("adj")
    pad = round_up(lev, 8)
    deep = round_up(lev, 16)
    flat = (lev * width_x, width_y)
    tall = (pad * width_x, width_y)
    small = innovation.shape
    sources = (
        kernel.reshape(flat),
        wind_x.reshape(flat),
        wind_y.reshape(flat),
        innovation,
        cluster,
        conv_strength,
        conv_matrix,
    )
    cell, weight = margin_cell.T, margin_weight.T
    outs = [tall, tall, tall, small, (small, jnp.int32), small, conv_matrix.shape]
    outs += [((pad, 3 * deep), BF16), (2 * pad + 8, width_y)]
    fetched = call(
        functools.partial(fetch_kernel, dims),
        outs,
        sources,
        scratch=(pltpu.SemaphoreType.DMA((len(sources),)),),
        far_in=True,
    )
    air, wx, wy, innov, group, strength, _, lhs, own_rim = fetched
    south_rim, north_rim = across(own_rim)
    to_east, to_west = call(
        functools.partial(first_ends_kernel, dims),
        [(5 * lev + 4, width_y), (4 * lev + 4, width_y)],
        (air, innov, strength, lhs, wx, wy, group),
    )
    before = ring(to_east, "tiles", 1)
    after = ring(to_west, "tiles", -1)
    (first,) = call(
        functools.partial(first_mix_kernel, dims), [(width_x, pad, width_y)], (air, innov, strength, lhs), cost=400000
    )
    (rim,) = call(
        functools.partial(rim_kernel, dims, subs),
        [(RIM_TILES * pad + 8, width_y)],
        (own_rim, south_rim, north_rim, lhs),
        cost=400000,
    )
    inner, ground = call(
        functools.partial(inner_kernel, dims, per_device),
        [(per_device, width_x - 2, pad, width_y), (per_device, width_x + 8, width_y)],
        (rim, first, wx, wy, group, strength, lhs),
        cost=4000000,
    )
    ends, far, surface, full = call(
        functools.partial(ends_kernel, dims, subs, per_device),
        [
            (per_device, 4, pad, width_y),
            ((per_device + 1) // 2, pad + 8, width_y),
            (per_device * width_x + 16, width_y),
            (3 * pad + 8, width_y),
        ],
        (rim, before, after, ground, first, wx, wy, group, strength, lhs),
        scratch=(
            pltpu.VMEM((per_device, width_x + 8, width_y), F32),
            pltpu.VMEM((width_x + 8, width_y), F32),
            pltpu.VMEM((width_x * round_up(per_device + 1, 8), width_y), F32),
        ),
    )
    south_surface, north_surface = across(surface)
    field, token, edge = call(
        functools.partial(output_kernel, dims, per_device),
        [(per_device, lev, width_x, 1, width_y), (8, width_y), (per_device, 2, pad, width_y)],
        (rim, before, inner, ends, far, wx, wy, group, strength),
        scratch=(
            pltpu.VMEM((per_device, width_x, pad, width_y), F32),
            pltpu.SemaphoreType.DMA((per_device * width_x,)),
        ),
        far_out=(0,),
        cost=4000000,
    )
    n_rim = min(subs, 3)
    rows = per_device * width_x
    seams = 1 if subs == 2 else 2
    whole, seam = call(
        functools.partial(patch_kernel, dims, subs, per_device),
        [(n_rim * rows, width_y), (seams, (4 + per_device) * pad, width_y)],
        (rim, full, surface, south_surface, north_surface, lhs, token),
    )
    if subs > 2:
        own = whole[rows : 2 * rows]
        south_surface, north_surface = across(own)
        whole = jnp.concatenate([south_surface, own, north_surface], axis=0)
    surface_before = ring(whole, "tiles", 1)
    surface_after = ring(whole, "tiles", -1)
    near, hbm = pl.BlockSpec(memory_space=pltpu.VMEM), pl.BlockSpec(memory_space=pl.ANY)
    field = pl.pallas_call(
        functools.partial(output_ends_kernel, dims, subs, per_device),
        out_shape=jax.ShapeDtypeStruct(field.shape, F32),
        in_specs=[hbm, near, near],
        out_specs=hbm,
        scratch_shapes=[pltpu.VMEM((per_device, 2, pad, width_y), F32), pltpu.SemaphoreType.DMA((2 * per_device,))],
        input_output_aliases={0: 0},
        compiler_params=pltpu.CompilerParams(vmem_limit_bytes=VMEM_BYTES),
        cost_estimate=pl.CostEstimate(flops=1000000, bytes_accessed=1000000, transcendentals=0),
        name="output_ends",
    )(field, *[pltpu.with_memory_space_constraint(v, pltpu.VMEM) for v in (seam, edge)])
    slots, elements = cell.shape
    hot, share = call(
        functools.partial(tables_kernel, dims, tiles, subs, n_rim),
        [((slots, n_rim * width_y, elements), BF16), (slots, 3 * width_x, elements)],
        (cell, weight),
        cost=2000000,
    )
    part = functools.partial(sense_part_kernel, dims, per_device, n_rim)
    found = [(per_device, elements)]
    (sensed,) = call(functools.partial(part, 0), found, (hot, share, whole), cost=2000000)
    (sensed,) = call(functools.partial(part, 1), found, (hot, share, surface_after, sensed), cost=2000000)
    (sensed,) = call(
        functools.partial(sense_last_kernel, dims, per_device, n_rim, -1),
        found,
        (hot, share, surface_before, sensed),
        scratch=(pltpu.VMEM((per_device, elements), F32), pltpu.SemaphoreType.DMA),
        far_out=(0,),
    )
    return (field.reshape(per_device, lev, width_x, width_y), sensed)


def solution(mesh):
    in_specs = (
        P(("groups", "tiles"), "sub"),
        P(("groups", "tiles"), "sub"),
        P(None, "tiles", "sub"),
        P(None, "tiles", "sub"),
        P(None, "tiles", "sub"),
        P("tiles", "sub"),
        P(),
        P(("tiles", "sub"), None),
        P(("tiles", "sub"), None),
    )
    out_specs = (P(("groups", "adj"), None, "tiles", "sub"), P(("groups", "adj"), ("tiles", "sub")))
    return jax.shard_map(body, mesh=mesh, in_specs=in_specs, out_specs=out_specs, check_vma=False)
```
